32 devices in a mesh: dp: 16 (over z, y, x), seq: 2 (over core).
Axes of the slice: x: 2, y: 2, z: 4, core: 2. Of those that a mesh axis runs over, the one named last changes fastest.
Arguments:
- layer_input: bfloat16 [2, 16, 1024, 1152], P(None, 'dp', 'seq'), may hold values from -6 to 6
- w_query: bfloat16 [1152, 1152], P('dp', 'seq'), may hold values from -0.1875 to 0.1875
- w_key: bfloat16 [1152, 384], P('dp', 'seq'), may hold values from -0.1875 to 0.1875
- w_value: bfloat16 [1152, 384], P('dp', 'seq'), may hold values from -0.1875 to 0.1875
- w_out: bfloat16 [1152, 1152], P('dp', 'seq'), may hold values from -1.5 to 1.5
- gain_attn: bfloat16 [1152], P('dp'), may hold values from 0.099609375 to 1.8984375
- w_gate: bfloat16 [1152, 3072], P('dp', 'seq'), may hold values from -0.1875 to 0.1875
- w_up: bfloat16 [1152, 3072], P('dp', 'seq'), may hold values from -0.1875 to 0.1875
- w_down: bfloat16 [3072, 1152], P('dp', 'seq'), may hold values from -0.109375 to 0.109375
- gain_mlp: bfloat16 [1152], P('dp'), may hold values from 0.099609375 to 1.8984375
- cotangent: bfloat16 [2, 16, 1024, 1152], P(None, 'dp', 'seq'), may hold values from -6 to 6
Outputs:
- output: bfloat16 [2, 16, 1024, 1152], P(None, 'dp', 'seq')
- grad_input: bfloat16 [2, 16, 1024, 1152], P(None, 'dp', 'seq')
- grad_query: float32 [1152, 1152], P('dp', 'seq')
- grad_key: float32 [1152, 384], P('dp', 'seq')
- grad_value: float32 [1152, 384], P('dp', 'seq')
- grad_out: float32 [1152, 1152], P('dp', 'seq')
- grad_gain_attn: float32 [1152], P('dp')
- grad_gate: float32 [1152, 3072], P('dp', 'seq')
- grad_up: float32 [1152, 3072], P('dp', 'seq')
- grad_down: float32 [3072, 1152], P('dp', 'seq')
- grad_gain_mlp: float32 [1152], P('dp')
The draws below stay inside these ranges and needn't reach their ends.
All inputs are finite; a program needn't handle non-finite values.
Results may differ from the reference program's by a relative error of at most 0.018.
Values may be sent and summed in bfloat16 or wider, within the bound.
A program may use at most 256 MiB of HBM per device.

```python
import jax
import jax.numpy as jnp
from jax import lax

D = 1152
QUERY_HEADS = 18
KEY_VALUE_HEADS = 6
HEAD_SIZE = 64
FF = 3072
BLOCK = 256
MB = 2
QD = 1152
KVD = 384
SEQ_LEN = 1024
SEQS = 16


def with_spikes(array, rng, source, target, parts, factor):
    def block_of(axis_at):
        return (jnp.arange(array.shape[axis_at]) // (array.shape[axis_at] // parts)).reshape((-1,) + (1,) * (array.ndim - 1 - axis_at))

    one_side = jax.random.permutation(rng, parts)[block_of(target)]
    far = (block_of(target) + parts // 2) % parts
    return jnp.where((block_of(source) == one_side) | (block_of(source) == far), factor * array, array)


def steps_of(stream_key, shape, cuts, low, largest):
    def one(axis_at, parts):
        steps = jax.random.uniform(jax.random.fold_in(jax.random.fold_in(stream_key, 6), axis_at), (parts,), jnp.float32, low / len(cuts), largest / len(cuts))
        return jnp.repeat(jnp.exp(steps), shape[axis_at] // parts).reshape((-1,) + (1,) * (len(shape) - axis_at - 1))

    gain = one(*cuts[0])
    for cut in cuts[1:]:
        gain = gain * one(*cut)
    return gain


def scatter_about(stream_key, shape, scale, most, cuts=(), dtype=jnp.bfloat16):
    entries = jax.random.normal(stream_key, shape, jnp.float32) * scale
    if len(cuts) > 0:
        entries = steps_of(stream_key, shape, cuts, -0.22, 0.18) * entries
    return jnp.clip(entries, min=-most, max=most).astype(dtype)


def heavy_noise(own_key, extent, width, most, cuts, heavy, kind=jnp.bfloat16):
    result = width * jax.random.normal(own_key, extent, jnp.float32)
    if cuts:
        result = result * steps_of(own_key, extent, cuts, -0.22, 0.18)
    return jnp.clip(with_spikes(result, jax.random.fold_in(own_key, 3), *heavy), -most, most).astype(kind)


def setup_inputs(seed: int = 0) -> dict:
    arg_keys = jax.random.split(jax.random.key(seed), 12)
    return {
        "layer_input": heavy_noise(arg_keys[0], (MB, SEQS, SEQ_LEN, D), 1.0, 6.0, ((1, 16), (2, 2)), (1, 3, 16, 2.0)),
        "w_query": scatter_about(arg_keys[1], (D, QD), D ** -0.5, 0.1875, ((0, 16), (1, 2))),
        "w_key": scatter_about(arg_keys[2], (D, KVD), D ** -0.5, 0.1875, ((0, 16), (1, 2))),
        "w_value": scatter_about(arg_keys[3], (D, KVD), D ** -0.5, 0.1875, ((0, 16), (1, 2))),
        "w_out": scatter_about(arg_keys[4], (QD, D), (QD // 64) ** -0.5, 1.5, ((0, 16), (1, 2))),
        "gain_attn": jnp.clip(1.0 + 0.18 * jax.random.normal(arg_keys[5], (D,), jnp.float32), 0.099609375, 1.8984375).astype(jnp.bfloat16),
        "w_gate": scatter_about(arg_keys[6], (D, FF), D ** -0.5, 0.1875, ((0, 16), (1, 2))),
        "w_up": scatter_about(arg_keys[7], (D, FF), D ** -0.5, 0.1875, ((0, 16), (1, 2))),
        "w_down": scatter_about(arg_keys[8], (FF, D), FF ** -0.5, 0.109375, ((0, 16), (1, 2))),
        "gain_mlp": jnp.clip(1.0 + 0.18 * jax.random.normal(arg_keys[9], (D,), jnp.float32), 0.099609375, 1.8984375).astype(jnp.bfloat16),
        "cotangent": scatter_about(arg_keys[10], (MB, SEQS, SEQ_LEN, D), 1.0, 6.0, ((1, 16), (2, 2))),
    }


@jax.custom_vjp
def lower_precision(v):
    return lax.optimization_barrier(v.astype(jnp.bfloat16)).astype(jnp.float32)

@jax.custom_vjp
def lower_precision_back(v):
    return v

def low_keep(v):
    return (lower_precision(v), None)

def low_pass(kept, grad):
    return (grad,)

def back_keep(v):
    return (v, None)

def back_low(kept, grad):
    return (lower_precision(grad),)
lower_precision.defvjp(low_keep, low_pass)
lower_precision_back.defvjp(back_keep, back_low)
highest = lax.Precision.HIGHEST
epsilon = 1e-05

def apply_rotary(values_in, position_shift, head_count):
    count_rows = values_in.shape[0]
    half_dim = HEAD_SIZE // 2
    places = (position_shift + jnp.arange(count_rows)).astype(jnp.float32)
    frequency = 10000.0 ** (-2.0 * jnp.arange(half_dim).astype(jnp.float32) / HEAD_SIZE)
    angles = places[:, None] * frequency[None, :]
    cosine = jnp.cos(angles)[:, None, :]
    sine_part = jnp.sin(angles)[:, None, :]
    split_heads = values_in.reshape(count_rows, head_count, HEAD_SIZE)
    first_half = split_heads[..., :half_dim]
    second = split_heads[..., half_dim:]
    turned = jnp.concatenate([first_half * cosine - second * sine_part, second * cosine + first_half * sine_part], axis=-1)
    return turned.reshape(count_rows, head_count * HEAD_SIZE)

def forward_layer(tokens_in, w_query, w_key, w_value, w_out, gain_attn, w_gate, w_up, w_down, gain_mlp):
    token_length = tokens_in.shape[0]
    query_group_width = QUERY_HEADS // KEY_VALUE_HEADS
    scale_attn = lax.rsqrt(lax.optimization_barrier(jnp.mean(tokens_in * tokens_in, -1, keepdims=True)) + epsilon)
    normalized_attention_input = lower_precision(tokens_in * scale_attn * gain_attn)
    query_lin = jnp.dot(normalized_attention_input, w_query, precision=highest)
    keys_linear = jnp.dot(normalized_attention_input, w_key, precision=highest)
    values_lin = jnp.dot(normalized_attention_input, w_value, precision=highest)
    query_rotated = lower_precision(apply_rotary(lower_precision_back(query_lin), 0, QUERY_HEADS))
    keys_rotated = lower_precision(apply_rotary(lower_precision_back(keys_linear), 0, KEY_VALUE_HEADS))
    values_lower_precision = lower_precision(lower_precision_back(values_lin))
    query_head_rows = query_rotated.reshape(token_length, KEY_VALUE_HEADS, query_group_width, HEAD_SIZE)
    key_head_rows = keys_rotated.reshape(token_length, KEY_VALUE_HEADS, HEAD_SIZE)
    value_head_rows = values_lower_precision.reshape(token_length, KEY_VALUE_HEADS, HEAD_SIZE)
    logits = lower_precision_back(jnp.einsum('qgjh,kgh->gjqk', query_head_rows, key_head_rows, precision=highest) * 0.125)
    blocks = jnp.arange(token_length) // BLOCK
    allowed = blocks[None, :] <= blocks[:, None]
    scores = jnp.where(allowed, logits, -jnp.inf)
    attn_prob = jax.nn.softmax(scores, axis=-1)
    prob_low = lower_precision(attn_prob)
    mixed_out = jnp.einsum('gjqk,kgh->qgjh', prob_low, value_head_rows, precision=highest).reshape(token_length, QUERY_HEADS * HEAD_SIZE)
    merged = lower_precision(lower_precision_back(mixed_out))
    residual = tokens_in + lower_precision_back(jnp.dot(merged, w_out, precision=highest))
    scale_mlp = lax.rsqrt(lax.optimization_barrier(jnp.mean(residual * residual, -1, keepdims=True)) + epsilon)
    normed_mlp = lower_precision(residual * scale_mlp * gain_mlp)
    gate_val = lower_precision_back(jnp.dot(normed_mlp, w_gate, precision=highest))
    up_val = lower_precision_back(jnp.dot(normed_mlp, w_up, precision=highest))
    hidden = lower_precision(jax.nn.silu(gate_val) * up_val)
    return residual + lower_precision_back(jnp.dot(hidden, w_down, precision=highest))

def reference(layer_input, w_query, w_key, w_value, w_out, gain_attn, w_gate, w_up, w_down, gain_mlp, cotangent):
    weights = tuple((weight.astype(jnp.float32) for weight in (w_query, w_key, w_value, w_out, gain_attn, w_gate, w_up, w_down, gain_mlp)))
    sequences = layer_input.reshape(MB * SEQS, SEQ_LEN, D).astype(jnp.float32)
    cotangents = cotangent.reshape(MB * SEQS, SEQ_LEN, D).astype(jnp.float32)
    start_sums = tuple((jnp.zeros(weight.shape, jnp.float32) for weight in weights))

    def per_sequence(grad_sums, inputs_pair):
        tokens_in, grad_in = inputs_pair
        layer_out, pullback = jax.vjp(forward_layer, tokens_in, *weights)
        gradients = pullback(grad_in)
        new_sums = tuple((earlier + added for earlier, added in zip(grad_sums, gradients[1:])))
        return (new_sums, (layer_out.astype(jnp.bfloat16), gradients[0].astype(jnp.bfloat16)))
    grad_sums, (outputs, grad_inputs) = lax.scan(per_sequence, start_sums, (sequences, cotangents))
    output = outputs.reshape(MB, SEQS, SEQ_LEN, D)
    grad_input = grad_inputs.reshape(MB, SEQS, SEQ_LEN, D)
    return (output, grad_input, grad_sums[0], grad_sums[1], grad_sums[2], grad_sums[3], grad_sums[4], grad_sums[5], grad_sums[6], grad_sums[7], grad_sums[8])
```

```python
import functools

import jax
import jax.numpy as jnp
from jax import lax
from jax.experimental import pallas as pl
from jax.experimental.pallas import tpu as pltpu
from jax.sharding import PartitionSpec as P

D = 1152
QUERY_HEADS = 18
KEY_VALUE_HEADS = 6
HEAD_SIZE = 64
FF = 3072
BLOCK = 256
QD = 1152
KVD = 384
HQ, HK = QUERY_HEADS // 2, KEY_VALUE_HEADS // 2
HALL = HQ + 2 * HK
QKV = HALL * HEAD_SIZE
FT = 256

epsilon = 1e-05
bf16, f32 = jnp.bfloat16, jnp.float32
NT = (((1,), (1,)), ((), ()))
NN = (((1,), (0,)), ((), ()))
TN = (((0,), (0,)), ((), ()))
VMEM_BYTES = 62 << 20


def dg(a, b, dims):
    return lax.dot_general(a, b, dims, preferred_element_type=f32)


def fwd_body(me, q, k, v, o, lse, kf, vf):
    piece = q.shape[3]
    shift = me[0]

    @pl.when(pl.program_id(1) % 3 == 0)
    def _():
        for a in range(2):
            kf[pl.ds(a * piece, piece), :] = k[shift ^ a, 0, 0]
            vf[pl.ds(a * piece, piece), :] = v[shift ^ a, 0, 0]

    for i in range(2 * piece // BLOCK):
        half, row = divmod(i * BLOCK, piece)
        r = pl.ds(row, BLOCK)
        kw = (i + 1) * BLOCK
        qs = q[shift ^ half, 0, 0, r, :] * jnp.asarray(0.125, bf16)
        s = dg(qs, kf[:kw, :], NT)
        m = jnp.max(s, axis=1, keepdims=True)
        p = jnp.exp(s - m)
        l = jnp.sum(p, axis=1, keepdims=True)
        mix = dg(p.astype(bf16), vf[:kw, :], NN)
        o[shift ^ half, 0, 0, r, :] = (mix / l).astype(bf16)
        lse[0, 0, pl.ds(i * BLOCK, BLOCK), :] = jnp.broadcast_to(m + jnp.log(l), (BLOCK, 128))


def bwd_body(me, q, k, v, o, do, lse, dq, dk, dv, kf, vf, dka, dva):
    piece = q.shape[3]
    shift = me[0]
    j = pl.program_id(2)

    @pl.when(j == 0)
    def _():
        for a in range(2):
            kf[pl.ds(a * piece, piece), :] = k[shift ^ a, 0, 0]
            vf[pl.ds(a * piece, piece), :] = v[shift ^ a, 0, 0]
        dka[...] = jnp.zeros_like(dka)
        dva[...] = jnp.zeros_like(dva)

    for i in range(2 * piece // BLOCK):
        half, row = divmod(i * BLOCK, piece)
        r = pl.ds(row, BLOCK)
        kw = (i + 1) * BLOCK
        at = shift ^ half
        qs = q[at, 0, 0, r, :] * jnp.asarray(0.125, bf16)
        dO = do[at, 0, 0, r, :]
        kk = kf[:kw, :]
        s = dg(qs, kk, NT)
        p = jnp.exp(s - lse[0, 0, pl.ds(i * BLOCK, BLOCK), :1])
        dp = dg(dO, vf[:kw, :], NT)
        inner = jnp.sum(dO.astype(f32) * o[at, 0, 0, r, :].astype(f32), axis=1, keepdims=True)
        ds = (p * (dp - inner)).astype(bf16)
        dq[at, 0, 0, r, :] = (dg(ds, kk, NN) * 0.125).astype(bf16)
        dka[:, :kw] += dg(qs.T, ds, NN)
        dva[:, :kw] += dg(dO.T, p.astype(bf16), NN)

    @pl.when(j == pl.num_programs(2) - 1)
    def _():
        for a in range(2):
            c = pl.ds(a * piece, piece)
            dk[shift ^ a, 0, 0] = dka[:, c].T.astype(bf16)
            dv[shift ^ a, 0, 0] = dva[:, c].T.astype(bf16)


def attend(me, heads):
    _, batch, _, piece, width = heads.shape
    at = lambda f: pl.BlockSpec((2, 1, 1, piece, width), lambda b, h, *_: (0, b, f(h), 0, 0))
    return pl.pallas_call(
        fwd_body,
        grid_spec=pltpu.PrefetchScalarGridSpec(
            num_scalar_prefetch=1,
            grid=(batch, HQ),
            in_specs=[at(lambda h: h), at(lambda h: HQ + h // 3), at(lambda h: HQ + HK + h // 3)],
            out_specs=[
                at(lambda h: h),
                pl.BlockSpec((1, 1, 2 * piece, 128), lambda b, h, *_: (b, h, 0, 0)),
            ],
            scratch_shapes=[pltpu.VMEM((2 * piece, width), bf16)] * 2,
        ),
        out_shape=[
            jax.ShapeDtypeStruct((2, batch, HQ, piece, width), bf16),
            jax.ShapeDtypeStruct((batch, HQ, 2 * piece, 128), f32),
        ],
        compiler_params=pltpu.CompilerParams(vmem_limit_bytes=VMEM_BYTES),
        cost_estimate=pl.CostEstimate(flops=24 * 10**9, bytes_accessed=20 * 10**6, transcendentals=12 * 10**6),
        name="attend",
    )(me, heads, heads, heads)


def attend_back(me, heads, mixed, grads, lse):
    _, batch, _, piece, width = heads.shape
    at = lambda f: pl.BlockSpec((2, 1, 1, piece, width), lambda b, g, j, *_: (0, b, f(g, j), 0, 0))
    query = at(lambda g, j: g * 3 + j)
    key = at(lambda g, j: g)
    return pl.pallas_call(
        bwd_body,
        grid_spec=pltpu.PrefetchScalarGridSpec(
            num_scalar_prefetch=1,
            grid=(batch, HK, 3),
            in_specs=[
                query,
                at(lambda g, j: HQ + g),
                at(lambda g, j: HQ + HK + g),
                query,
                query,
                pl.BlockSpec((1, 1, 2 * piece, 128), lambda b, g, j, *_: (b, g * 3 + j, 0, 0)),
            ],
            out_specs=[query, key, key],
            scratch_shapes=[pltpu.VMEM((2 * piece, width), bf16)] * 2
            + [pltpu.VMEM((width, 2 * piece), f32)] * 2,
        ),
        out_shape=[
            jax.ShapeDtypeStruct((2, batch, HQ, piece, width), bf16),
            jax.ShapeDtypeStruct((2, batch, HK, piece, width), bf16),
            jax.ShapeDtypeStruct((2, batch, HK, piece, width), bf16),
        ],
        compiler_params=pltpu.CompilerParams(vmem_limit_bytes=VMEM_BYTES),
        cost_estimate=pl.CostEstimate(flops=27 * 10**9, bytes_accessed=40 * 10**6, transcendentals=12 * 10**6),
        name="attend_back",
    )(me, heads, heads, heads, mixed, grads, lse)


def mlp_body(n2, n2t, cot, res, wg, wu, wd, out, gn, gg, gu, gd, y):
    t = pl.program_id(0)

    @pl.when(t == 0)
    def _():
        y[...] = res[...]
        gn[...] = jnp.zeros_like(gn)

    half = wd.shape[2]
    wdt = jnp.concatenate([wd[0], wd[1]], axis=1)
    gate = dg(n2[...], wg[0], NN)
    up = dg(n2[...], wu[0], NN)
    gh = dg(cot[...], wdt, NT)
    sig = jax.nn.sigmoid(gate)
    act = gate * sig
    hidden = (act * up).astype(bf16)
    ggv = (gh * up * sig * (1.0 + gate * (1.0 - sig))).astype(bf16)
    guv = (gh * act).astype(bf16)
    y[...] += dg(hidden, wdt, NN)
    gdt = dg(hidden, cot[...], TN).astype(bf16)
    gd[0] = gdt[:, :half]
    gd[1] = gdt[:, half:]
    gg[0] = dg(n2t[...], ggv, NN).astype(bf16)
    gu[0] = dg(n2t[...], guv, NN).astype(bf16)
    gn[...] += dg(ggv, wg[0], NT) + dg(guv, wu[0], NT)

    @pl.when(t == pl.num_programs(0) - 1)
    def _():
        out[...] = y[...].astype(bf16)


def mlp(n2, n2t, cot, res, wg, wu, wd):
    rows = n2.shape[0]
    cols = wg.shape[2]
    per = cols // FT
    whole = lambda a: pl.BlockSpec(a.shape, lambda t: (0, 0), pipeline_mode=pl.Buffered(1))
    col = pl.BlockSpec((1, D, FT), lambda t: (t // per, 0, t % per))
    row = pl.BlockSpec((2, FT, D // 2), lambda t: (0, t, 0))
    one = lambda: pl.BlockSpec((rows, D), lambda t: (0, 0), pipeline_mode=pl.Buffered(1))
    return pl.pallas_call(
        mlp_body,
        grid=(FF // FT,),
        in_specs=[whole(n2), whole(n2t), whole(cot), whole(res), col, col, row],
        out_specs=[one(), one(), col, col, row],
        out_shape=[
            jax.ShapeDtypeStruct((rows, D), bf16),
            jax.ShapeDtypeStruct((rows, D), f32),
            jax.ShapeDtypeStruct(wg.shape, bf16),
            jax.ShapeDtypeStruct(wu.shape, bf16),
            jax.ShapeDtypeStruct(wd.shape, bf16),
        ],
        scratch_shapes=[pltpu.VMEM((rows, D), f32)],
        compiler_params=pltpu.CompilerParams(vmem_limit_bytes=VMEM_BYTES),
        cost_estimate=pl.CostEstimate(flops=65 * 10**9, bytes_accessed=60 * 10**6, transcendentals=3 * 10**6),
        name="mlp",
    )(n2, n2t, cot, res, wg, wu, wd)


def turn(u, shift, heads, inverse):
    tokens = u.shape[1]
    h = HEAD_SIZE // 2
    places = (shift + jnp.arange(tokens)).astype(f32)
    frequency = 10000.0 ** (-2.0 * jnp.arange(h).astype(f32) / HEAD_SIZE)
    angles = places[:, None] * frequency[None, :]
    cosine, sine = jnp.cos(angles)[:, None, :], jnp.sin(angles)[:, None, :]
    if inverse:
        sine = -sine
    a, b = u[..., :heads, :h], u[..., :heads, h:]
    turned = jnp.concatenate([a * cosine - b * sine, b * cosine + a * sine], -1)
    return jnp.concatenate([turned, u[..., heads:, :]], -2)


def norm_back(grad_norm, rows_in, scale_rows, gain_rows):
    weighted = grad_norm * gain_rows
    cube_rows = scale_rows * scale_rows * scale_rows
    return scale_rows * weighted - rows_in * cube_rows * jnp.mean(
        weighted * rows_in, -1, keepdims=True
    )


def swap(a):
    return lax.ppermute(a, "seq", [(0, 1), (1, 0)])


def in_order(me, mine, theirs, axis):
    return jnp.where(
        me == 0,
        jnp.concatenate([mine, theirs], axis),
        jnp.concatenate([theirs, mine], axis),
    )


BOTH = ("dp", "seq")


def fetch(shards):
    out = []
    for w in shards:
        g = lax.all_gather(w, BOTH, axis=0, tiled=True)
        g = g.reshape(lax.axis_size("dp"), 2, *w.shape)
        out.append(jnp.swapaxes(g, 0, 1).reshape(2, -1, w.shape[1]))
    return out


def reduce_all(grads):
    out = []
    for g in grads:
        n = lax.axis_size("dp")
        t = jnp.swapaxes(g.reshape(2, n, -1, g.shape[2]), 0, 1).reshape(-1, g.shape[2])
        out.append(lax.psum_scatter(t, BOTH, scatter_dimension=0, tiled=True))
    return out


def local(
    layer_input,
    w_query,
    w_key,
    w_value,
    w_out,
    gain_attn,
    w_gate,
    w_up,
    w_down,
    gain_mlp,
    cotangent,
):
    batch, _, piece, _ = layer_input.shape
    tokens = batch * piece
    me = lax.axis_index("seq")
    shift = me * piece
    me_arr = jnp.full((1,), me, jnp.int32)
    gains = jnp.pad(jnp.stack([gain_attn, gain_mlp], 1), ((0, 0), (0, 126)))
    pack = jnp.concatenate([w_query, w_key, w_value, w_out, gains], 1)
    (full,) = fetch([pack])
    full_gate, full_up, full_down = fetch([w_gate, w_up, w_down])
    gain_one = full[0, :, QKV + D // 2].astype(f32)
    gain_two = full[0, :, QKV + D // 2 + 1].astype(f32)
    w_mine = lax.dynamic_index_in_dim(full, me, 0, keepdims=False)[:, :QKV]
    w_theirs = lax.dynamic_index_in_dim(full, 1 - me, 0, keepdims=False)[:, :QKV]
    full_out = jnp.concatenate([full[0, :, QKV : QKV + D // 2], full[1, :, QKV : QKV + D // 2]], 1)

    floats = layer_input.reshape(tokens, D).astype(f32)
    cot = cotangent.reshape(tokens, D)
    scale_attn = lax.rsqrt(jnp.mean(floats * floats, -1, keepdims=True) + epsilon)
    n1 = (floats * scale_attn * gain_one).astype(bf16)

    def heads_of(w):
        u = jnp.dot(n1, w, preferred_element_type=f32).reshape(batch, piece, HALL, HEAD_SIZE)
        return jnp.transpose(turn(u, shift, HQ + HK, False).astype(bf16), (0, 2, 1, 3))

    theirs = swap(heads_of(w_theirs))
    heads = jnp.stack([heads_of(w_mine), theirs])
    mixed, lse = attend(me_arr, heads)
    mixed_back = swap(mixed[1])
    rows_of = lambda a: jnp.transpose(a, (0, 2, 1, 3)).reshape(tokens, -1)
    merged = in_order(me, rows_of(mixed[0]), rows_of(mixed_back), 1)
    residual = floats + jnp.dot(merged, full_out, preferred_element_type=f32)
    scale_mlp = lax.rsqrt(jnp.mean(residual * residual, -1, keepdims=True) + epsilon)
    n2 = (residual * scale_mlp * gain_two).astype(bf16)
    layer_out, grad_n2, grad_gate, grad_up, grad_down = mlp(
        n2, n2.T, cot, residual, full_gate, full_up, full_down
    )
    sum_gain_mlp = jnp.sum(grad_n2 * residual * scale_mlp, 0)
    grad_residual = cot.astype(f32) + norm_back(grad_n2, residual, scale_mlp, gain_two)
    grad_low = grad_residual.astype(bf16)
    grad_out = jnp.einsum("tq,td->qd", merged, grad_low, preferred_element_type=f32)
    grad_merged = jnp.einsum("td,qd->tq", grad_low, full_out, preferred_element_type=f32).astype(bf16)
    by_head = lambda a: jnp.transpose(a.reshape(batch, piece, HQ, HEAD_SIZE), (0, 2, 1, 3))
    part = lambda i: by_head(lax.dynamic_slice_in_dim(grad_merged, i * (QD // 2), QD // 2, 1))
    grad_mixed = jnp.stack([part(me), swap(part(1 - me))])
    d_query, d_key, d_value = attend_back(me_arr, heads, mixed, grad_mixed, lse)
    d_heads = jnp.concatenate([d_query, d_key, d_value], 2)

    def linear_of(a):
        u = jnp.transpose(a.astype(f32), (0, 2, 1, 3))
        return turn(u, shift, HQ + HK, True).astype(bf16).reshape(tokens, QKV)

    lin_theirs = linear_of(swap(d_heads[1]))
    lin_mine = linear_of(d_heads[0])
    weight_grad = lambda lin: jnp.einsum("td,tq->dq", n1, lin, preferred_element_type=f32).astype(bf16)
    grad_n1 = jnp.einsum("tq,dq->td", lin_mine, w_mine, preferred_element_type=f32) + jnp.einsum(
        "tq,dq->td", lin_theirs, w_theirs, preferred_element_type=f32
    )
    sum_gain_attn = jnp.sum(grad_n1 * floats * scale_attn, 0)
    grad_input = (grad_residual + norm_back(grad_n1, floats, scale_attn, gain_one)).astype(bf16)
    grad_qkv = in_order(me, weight_grad(lin_mine)[None], weight_grad(lin_theirs)[None], 0)
    sums = jnp.pad(jnp.stack([sum_gain_attn, sum_gain_mlp], 1), ((0, 0), (0, 126))).astype(bf16)
    go = grad_out.astype(bf16)
    grad_pack = jnp.concatenate(
        [
            grad_qkv,
            jnp.stack([go[:, : D // 2], go[:, D // 2 :]]),
            jnp.stack([sums, sums]),
        ],
        2,
    )
    r_gate, r_up, r_down = reduce_all([grad_gate, grad_up, grad_down])
    (r_pack,) = reduce_all([grad_pack])
    r_pack = r_pack.astype(f32)
    a, b, c, d = HQ * HEAD_SIZE, (HQ + HK) * HEAD_SIZE, QKV, QKV + D // 2
    shape = layer_input.shape
    return (
        layer_out.reshape(shape),
        grad_input.reshape(shape),
        r_pack[:, :a],
        r_pack[:, a:b],
        r_pack[:, b:c],
        r_pack[:, c:d],
        r_pack[:, d],
        r_gate.astype(f32),
        r_up.astype(f32),
        r_down.astype(f32),
        r_pack[:, d + 1],
    )


def solution(mesh):
    tokens, matrix, vector = P(None, "dp", "seq", None), P("dp", "seq"), P("dp")
    placed = (tokens, *[matrix] * 4, vector, *[matrix] * 3, vector, tokens)
    return jax.shard_map(
        local,
        mesh=mesh,
        in_specs=placed,
        out_specs=(tokens, tokens, *[matrix] * 4, vector, *[matrix] * 3, vector),
        check_vma=False,
    )
```

```python
import functools

import jax
import jax.numpy as jnp
from jax import lax
from jax.experimental import pallas as pl
from jax.experimental.pallas import tpu as pltpu
from jax.sharding import PartitionSpec as P

D = 1152
QUERY_HEADS = 18
KEY_VALUE_HEADS = 6
HEAD_SIZE = 64
FF = 3072
BLOCK = 256
QD = 1152
KVD = 384
HQ, HK = QUERY_HEADS // 2, KEY_VALUE_HEADS // 2
HALL = HQ + 2 * HK
QKV = HALL * HEAD_SIZE
FT = 256

epsilon = 1e-05
bf16, f32 = jnp.bfloat16, jnp.float32
NT = (((1,), (1,)), ((), ()))
NN = (((1,), (0,)), ((), ()))
TN = (((0,), (0,)), ((), ()))
VMEM_BYTES = 62 << 20


def dg(a, b, dims):
    return lax.dot_general(a, b, dims, preferred_element_type=f32)


def fwd_body(me, q, k, v, o, lse, kf, vf):
    piece = q.shape[3]
    shift = me[0]

    @pl.when(pl.program_id(1) % 3 == 0)
    def _():
        for a in range(2):
            kf[pl.ds(a * piece, piece), :] = k[shift ^ a, 0, 0]
            vf[pl.ds(a * piece, piece), :] = v[shift ^ a, 0, 0]

    for i in range(2 * piece // BLOCK):
        half, row = divmod(i * BLOCK, piece)
        r = pl.ds(row, BLOCK)
        kw = (i + 1) * BLOCK
        qs = q[shift ^ half, 0, 0, r, :] * jnp.asarray(0.125, bf16)
        s = dg(qs, kf[:kw, :], NT)
        m = jnp.max(s, axis=1, keepdims=True)
        p = jnp.exp(s - m)
        l = jnp.sum(p, axis=1, keepdims=True)
        mix = dg(p.astype(bf16), vf[:kw, :], NN)
        o[shift ^ half, 0, 0, r, :] = (mix / l).astype(bf16)
        lse[0, 0, pl.ds(i * BLOCK, BLOCK), :] = jnp.broadcast_to(m + jnp.log(l), (BLOCK, 128))


def bwd_body(me, q, k, v, o, do, lse, dq, dk, dv, kf, vf, dka, dva):
    piece = q.shape[3]
    shift = me[0]
    j = pl.program_id(2)

    @pl.when(j == 0)
    def _():
        for a in range(2):
            kf[pl.ds(a * piece, piece), :] = k[shift ^ a, 0, 0]
            vf[pl.ds(a * piece, piece), :] = v[shift ^ a, 0, 0]
        dka[...] = jnp.zeros_like(dka)
        dva[...] = jnp.zeros_like(dva)

    for i in range(2 * piece // BLOCK):
        half, row = divmod(i * BLOCK, piece)
        r = pl.ds(row, BLOCK)
        kw = (i + 1) * BLOCK
        at = shift ^ half
        qs = q[at, 0, 0, r, :] * jnp.asarray(0.125, bf16)
        dO = do[at, 0, 0, r, :]
        kk = kf[:kw, :]
        s = dg(qs, kk, NT)
        p = jnp.exp(s - lse[0, 0, pl.ds(i * BLOCK, BLOCK), :1])
        dp = dg(dO, vf[:kw, :], NT)
        inner = jnp.sum(dO.astype(f32) * o[at, 0, 0, r, :].astype(f32), axis=1, keepdims=True)
        ds = (p * (dp - inner)).astype(bf16)
        dq[at, 0, 0, r, :] = (dg(ds, kk, NN) * 0.125).astype(bf16)
        dka[:, :kw] += dg(qs.T, ds, NN)
        dva[:, :kw] += dg(dO.T, p.astype(bf16), NN)

    @pl.when(j == pl.num_programs(2) - 1)
    def _():
        for a in range(2):
            c = pl.ds(a * piece, piece)
            dk[shift ^ a, 0, 0] = dka[:, c].T.astype(bf16)
            dv[shift ^ a, 0, 0] = dva[:, c].T.astype(bf16)


def attend(me, heads):
    _, batch, _, piece, width = heads.shape
    at = lambda f: pl.BlockSpec((2, 1, 1, piece, width), lambda b, h, *_: (0, b, f(h), 0, 0))
    return pl.pallas_call(
        fwd_body,
        grid_spec=pltpu.PrefetchScalarGridSpec(
            num_scalar_prefetch=1,
            grid=(batch, HQ),
            in_specs=[at(lambda h: h), at(lambda h: HQ + h // 3), at(lambda h: HQ + HK + h // 3)],
            out_specs=[
                at(lambda h: h),
                pl.BlockSpec((1, 1, 2 * piece, 128), lambda b, h, *_: (b, h, 0, 0)),
            ],
            scratch_shapes=[pltpu.VMEM((2 * piece, width), bf16)] * 2,
        ),
        out_shape=[
            jax.ShapeDtypeStruct((2, batch, HQ, piece, width), bf16),
            jax.ShapeDtypeStruct((batch, HQ, 2 * piece, 128), f32),
        ],
        compiler_params=pltpu.CompilerParams(vmem_limit_bytes=VMEM_BYTES),
        cost_estimate=pl.CostEstimate(flops=24 * 10**9, bytes_accessed=20 * 10**6, transcendentals=12 * 10**6),
        name="attend",
    )(me, heads, heads, heads)


def attend_back(me, heads, mixed, grads, lse):
    _, batch, _, piece, width = heads.shape
    at = lambda f: pl.BlockSpec((2, 1, 1, piece, width), lambda b, g, j, *_: (0, b, f(g, j), 0, 0))
    query = at(lambda g, j: g * 3 + j)
    key = at(lambda g, j: g)
    return pl.pallas_call(
        bwd_body,
        grid_spec=pltpu.PrefetchScalarGridSpec(
            num_scalar_prefetch=1,
            grid=(batch, HK, 3),
            in_specs=[
                query,
                at(lambda g, j: HQ + g),
                at(lambda g, j: HQ + HK + g),
                query,
                query,
                pl.BlockSpec((1, 1, 2 * piece, 128), lambda b, g, j, *_: (b, g * 3 + j, 0, 0)),
            ],
            out_specs=[query, key, key],
            scratch_shapes=[pltpu.VMEM((2 * piece, width), bf16)] * 2
            + [pltpu.VMEM((width, 2 * piece), f32)] * 2,
        ),
        out_shape=[
            jax.ShapeDtypeStruct((2, batch, HQ, piece, width), bf16),
            jax.ShapeDtypeStruct((2, batch, HK, piece, width), bf16),
            jax.ShapeDtypeStruct((2, batch, HK, piece, width), bf16),
        ],
        compiler_params=pltpu.CompilerParams(vmem_limit_bytes=VMEM_BYTES),
        cost_estimate=pl.CostEstimate(flops=27 * 10**9, bytes_accessed=40 * 10**6, transcendentals=12 * 10**6),
        name="attend_back",
    )(me, heads, heads, heads, mixed, grads, lse)


def mlp_body(n2, n2t, cot, res, wg, wu, wd, out, gn, ggu, gd, y):
    t = pl.program_id(0)

    @pl.when(t == 0)
    def _():
        y[...] = res[...]
        gn[...] = jnp.zeros_like(gn)

    half = wd.shape[2]
    wdt = jnp.concatenate([wd[0], wd[1]], axis=1)
    gate = dg(n2[...], wg[0], NN)
    up = dg(n2[...], wu[0], NN)
    gh = dg(cot[...], wdt, NT)
    sig = jax.nn.sigmoid(gate)
    act = gate * sig
    hidden = (act * up).astype(bf16)
    ggv = (gh * up * sig * (1.0 + gate * (1.0 - sig))).astype(bf16)
    guv = (gh * act).astype(bf16)
    y[...] += dg(hidden, wdt, NN)
    gdt = dg(hidden, cot[...], TN).astype(bf16)
    gd[0] = gdt[:, :half]
    gd[1] = gdt[:, half:]
    ggu[0, :, :FT] = dg(n2t[...], ggv, NN).astype(bf16)
    ggu[0, :, FT:] = dg(n2t[...], guv, NN).astype(bf16)
    gn[...] += dg(ggv, wg[0], NT) + dg(guv, wu[0], NT)

    @pl.when(t == pl.num_programs(0) - 1)
    def _():
        out[...] = y[...].astype(bf16)


def mlp(n2, n2t, cot, res, wide, wd):
    rows = n2.shape[0]
    cols = FF // 2
    per = cols // FT
    whole = lambda a: pl.BlockSpec(a.shape, lambda t: (0, 0), pipeline_mode=pl.Buffered(1))
    col = lambda first, width: pl.BlockSpec((1, D, width), lambda t: (t // per, 0, first + t % per))
    row = pl.BlockSpec((2, FT, D // 2), lambda t: (0, t, 0))
    one = lambda: pl.BlockSpec((rows, D), lambda t: (0, 0), pipeline_mode=pl.Buffered(1))
    return pl.pallas_call(
        mlp_body,
        grid=(FF // FT,),
        in_specs=[whole(n2), whole(n2t), whole(cot), whole(res), col(0, FT), col(per, FT), row],
        out_specs=[one(), one(), col(0, 2 * FT), row],
        out_shape=[
            jax.ShapeDtypeStruct((rows, D), bf16),
            jax.ShapeDtypeStruct((rows, D), f32),
            jax.ShapeDtypeStruct((2, D, 2 * cols), bf16),
            jax.ShapeDtypeStruct(wd.shape, bf16),
        ],
        scratch_shapes=[pltpu.VMEM((rows, D), f32)],
        compiler_params=pltpu.CompilerParams(vmem_limit_bytes=VMEM_BYTES),
        cost_estimate=pl.CostEstimate(flops=65 * 10**9, bytes_accessed=60 * 10**6, transcendentals=3 * 10**6),
        name="mlp",
    )(n2, n2t, cot, res, wide, wide, wd)


def turn(u, shift, heads, inverse):
    tokens = u.shape[1]
    h = HEAD_SIZE // 2
    places = (shift + jnp.arange(tokens)).astype(f32)
    frequency = 10000.0 ** (-2.0 * jnp.arange(h).astype(f32) / HEAD_SIZE)
    angles = places[:, None] * frequency[None, :]
    cosine, sine = jnp.cos(angles)[:, None, :], jnp.sin(angles)[:, None, :]
    if inverse:
        sine = -sine
    a, b = u[..., :heads, :h], u[..., :heads, h:]
    turned = jnp.concatenate([a * cosine - b * sine, b * cosine + a * sine], -1)
    return jnp.concatenate([turned, u[..., heads:, :]], -2)


def norm_back(grad_norm, rows_in, scale_rows, gain_rows):
    weighted = grad_norm * gain_rows
    cube_rows = scale_rows * scale_rows * scale_rows
    return scale_rows * weighted - rows_in * cube_rows * jnp.mean(
        weighted * rows_in, -1, keepdims=True
    )


def swap(a):
    return lax.ppermute(a, "seq", [(0, 1), (1, 0)])


def in_order(me, mine, theirs, axis):
    return jnp.where(
        me == 0,
        jnp.concatenate([mine, theirs], axis),
        jnp.concatenate([theirs, mine], axis),
    )


BOTH = ("dp", "seq")


def fetch(w):
    g = lax.all_gather(w, BOTH, axis=0, tiled=True)
    g = g.reshape(lax.axis_size("dp"), 2, *w.shape)
    return jnp.swapaxes(g, 0, 1).reshape(2, -1, w.shape[1])


def reduce_all(g):
    n = lax.axis_size("dp")
    t = jnp.swapaxes(g.reshape(2, n, -1, g.shape[2]), 0, 1).reshape(-1, g.shape[2])
    return lax.psum_scatter(t, BOTH, scatter_dimension=0, tiled=True)


def add(a, b):
    return a.astype(f32) + b.astype(f32)


def reduce_halving(g, me):
    n = lax.axis_size("dp")
    bits = n.bit_length() - 1
    dp = lax.axis_index("dp")
    mine = lax.dynamic_index_in_dim(g, me, 0, keepdims=False)
    theirs = lax.dynamic_index_in_dim(g, 1 - me, 0, keepdims=False)
    both = add(mine, swap(theirs)).astype(bf16)
    cols = g.shape[2]
    cut = cols // 256 * 128
    out = []
    for part, order in ((both[:, :cut], [0, 1]), (both[:, cut:], [1, 0])):
        left = list(range(bits))[::-1]
        a = part.reshape(*[2] * bits, -1, part.shape[1])
        for bit in order + list(range(2, bits)):
            axis = left.index(bit)
            left.remove(bit)
            mybit = (dp >> bit) & 1
            keep = lax.dynamic_index_in_dim(a, mybit, axis, keepdims=False)
            send = lax.dynamic_index_in_dim(a, 1 - mybit, axis, keepdims=False)
            got = lax.ppermute(send, "dp", [(i, i ^ (1 << bit)) for i in range(n)])
            a = add(keep, got)
            if left:
                a = a.astype(bf16)
        out.append(a)
    return jnp.concatenate(out, 1)


def local(
    layer_input,
    w_query,
    w_key,
    w_value,
    w_out,
    gain_attn,
    w_gate,
    w_up,
    w_down,
    gain_mlp,
    cotangent,
):
    batch, _, piece, _ = layer_input.shape
    tokens = batch * piece
    me = lax.axis_index("seq")
    shift = me * piece
    me_arr = jnp.full((1,), me, jnp.int32)
    gains = jnp.pad(jnp.stack([gain_attn, gain_mlp], 1), ((0, 0), (0, 62)))
    full = fetch(jnp.concatenate([w_query, w_key, w_value, gains], 1))
    wide = fetch(jnp.concatenate([w_gate, w_up, w_out], 1))
    full_down = fetch(w_down)
    gain_one = full[0, :, QKV].astype(f32)
    gain_two = full[0, :, QKV + 1].astype(f32)
    w_mine = lax.dynamic_index_in_dim(full, me, 0, keepdims=False)[:, :QKV]
    w_theirs = lax.dynamic_index_in_dim(full, 1 - me, 0, keepdims=False)[:, :QKV]
    full_out = jnp.concatenate([wide[0, :, FF:], wide[1, :, FF:]], 1)

    floats = layer_input.reshape(tokens, D).astype(f32)
    cot = cotangent.reshape(tokens, D)
    scale_attn = lax.rsqrt(jnp.mean(floats * floats, -1, keepdims=True) + epsilon)
    n1 = (floats * scale_attn * gain_one).astype(bf16)

    def heads_of(w):
        u = jnp.dot(n1, w, preferred_element_type=f32).reshape(batch, piece, HALL, HEAD_SIZE)
        return jnp.transpose(turn(u, shift, HQ + HK, False).astype(bf16), (0, 2, 1, 3))

    theirs = swap(heads_of(w_theirs))
    heads = jnp.stack([heads_of(w_mine), theirs])
    mixed, lse = attend(me_arr, heads)
    mixed_back = swap(mixed[1])
    rows_of = lambda a: jnp.transpose(a, (0, 2, 1, 3)).reshape(tokens, -1)
    merged = in_order(me, rows_of(mixed[0]), rows_of(mixed_back), 1)
    residual = floats + jnp.dot(merged, full_out, preferred_element_type=f32)
    scale_mlp = lax.rsqrt(jnp.mean(residual * residual, -1, keepdims=True) + epsilon)
    n2 = (residual * scale_mlp * gain_two).astype(bf16)
    layer_out, grad_n2, grad_wide, grad_down = mlp(n2, n2.T, cot, residual, wide, full_down)
    r_wide = reduce_all(grad_wide)
    r_down = reduce_halving(grad_down, me)
    sum_gain_mlp = jnp.sum(grad_n2 * residual * scale_mlp, 0)
    grad_residual = cot.astype(f32) + norm_back(grad_n2, residual, scale_mlp, gain_two)
    grad_low = grad_residual.astype(bf16)
    grad_out = jnp.einsum("tq,td->qd", merged, grad_low, preferred_element_type=f32)
    grad_merged = jnp.einsum("td,qd->tq", grad_low, full_out, preferred_element_type=f32).astype(bf16)
    by_head = lambda a: jnp.transpose(a.reshape(batch, piece, HQ, HEAD_SIZE), (0, 2, 1, 3))
    part = lambda i: by_head(lax.dynamic_slice_in_dim(grad_merged, i * (QD // 2), QD // 2, 1))
    grad_mixed = jnp.stack([part(me), swap(part(1 - me))])
    d_query, d_key, d_value = attend_back(me_arr, heads, mixed, grad_mixed, lse)
    d_heads = jnp.concatenate([d_query, d_key, d_value], 2)

    def linear_of(a):
        u = jnp.transpose(a.astype(f32), (0, 2, 1, 3))
        return turn(u, shift, HQ + HK, True).astype(bf16).reshape(tokens, QKV)

    lin_theirs = linear_of(swap(d_heads[1]))
    lin_mine = linear_of(d_heads[0])
    weight_grad = lambda lin: jnp.einsum("td,tq->dq", n1, lin, preferred_element_type=f32).astype(bf16)
    grad_n1 = jnp.einsum("tq,dq->td", lin_mine, w_mine, preferred_element_type=f32) + jnp.einsum(
        "tq,dq->td", lin_theirs, w_theirs, preferred_element_type=f32
    )
    sum_gain_attn = jnp.sum(grad_n1 * floats * scale_attn, 0)
    grad_input = (grad_residual + norm_back(grad_n1, floats, scale_attn, gain_one)).astype(bf16)
    grad_qkv = in_order(me, weight_grad(lin_mine)[None], weight_grad(lin_theirs)[None], 0)
    sums = jnp.pad(jnp.stack([sum_gain_attn, sum_gain_mlp], 1), ((0, 0), (0, 62))).astype(bf16)
    grad_pack = jnp.concatenate([grad_qkv, jnp.stack([sums, sums])], 2)
    r_pack = reduce_halving(grad_pack, me)
    go = grad_out.astype(bf16)
    r_out = reduce_halving(jnp.stack([go[:, : D // 2], go[:, D // 2 :]]), me)
    r_gate, r_up = [
        a.reshape(a.shape[0], -1).astype(f32)
        for a in jnp.split(r_wide.reshape(-1, FF // 2 // FT, 2, FT), 2, 2)
    ]
    a, b, c = HQ * HEAD_SIZE, (HQ + HK) * HEAD_SIZE, QKV
    shape = layer_input.shape
    return (
        layer_out.reshape(shape),
        grad_input.reshape(shape),
        r_pack[:, :a],
        r_pack[:, a:b],
        r_pack[:, b:c],
        r_out,
        r_pack[:, c],
        r_gate,
        r_up,
        r_down,
        r_pack[:, c + 1],
    )


def solution(mesh):
    tokens, matrix, vector = P(None, "dp", "seq", None), P("dp", "seq"), P("dp")
    placed = (tokens, *[matrix] * 4, vector, *[matrix] * 3, vector, tokens)
    return jax.shard_map(
        local,
        mesh=mesh,
        in_specs=placed,
        out_specs=(tokens, tokens, *[matrix] * 4, vector, *[matrix] * 3, vector),
        check_vma=False,
    )
```

```python
import functools

import jax
import jax.numpy as jnp
from jax import lax
from jax.experimental import pallas as pl
from jax.experimental.pallas import tpu as pltpu
from jax.sharding import PartitionSpec as P

D = 1152
QUERY_HEADS = 18
KEY_VALUE_HEADS = 6
HEAD_SIZE = 64
FF = 3072
BLOCK = 256
QD = 1152
KVD = 384
HQ, HK = QUERY_HEADS // 2, KEY_VALUE_HEADS // 2
HALL = HQ + 2 * HK
QKV = HALL * HEAD_SIZE
FT = 256
WIDE = 1024

epsilon = 1e-05
bf16, f32 = jnp.bfloat16, jnp.float32
NT = (((1,), (1,)), ((), ()))
NN = (((1,), (0,)), ((), ()))
TN = (((0,), (0,)), ((), ()))
VMEM_BYTES = 62 << 20


def dg(a, b, dims):
    return lax.dot_general(a, b, dims, preferred_element_type=f32)


def assemble(w):
    if w.shape[0] == 1:
        return w[0, 0]
    return jnp.concatenate([w[i, 0].astype(f32) for i in range(w.shape[0])], 0).astype(bf16)


def scatter_rows(out, cols, u):
    rows = out.shape[2]
    for i in range(out.shape[0]):
        out[i, 0, :, cols] = u[rows * i : rows * (i + 1)].astype(bf16)


def turned(u, cosine, sine):
    lane = lax.broadcasted_iota(jnp.int32, u.shape, 1)
    h = HEAD_SIZE // 2
    other = jnp.where(lane % HEAD_SIZE < h, pltpu.roll(u, 128 - h, 1), pltpu.roll(u, h, 1))
    return u * cosine + other * sine


def project_body(me, n1, w, cosine, sine, out, flat):
    @pl.when(pl.program_id(0) == 0)
    def _():
        flat[...] = assemble(w)

    u = dg(n1[...], flat[...], NN)
    turns = (HQ + HK) * HEAD_SIZE
    for c in range(0, turns, 128):
        out[:, c : c + 128] = turned(u[:, c : c + 128], cosine[...], sine[...]).astype(bf16)
    out[:, turns:] = u[:, turns:].astype(bf16)


def project(half, me, n1, w, cosine, sine, piece):
    n, _, rows, width = w.shape
    batch = n1.shape[0] // piece
    return pl.pallas_call(
        project_body,
        grid_spec=pltpu.PrefetchScalarGridSpec(
            num_scalar_prefetch=1,
            grid=(batch,),
            in_specs=[
                pl.BlockSpec((piece, D), lambda b, m: (b, 0)),
                pl.BlockSpec((n, 1, rows, width), lambda b, m: (0, m[0] ^ half, 0, 0)),
                pl.BlockSpec((piece, 128), lambda b, m: (m[0], 0)),
                pl.BlockSpec((piece, 128), lambda b, m: (m[0], 0)),
            ],
            out_specs=[
                pl.BlockSpec((piece, width), lambda b, m: (b, 0)),
                pl.BlockSpec((D, width), lambda b, m: (0, 0)),
            ],
        ),
        out_shape=[
            jax.ShapeDtypeStruct((n1.shape[0], width), bf16),
            jax.ShapeDtypeStruct((D, width), bf16),
        ],
        compiler_params=pltpu.CompilerParams(vmem_limit_bytes=VMEM_BYTES),
        cost_estimate=pl.CostEstimate(flops=3 * 10**9, bytes_accessed=12 * 10**6, transcendentals=0),
        name="project",
    )(me, n1, w, cosine, sine)


def head_cols(j):
    return slice(j * HEAD_SIZE, (j + 1) * HEAD_SIZE)


def lane_of(j, shape):
    return lax.broadcasted_iota(jnp.int32, shape, 1) == j


def place(me, mine, got, q, k, v):
    piece = mine.shape[0]
    at = [pl.ds(pl.multiple_of((me[0] ^ a) * piece, piece), piece) for a in range(2)]
    for src, rows in zip((mine, got), at):
        for j in range(HQ):
            q[j, rows, :] = src[:, head_cols(j)] * jnp.asarray(0.125, bf16)
        for j in range(HK):
            k[j, rows, :] = src[:, head_cols(HQ + j)]
            v[j, rows, :] = src[:, head_cols(HQ + HK + j)]
    return at


def fwd_body(me, mine, got, o_mine, o_theirs, lse, q, k, v, o):
    at = place(me, mine, got, q, k, v)
    lse[...] = jnp.zeros_like(lse)

    def head(j, _):
        g = j // (HQ // HK)
        for i in range(lse.shape[0] // BLOCK):
            r = pl.ds(i * BLOCK, BLOCK)
            kw = (i + 1) * BLOCK
            s = dg(q[j, r, :], k[g, :kw, :], NT)
            m = jnp.max(s, axis=1, keepdims=True)
            p = jnp.exp(s - m)
            l = jnp.sum(p, axis=1, keepdims=True)
            mix = dg(p.astype(bf16), v[g, :kw, :], NN)
            o[j, r, :] = (mix / l).astype(bf16)
            lse[r, :] = jnp.where(lane_of(j, (BLOCK, 128)), m + jnp.log(l), lse[r, :])
        return 0

    lax.fori_loop(0, HQ, head, 0)
    for dst, rows in zip((o_mine, o_theirs), at):
        for j in range(HQ):
            dst[:, head_cols(j)] = o[j, rows, :]


def bwd_body(
    me, mine, got, o_mine, o_theirs, do_mine, do_got, lse, cosine, sine,
    lin_mine, lin_theirs, q, k, v, do, d, dka, dva, inner,
):
    at = place(me, mine, got, q, k, v)
    inner[...] = jnp.zeros_like(inner)
    for dsrc, osrc, rows in zip((do_mine, do_got), (o_mine, o_theirs), at):
        for j in range(HQ):
            dj = dsrc[:, head_cols(j)]
            do[j, rows, :] = dj
            part = jnp.sum(dj.astype(f32) * osrc[:, head_cols(j)].astype(f32), axis=1, keepdims=True)
            inner[rows, :] = jnp.where(lane_of(j, (dj.shape[0], 128)), part, inner[rows, :])

    def group(g, _):
        dka[...] = jnp.zeros_like(dka)
        dva[...] = jnp.zeros_like(dva)
        for jj in range(HQ // HK):
            j = g * (HQ // HK) + jj
            for i in range(lse.shape[0] // BLOCK):
                r = pl.ds(i * BLOCK, BLOCK)
                kw = (i + 1) * BLOCK
                mark = lane_of(j, (BLOCK, 128))
                column = lambda a: jnp.sum(jnp.where(mark, a[r, :], 0.0), axis=1, keepdims=True)
                qs = q[j, r, :]
                dO = do[j, r, :]
                kk = k[g, :kw, :]
                p = jnp.exp(dg(qs, kk, NT) - column(lse))
                dp = dg(dO, v[g, :kw, :], NT)
                ds = (p * (dp - column(inner))).astype(bf16)
                d[j, r, :] = dg(ds, kk, NN) * 0.125
                dka[:, :kw] += dg(qs.T, ds, NN)
                dva[:, :kw] += dg(dO.T, p.astype(bf16), NN)
        d[HQ + g] = dka[...].T
        d[HQ + HK + g] = dva[...].T
        return 0

    lax.fori_loop(0, HK, group, 0)
    turns = HQ + HK
    for dst, rows in zip((lin_mine, lin_theirs), at):
        for j in range(0, HALL + 1, 2):
            a = d[j, rows, :]
            b = d[j + 1, rows, :] if j + 1 < HALL else jnp.zeros_like(a)
            u = jnp.concatenate([a, b], 1)
            if j < turns:
                u = turned(u, cosine[rows, :], -sine[rows, :])
            dst[:, j * HEAD_SIZE : (j + 2) * HEAD_SIZE] = u.astype(bf16)


def attend(me, mine, got, piece):
    tokens, width = mine.shape
    batch = tokens // piece
    row = lambda a, c: pl.BlockSpec((a, c), lambda b, m: (b, 0))
    cols = HQ * HEAD_SIZE
    heads = lambda n: pltpu.VMEM((n, 2 * piece, HEAD_SIZE), bf16)
    return pl.pallas_call(
        fwd_body,
        grid_spec=pltpu.PrefetchScalarGridSpec(
            num_scalar_prefetch=1,
            grid=(batch,),
            in_specs=[row(piece, width)] * 2,
            out_specs=[row(piece, cols), row(piece, cols), row(2 * piece, 128)],
            scratch_shapes=[heads(HQ), heads(HK), heads(HK), heads(HQ)],
        ),
        out_shape=[
            jax.ShapeDtypeStruct((tokens, cols), bf16),
            jax.ShapeDtypeStruct((tokens, cols), bf16),
            jax.ShapeDtypeStruct((2 * tokens, 128), f32),
        ],
        compiler_params=pltpu.CompilerParams(vmem_limit_bytes=VMEM_BYTES),
        cost_estimate=pl.CostEstimate(flops=24 * 10**9, bytes_accessed=20 * 10**6, transcendentals=12 * 10**6),
        name="attend",
    )(me, mine, got)


def attend_back(me, mine, got, o_mine, o_theirs, do_mine, do_got, lse, cosine, sine, piece):
    tokens, width = mine.shape
    batch = tokens // piece
    row = lambda a, c: pl.BlockSpec((a, c), lambda b, m: (b, 0))
    cols = HQ * HEAD_SIZE
    table = pl.BlockSpec((2 * piece, 128), lambda b, m: (0, 0))
    heads = lambda n, t: pltpu.VMEM((n, 2 * piece, HEAD_SIZE), t)
    return pl.pallas_call(
        bwd_body,
        grid_spec=pltpu.PrefetchScalarGridSpec(
            num_scalar_prefetch=1,
            grid=(batch,),
            in_specs=[row(piece, width)] * 2 + [row(piece, cols)] * 4 + [row(2 * piece, 128), table, table],
            out_specs=[row(piece, width)] * 2,
            scratch_shapes=[heads(HQ, bf16), heads(HK, bf16), heads(HK, bf16), heads(HQ, bf16)]
            + [heads(HALL, f32)]
            + [pltpu.VMEM((HEAD_SIZE, 2 * piece), f32)] * 2
            + [pltpu.VMEM((2 * piece, 128), f32)],
        ),
        out_shape=[jax.ShapeDtypeStruct((tokens, width), bf16)] * 2,
        compiler_params=pltpu.CompilerParams(vmem_limit_bytes=VMEM_BYTES),
        cost_estimate=pl.CostEstimate(flops=27 * 10**9, bytes_accessed=40 * 10**6, transcendentals=12 * 10**6),
        name="attend_back",
    )(me, mine, got, o_mine, o_theirs, do_mine, do_got, lse, cosine, sine)


def mlp_body(me, n2, n2t, cot, res, wg, wu, wd, out, gn, ggu, gd_mine, gd_theirs, y):
    t = pl.program_id(0)

    @pl.when(t == 0)
    def _():
        y[...] = res[...]
        gn[...] = jnp.zeros_like(gn)

    half = wd.shape[2]
    wdt = jnp.concatenate([wd[0], wd[1]], axis=1)
    wgt, wut = assemble(wg), assemble(wu)
    gate = dg(n2[...], wgt, NN)
    up = dg(n2[...], wut, NN)
    gh = dg(cot[...], wdt, NT)
    sig = jax.nn.sigmoid(gate)
    act = gate * sig
    hidden = (act * up).astype(bf16)
    ggv = (gh * up * sig * (1.0 + gate * (1.0 - sig))).astype(bf16)
    guv = (gh * act).astype(bf16)
    y[...] += dg(hidden, wdt, NN)
    gdt = dg(hidden, cot[...], TN)
    first = me[0] == 0
    gd_mine[...] = jnp.where(first, gdt[:, :half], gdt[:, half:]).astype(bf16)
    gd_theirs[...] = jnp.where(first, gdt[:, half:], gdt[:, :half]).astype(bf16)
    scatter_rows(ggu, slice(0, FT), dg(n2t[...], ggv, NN))
    scatter_rows(ggu, slice(FT, 2 * FT), dg(n2t[...], guv, NN))
    gn[...] += dg(ggv, wgt, NT) + dg(guv, wut, NT)

    @pl.when(t == pl.num_programs(0) - 1)
    def _():
        out[...] = y[...].astype(bf16)


def mlp(me, n2, n2t, cot, res, wide, wd):
    tokens = n2.shape[0]
    n, _, rows, _ = wide.shape
    cols = FF // 2
    per = cols // FT
    whole = lambda a: pl.BlockSpec(a.shape, lambda t, m: (0, 0), pipeline_mode=pl.Buffered(1))
    col = lambda first, width: pl.BlockSpec(
        (n, 1, rows, width), lambda t, m: (0, t // per, 0, first + t % per)
    )
    row = pl.BlockSpec((2, FT, D // 2), lambda t, m: (0, t, 0))
    part = pl.BlockSpec((FT, D // 2), lambda t, m: (t, 0))
    one = lambda: pl.BlockSpec((tokens, D), lambda t, m: (0, 0), pipeline_mode=pl.Buffered(1))
    return pl.pallas_call(
        mlp_body,
        grid_spec=pltpu.PrefetchScalarGridSpec(
            num_scalar_prefetch=1,
            grid=(FF // FT,),
            in_specs=[whole(n2), whole(n2t), whole(cot), whole(res), col(0, FT), col(per, FT), row],
            out_specs=[one(), one(), col(0, 2 * FT), part, part],
            scratch_shapes=[pltpu.VMEM((tokens, D), f32)],
        ),
        out_shape=[
            jax.ShapeDtypeStruct((tokens, D), bf16),
            jax.ShapeDtypeStruct((tokens, D), f32),
            jax.ShapeDtypeStruct((n, 2, rows, 2 * cols), bf16),
            jax.ShapeDtypeStruct((FF, D // 2), bf16),
            jax.ShapeDtypeStruct((FF, D // 2), bf16),
        ],
        compiler_params=pltpu.CompilerParams(vmem_limit_bytes=VMEM_BYTES),
        cost_estimate=pl.CostEstimate(flops=65 * 10**9, bytes_accessed=60 * 10**6, transcendentals=3 * 10**6),
        name="mlp",
    )(me, n2, n2t, cot, res, wide, wide, wd)


def norm_back(grad_norm, rows_in, scale_rows, gain_rows):
    weighted = grad_norm * gain_rows
    cube_rows = scale_rows * scale_rows * scale_rows
    return scale_rows * weighted - rows_in * cube_rows * jnp.mean(
        weighted * rows_in, -1, keepdims=True
    )


def swap(a):
    return lax.ppermute(a, "seq", [(0, 1), (1, 0)])


BOTH = ("dp", "seq")


def whole_halves(g):
    return jnp.swapaxes(g, 0, 1).reshape(1, 2, -1, g.shape[3])


def fetch(w):
    g = lax.all_gather(w, BOTH, axis=0, tiled=True).reshape(lax.axis_size("dp"), 2, *w.shape)
    return g if w.shape[0] % 8 == 0 else whole_halves(g)


def reduce_all(g):
    n = lax.axis_size("dp")
    if g.shape[0] != n:
        g = jnp.swapaxes(g.reshape(2, n, -1, g.shape[3]), 0, 1)
    return lax.psum_scatter(g.reshape(-1, g.shape[3]), BOTH, scatter_dimension=0, tiled=True)


def add(a, b):
    return a.astype(f32) + b.astype(f32)


def reduce_halving(mine, theirs, kind=bf16):
    n = lax.axis_size("dp")
    bits = n.bit_length() - 1
    dp = lax.axis_index("dp")
    both = add(mine, swap(theirs)).astype(kind)
    cut = mine.shape[1] // 256 * 128
    out = []
    for part, order in ((both[:, :cut], [0, 1]), (both[:, cut:], [1, 0])):
        if not part.shape[1]:
            continue
        left = list(range(bits))[::-1]
        a = part.reshape(*[2] * bits, -1, part.shape[1])
        for bit in order + list(range(2, bits)):
            axis = left.index(bit)
            left.remove(bit)
            mybit = (dp >> bit) & 1
            keep = lax.dynamic_index_in_dim(a, mybit, axis, keepdims=False)
            send = lax.dynamic_index_in_dim(a, 1 - mybit, axis, keepdims=False)
            a = add(keep, lax.ppermute(send, "dp", [(i, i ^ (1 << bit)) for i in range(n)]))
            if left:
                a = a.astype(kind)
        out.append(a)
    return jnp.concatenate(out, 1)


def local(
    layer_input,
    w_query,
    w_key,
    w_value,
    w_out,
    gain_attn,
    w_gate,
    w_up,
    w_down,
    gain_mlp,
    cotangent,
):
    batch, _, piece, _ = layer_input.shape
    tokens = batch * piece
    me = lax.axis_index("seq")
    me_arr = jnp.full((1,), me, jnp.int32)
    pick = lambda a, b: jnp.where(me == 0, a, b)
    h = HEAD_SIZE // 2
    frequency = 10000.0 ** (-2.0 * jnp.arange(h).astype(f32) / HEAD_SIZE)
    angles = jnp.arange(2 * piece).astype(f32)[:, None] * jnp.tile(frequency, 128 // h)[None, :]
    cosine = jnp.cos(angles)
    sine = jnp.sin(angles) * jnp.where(jnp.arange(128) % HEAD_SIZE < h, -1.0, 1.0)[None, :]

    gains = jnp.pad(jnp.stack([gain_attn, gain_mlp], 1), ((0, 0), (0, WIDE - QKV - 2)))
    full = fetch(jnp.concatenate([w_query, w_key, w_value, gains], 1))
    wide = fetch(jnp.concatenate([w_gate, w_up, w_out], 1))
    down = lax.all_gather(w_down, BOTH, axis=0, tiled=True)
    full_down = whole_halves(down.reshape(-1, 2, *w_down.shape))[0]
    gain_one = full[:, 0, :, QKV].reshape(D).astype(f32)
    gain_two = full[:, 0, :, QKV + 1].reshape(D).astype(f32)
    out_halves = whole_halves(wide[..., FF:])[0].reshape(2, 2, D // 2, D // 2)
    out_rows = lambda c: jnp.concatenate(
        [lax.dynamic_index_in_dim(out_halves[i], c, 0, keepdims=False) for i in range(2)], 1
    )
    out_mine, out_theirs = out_rows(me), out_rows(1 - me)

    floats = layer_input.reshape(tokens, D).astype(f32)
    cot = cotangent.reshape(tokens, D)
    scale_attn = lax.rsqrt(jnp.mean(floats * floats, -1, keepdims=True) + epsilon)
    n1 = (floats * scale_attn * gain_one).astype(bf16)
    dot = lambda a, b: lax.dot_general(a, b, NN, preferred_element_type=f32)

    heads_out, w_theirs = project(1, me_arr, n1, full, cosine, sine, piece)
    got = swap(heads_out)
    mine, w_mine = project(0, me_arr, n1, full, cosine, sine, piece)
    mixed, mixed_out, lse = attend(me_arr, mine, got, piece)
    mixed_got = swap(mixed_out)
    residual = floats + (dot(mixed, out_mine) + dot(mixed_got, out_theirs))
    scale_mlp = lax.rsqrt(jnp.mean(residual * residual, -1, keepdims=True) + epsilon)
    n2 = (residual * scale_mlp * gain_two).astype(bf16)
    layer_out, grad_n2, grad_wide, grad_down_mine, grad_down_theirs = mlp(
        me_arr, n2, n2.T, cot, residual, wide, full_down
    )
    r_wide = reduce_all(grad_wide)
    sum_gain_mlp = jnp.sum(grad_n2 * residual * scale_mlp, 0)
    grad_residual = cot.astype(f32) + norm_back(grad_n2, residual, scale_mlp, gain_two)
    grad_low = grad_residual.astype(bf16)
    d_out = lax.dot_general(grad_low, out_theirs, NT, preferred_element_type=f32).astype(bf16)
    d_got = swap(d_out)
    d_mine = lax.dot_general(grad_low, out_mine, NT, preferred_element_type=f32).astype(bf16)
    r_down = reduce_halving(grad_down_mine, grad_down_theirs)
    low = grad_low[:, : D // 2], grad_low[:, D // 2 :]

    def grad_out(columns):
        a = lax.dot_general(mixed, columns, TN, preferred_element_type=f32).astype(bf16)
        b = lax.dot_general(mixed_got, columns, TN, preferred_element_type=f32).astype(bf16)
        return pick(jnp.concatenate([a, b], 0), jnp.concatenate([b, a], 0))

    r_out = reduce_halving(grad_out(pick(*low)), grad_out(pick(*low[::-1])))
    lin_mine, lin_out = attend_back(
        me_arr, mine, got, mixed, mixed_out, d_mine, d_got, lse, cosine, sine, piece
    )
    lin_got = swap(lin_out)
    weight_grad = lambda lin: lax.dot_general(n1, lin, TN, preferred_element_type=f32).astype(bf16)
    lin_got, r_out, r_down = lax.optimization_barrier((lin_got, r_out, r_down))
    r_pack = reduce_halving(weight_grad(lin_mine), weight_grad(lin_got))
    grad_n1 = lax.dot_general(lin_mine, w_mine, NT, preferred_element_type=f32) + lax.dot_general(
        lin_got, w_theirs, NT, preferred_element_type=f32
    )
    sum_gain_attn = jnp.sum(grad_n1 * floats * scale_attn, 0)
    grad_input = (grad_residual + norm_back(grad_n1, floats, scale_attn, gain_one)).astype(bf16)
    sums = jnp.pad(jnp.stack([sum_gain_attn, sum_gain_mlp], 1), ((0, 0), (0, 126)))
    r_sums = reduce_halving(sums, sums, f32)
    r_gate, r_up = [
        a.reshape(a.shape[0], -1).astype(f32)
        for a in jnp.split(r_wide.reshape(-1, FF // 2 // FT, 2, FT), 2, 2)
    ]
    a, b, c = HQ * HEAD_SIZE, (HQ + HK) * HEAD_SIZE, QKV
    shape = layer_input.shape
    return (
        layer_out.reshape(shape),
        grad_input.reshape(shape),
        r_pack[:, :a],
        r_pack[:, a:b],
        r_pack[:, b:c],
        r_out,
        r_sums[:, 0],
        r_gate,
        r_up,
        r_down,
        r_sums[:, 1],
    )


def solution(mesh):
    tokens, matrix, vector = P(None, "dp", "seq", None), P("dp", "seq"), P("dp")
    placed = (tokens, *[matrix] * 4, vector, *[matrix] * 3, vector, tokens)
    return jax.shard_map(
        local,
        mesh=mesh,
        in_specs=placed,
        out_specs=(tokens, tokens, *[matrix] * 4, vector, *[matrix] * 3, vector),
        check_vma=False,
    )
```

```python
import functools

import jax
import jax.numpy as jnp
from jax import lax
from jax.experimental import pallas as pl
from jax.experimental.pallas import tpu as pltpu
from jax.sharding import PartitionSpec as P

D = 1152
QUERY_HEADS = 18
KEY_VALUE_HEADS = 6
HEAD_SIZE = 64
FF = 3072
BLOCK = 256
QD = 1152
KVD = 384
HQ, HK = QUERY_HEADS // 2, KEY_VALUE_HEADS // 2
HALL = HQ + 2 * HK
QKV = HALL * HEAD_SIZE
FT = 256
WIDE = 1024

epsilon = 1e-05
bf16, f32 = jnp.bfloat16, jnp.float32
NT = (((1,), (1,)), ((), ()))
NN = (((1,), (0,)), ((), ()))
TN = (((0,), (0,)), ((), ()))
VMEM_BYTES = 62 << 20


def dg(a, b, dims):
    return lax.dot_general(a, b, dims, preferred_element_type=f32)


def assemble(w):
    if w.shape[0] == 1:
        return w[0, 0]
    return jnp.concatenate([w[i, 0].astype(f32) for i in range(w.shape[0])], 0).astype(bf16)


def turned(u, cosine, sine):
    lane = lax.broadcasted_iota(jnp.int32, u.shape, 1)
    h = HEAD_SIZE // 2
    other = jnp.where(lane % HEAD_SIZE < h, pltpu.roll(u, 128 - h, 1), pltpu.roll(u, h, 1))
    return u * cosine + other * sine


def project_body(me, n1, w, cosine, sine, out, flat):
    @pl.when(pl.program_id(0) == 0)
    def _():
        flat[...] = assemble(w)

    u = dg(n1[...], flat[...], NN)
    turns = (HQ + HK) * HEAD_SIZE
    for c in range(0, turns, 128):
        out[:, c : c + 128] = turned(u[:, c : c + 128], cosine[...], sine[...]).astype(bf16)
    out[:, turns:] = u[:, turns:].astype(bf16)


def project(half, me, n1, w, cosine, sine, piece):
    n, _, rows, _ = w.shape
    width = WIDE
    batch = n1.shape[0] // piece
    return pl.pallas_call(
        project_body,
        grid_spec=pltpu.PrefetchScalarGridSpec(
            num_scalar_prefetch=1,
            grid=(batch,),
            in_specs=[
                pl.BlockSpec((piece, D), lambda b, m: (b, 0)),
                pl.BlockSpec((n, 1, rows, width), lambda b, m: (0, m[0] ^ half, 0, 0)),
                pl.BlockSpec((piece, 128), lambda b, m: (m[0], 0)),
                pl.BlockSpec((piece, 128), lambda b, m: (m[0], 0)),
            ],
            out_specs=[
                pl.BlockSpec((piece, width), lambda b, m: (b, 0)),
                pl.BlockSpec((D, width), lambda b, m: (0, 0)),
            ],
        ),
        out_shape=[
            jax.ShapeDtypeStruct((n1.shape[0], width), bf16),
            jax.ShapeDtypeStruct((D, width), bf16),
        ],
        compiler_params=pltpu.CompilerParams(vmem_limit_bytes=VMEM_BYTES),
        cost_estimate=pl.CostEstimate(flops=3 * 10**9, bytes_accessed=12 * 10**6, transcendentals=0),
        name="project",
    )(me, n1, w, cosine, sine)


def head_cols(j):
    return slice(j * HEAD_SIZE, (j + 1) * HEAD_SIZE)


def lane_of(j, shape):
    return lax.broadcasted_iota(jnp.int32, shape, 1) == j


def place(me, mine, got, q, k, v):
    piece = mine.shape[0]
    at = [pl.ds(pl.multiple_of((me[0] ^ a) * piece, piece), piece) for a in range(2)]
    for src, rows in zip((mine, got), at):
        for j in range(HQ):
            q[j, rows, :] = src[:, head_cols(j)] * jnp.asarray(0.125, bf16)
        for j in range(HK):
            k[j, rows, :] = src[:, head_cols(HQ + j)]
            v[j, rows, :] = src[:, head_cols(HQ + HK + j)]
    return at


def fwd_body(me, mine, got, o_mine, o_theirs, lse, q, k, v, o):
    at = place(me, mine, got, q, k, v)
    lse[...] = jnp.zeros_like(lse)

    def head(j, _):
        g = j // (HQ // HK)
        for i in range(lse.shape[0] // BLOCK):
            r = pl.ds(i * BLOCK, BLOCK)
            kw = (i + 1) * BLOCK
            s = dg(q[j, r, :], k[g, :kw, :], NT)
            m = jnp.max(s, axis=1, keepdims=True)
            p = jnp.exp(s - m)
            l = jnp.sum(p, axis=1, keepdims=True)
            mix = dg(p.astype(bf16), v[g, :kw, :], NN)
            o[j, r, :] = (mix / l).astype(bf16)
            lse[r, :] = jnp.where(lane_of(j, (BLOCK, 128)), m + jnp.log(l), lse[r, :])
        return 0

    lax.fori_loop(0, HQ, head, 0)
    for dst, rows in zip((o_mine, o_theirs), at):
        for j in range(HQ):
            dst[:, head_cols(j)] = o[j, rows, :]


def bwd_body(
    me, mine, got, o_mine, o_theirs, do_mine, do_got, lse, cosine, sine, *rest
):
    lin_mine, lin_theirs, q, k, v, do, d, dka, dva, inner = rest[-10:]
    at = place(me, mine, got, q, k, v)
    inner[...] = jnp.zeros_like(inner)
    for dsrc, osrc, rows in zip((do_mine, do_got), (o_mine, o_theirs), at):
        for j in range(HQ):
            dj = dsrc[:, head_cols(j)]
            do[j, rows, :] = dj
            part = jnp.sum(dj.astype(f32) * osrc[:, head_cols(j)].astype(f32), axis=1, keepdims=True)
            inner[rows, :] = jnp.where(lane_of(j, (dj.shape[0], 128)), part, inner[rows, :])

    def group(g, _):
        dka[...] = jnp.zeros_like(dka)
        dva[...] = jnp.zeros_like(dva)
        for jj in range(HQ // HK):
            j = g * (HQ // HK) + jj
            for i in range(lse.shape[0] // BLOCK):
                r = pl.ds(i * BLOCK, BLOCK)
                kw = (i + 1) * BLOCK
                mark = lane_of(j, (BLOCK, 128))
                column = lambda a: jnp.sum(jnp.where(mark, a[r, :], 0.0), axis=1, keepdims=True)
                qs = q[j, r, :]
                dO = do[j, r, :]
                kk = k[g, :kw, :]
                p = jnp.exp(dg(qs, kk, NT) - column(lse))
                dp = dg(dO, v[g, :kw, :], NT)
                ds = (p * (dp - column(inner))).astype(bf16)
                d[j, r, :] = dg(ds, kk, NN) * 0.125
                dka[:, :kw] += dg(qs.T, ds, NN)
                dva[:, :kw] += dg(dO.T, p.astype(bf16), NN)
        d[HQ + g] = dka[...].T
        d[HQ + HK + g] = dva[...].T
        return 0

    lax.fori_loop(0, HK, group, 0)
    turns = HQ + HK
    for dst, rows in zip((lin_mine, lin_theirs), at):
        for j in range(0, HALL + 1, 2):
            a = d[j, rows, :]
            b = d[j + 1, rows, :] if j + 1 < HALL else jnp.zeros_like(a)
            u = jnp.concatenate([a, b], 1)
            if j < turns:
                u = turned(u, cosine[rows, :], -sine[rows, :])
            dst[:, j * HEAD_SIZE : (j + 2) * HEAD_SIZE] = u.astype(bf16)


def attend(me, mine, got, piece):
    tokens, width = mine.shape
    batch = tokens // piece
    row = lambda a, c: pl.BlockSpec((a, c), lambda b, m: (b, 0))
    cols = HQ * HEAD_SIZE
    heads = lambda n: pltpu.VMEM((n, 2 * piece, HEAD_SIZE), bf16)
    return pl.pallas_call(
        fwd_body,
        grid_spec=pltpu.PrefetchScalarGridSpec(
            num_scalar_prefetch=1,
            grid=(batch,),
            in_specs=[row(piece, width)] * 2,
            out_specs=[row(piece, cols), row(piece, cols), row(2 * piece, 128)],
            scratch_shapes=[heads(HQ), heads(HK), heads(HK), heads(HQ)],
        ),
        out_shape=[
            jax.ShapeDtypeStruct((tokens, cols), bf16),
            jax.ShapeDtypeStruct((tokens, cols), bf16),
            jax.ShapeDtypeStruct((2 * tokens, 128), f32),
        ],
        compiler_params=pltpu.CompilerParams(vmem_limit_bytes=VMEM_BYTES),
        cost_estimate=pl.CostEstimate(flops=24 * 10**9, bytes_accessed=20 * 10**6, transcendentals=12 * 10**6),
        name="attend",
    )(me, mine, got)


def attend_back(b, before, me, mine, got, o_mine, o_theirs, do_mine, do_got, lse, cosine, sine, piece):
    tokens, width = mine.shape
    row = lambda a, c: pl.BlockSpec((a, c), lambda _, m: (b, 0))
    cols = HQ * HEAD_SIZE
    table = pl.BlockSpec((2 * piece, 128), lambda _, m: (0, 0))
    heads = lambda n, t: pltpu.VMEM((n, 2 * piece, HEAD_SIZE), t)
    return pl.pallas_call(
        bwd_body,
        grid_spec=pltpu.PrefetchScalarGridSpec(
            num_scalar_prefetch=1,
            grid=(1,),
            in_specs=[row(piece, width)] * 2
            + [row(piece, cols)] * 4
            + [row(2 * piece, 128), table, table]
            + [pl.BlockSpec(memory_space=pl.ANY)] * len(before),
            out_specs=[row(piece, width)] * 2,
            scratch_shapes=[heads(HQ, bf16), heads(HK, bf16), heads(HK, bf16), heads(HQ, bf16)]
            + [heads(HALL, f32)]
            + [pltpu.VMEM((HEAD_SIZE, 2 * piece), f32)] * 2
            + [pltpu.VMEM((2 * piece, 128), f32)],
        ),
        out_shape=[jax.ShapeDtypeStruct((tokens, width), bf16)] * 2,
        input_output_aliases={10 + i: i for i in range(len(before))},
        compiler_params=pltpu.CompilerParams(vmem_limit_bytes=VMEM_BYTES),
        cost_estimate=pl.CostEstimate(flops=13 * 10**9, bytes_accessed=20 * 10**6, transcendentals=6 * 10**6),
        name="attend_back",
    )(me, mine, got, o_mine, o_theirs, do_mine, do_got, lse, cosine, sine, *before)


def mlp_body(me, n2, n2t, cot, res, wg, wu, wd_mine, wd_theirs, out, gn, g_mine, g_theirs, gd_mine, gd_theirs, y, wd):
    t = pl.program_id(0)
    per = pl.num_programs(0) // 2

    @pl.when(t == 0)
    def _():
        y[...] = res[...]
        gn[...] = jnp.zeros_like(gn)

    half = wd_mine.shape[1]
    first = me[0] == 0

    @pl.when(first)
    def _():
        wd[:, :half] = wd_mine[...]
        wd[:, half:] = wd_theirs[...]

    @pl.when(jnp.logical_not(first))
    def _():
        wd[:, :half] = wd_theirs[...]
        wd[:, half:] = wd_mine[...]

    wgt, wut = assemble(wg), assemble(wu)
    gate = dg(n2[...], wgt, NN)
    up = dg(n2[...], wut, NN)
    gh = dg(cot[...], wd[...], NT)
    sig = jax.nn.sigmoid(gate)
    act = gate * sig
    hidden = (act * up).astype(bf16)
    ggv = (gh * up * sig * (1.0 + gate * (1.0 - sig))).astype(bf16)
    guv = (gh * act).astype(bf16)
    y[...] += dg(hidden, wd[...], NN)
    gdt = dg(hidden, cot[...], TN)
    gd_mine[...] = jnp.where(first, gdt[:, :half], gdt[:, half:]).astype(bf16)
    gd_theirs[...] = jnp.where(first, gdt[:, half:], gdt[:, :half]).astype(bf16)
    gg = dg(n2t[...], ggv, NN).astype(bf16)
    gu = dg(n2t[...], guv, NN).astype(bf16)

    @pl.when(t < per)
    def _():
        g_theirs[:, :FT] = gg
        g_theirs[:, FT:] = gu

    @pl.when(t >= per)
    def _():
        g_mine[:, :FT] = gg
        g_mine[:, FT:] = gu

    gn[...] += dg(ggv, wgt, NT) + dg(guv, wut, NT)

    @pl.when(t == pl.num_programs(0) - 1)
    def _():
        out[...] = y[...].astype(bf16)


def mlp(me, n2, n2t, cot, res, wide, wd_mine, wd_theirs):
    tokens = n2.shape[0]
    n, _, rows, _ = wide.shape
    cols = FF // 2
    per = cols // FT
    half = lambda t, m: 1 - m[0] ^ t // per
    whole = lambda a: pl.BlockSpec(a.shape, lambda t, m: (0, 0), pipeline_mode=pl.Buffered(1))
    col = lambda first: pl.BlockSpec(
        (n, 1, rows, FT), lambda t, m: (0, half(t, m), 0, first + t % per)
    )
    part = pl.BlockSpec((FT, D // 2), lambda t, m: (half(t, m) * per + t % per, 0))
    one = lambda: pl.BlockSpec((tokens, D), lambda t, m: (0, 0), pipeline_mode=pl.Buffered(1))
    return pl.pallas_call(
        mlp_body,
        grid_spec=pltpu.PrefetchScalarGridSpec(
            num_scalar_prefetch=1,
            grid=(FF // FT,),
            in_specs=[whole(n2), whole(n2t), whole(cot), whole(res), col(0), col(per), part, part],
            out_specs=[
                one(),
                one(),
                pl.BlockSpec((D, 2 * FT), lambda t, m: (0, jnp.maximum(t - per, 0))),
                pl.BlockSpec((D, 2 * FT), lambda t, m: (0, jnp.minimum(t, per - 1))),
                part,
                part,
            ],
            scratch_shapes=[pltpu.VMEM((tokens, D), f32), pltpu.VMEM((FT, D), bf16)],
        ),
        out_shape=[
            jax.ShapeDtypeStruct((tokens, D), bf16),
            jax.ShapeDtypeStruct((tokens, D), f32),
            jax.ShapeDtypeStruct((D, 2 * cols), bf16),
            jax.ShapeDtypeStruct((D, 2 * cols), bf16),
            jax.ShapeDtypeStruct((FF, D // 2), bf16),
            jax.ShapeDtypeStruct((FF, D // 2), bf16),
        ],
        compiler_params=pltpu.CompilerParams(vmem_limit_bytes=VMEM_BYTES),
        cost_estimate=pl.CostEstimate(flops=65 * 10**9, bytes_accessed=60 * 10**6, transcendentals=3 * 10**6),
        name="mlp",
    )(me, n2, n2t, cot, res, wide, wide, wd_mine, wd_theirs)


def norm_back(grad_norm, rows_in, scale_rows, gain_rows):
    weighted = grad_norm * gain_rows
    cube_rows = scale_rows * scale_rows * scale_rows
    return scale_rows * weighted - rows_in * cube_rows * jnp.mean(
        weighted * rows_in, -1, keepdims=True
    )


def swap(a):
    return lax.ppermute(a, "seq", [(0, 1), (1, 0)])


BOTH = ("dp", "seq")


def whole_halves(g):
    return jnp.swapaxes(g, 0, 1).reshape(1, 2, -1, g.shape[3])


def fetch(w):
    g = lax.all_gather(w, BOTH, axis=0, tiled=True).reshape(lax.axis_size("dp"), 2, *w.shape)
    return g if w.shape[0] % 8 == 0 else whole_halves(g)


def exchange(a, bit):
    return lax.ppermute(a, "dp", [(i, i ^ (1 << bit)) for i in range(lax.axis_size("dp"))])


def column_parts(cols):
    cut = cols // 256 * 128
    parts = (slice(0, cut), (0, 1)), (slice(cut, cols), (1, 0))
    return parts if cut else parts[1:]


def gather_doubling(w):
    bits = lax.axis_size("dp").bit_length() - 1
    dp = lax.axis_index("dp")
    out = []
    for part, order in column_parts(w.shape[1]):
        a, have = w[:, part], []
        for bit in list(range(bits))[:1:-1] + list(order[::-1]):
            got = exchange(a, bit)
            axis = sum(b > bit for b in have)
            have.append(bit)
            a = jnp.where((dp >> bit) & 1 == 0, jnp.stack([a, got], axis), jnp.stack([got, a], axis))
        out.append(a.reshape(-1, a.shape[-1]))
    mine = jnp.concatenate(out, 1)
    return mine, swap(mine)


def add(a, b):
    return a.astype(f32) + b.astype(f32)


class Halving:
    def __init__(self, mine, theirs, kind=bf16):
        self.kind = kind
        self.bits = lax.axis_size("dp").bit_length() - 1
        both = add(mine, swap(theirs)).astype(kind)
        self.left = [list(range(self.bits))[::-1] for _ in column_parts(mine.shape[1])]
        self.sums = []
        for part, _ in column_parts(mine.shape[1]):
            self.sums.append(both[:, part].reshape(*[2] * self.bits, -1, both[:, part].shape[1]))
        for i in range(2):
            for p, (_, order) in enumerate(column_parts(mine.shape[1])):
                self.step(p, order[i])

    def step(self, p, bit):
        axis = self.left[p].index(bit)
        self.left[p].remove(bit)
        mybit = (lax.axis_index("dp") >> bit) & 1
        a = self.sums[p]
        keep = lax.dynamic_index_in_dim(a, mybit, axis, keepdims=False)
        send = lax.dynamic_index_in_dim(a, 1 - mybit, axis, keepdims=False)
        a = add(keep, exchange(send, bit))
        self.sums[p] = a.astype(self.kind) if self.left[p] else a

    def finish(self):
        for bit in range(2, self.bits):
            for p in range(len(self.sums)):
                self.step(p, bit)
        return jnp.concatenate(self.sums, 1)


def local(
    layer_input,
    w_query,
    w_key,
    w_value,
    w_out,
    gain_attn,
    w_gate,
    w_up,
    w_down,
    gain_mlp,
    cotangent,
):
    batch, _, piece, _ = layer_input.shape
    tokens = batch * piece
    me = lax.axis_index("seq")
    me_arr = jnp.full((1,), me, jnp.int32)
    pick = lambda a, b: jnp.where(me == 0, a, b)
    h = HEAD_SIZE // 2
    frequency = 10000.0 ** (-2.0 * jnp.arange(h).astype(f32) / HEAD_SIZE)
    angles = jnp.arange(2 * piece).astype(f32)[:, None] * jnp.tile(frequency, 128 // h)[None, :]
    cosine = jnp.cos(angles)
    sine = jnp.sin(angles) * jnp.where(jnp.arange(128) % HEAD_SIZE < h, -1.0, 1.0)[None, :]

    gains = jnp.pad(jnp.stack([gain_attn, gain_mlp], 1), ((0, 0), (0, WIDE - QKV - 2)))
    full = fetch(jnp.concatenate([w_query, w_key, w_value, gains, w_out], 1))
    wide = fetch(jnp.concatenate([w_gate, w_up], 1))
    down_mine, down_theirs = gather_doubling(w_down)
    gain_one = full[:, 0, :, QKV].reshape(D).astype(f32)
    gain_two = full[:, 0, :, QKV + 1].reshape(D).astype(f32)
    out_halves = whole_halves(full[..., WIDE:])[0].reshape(2, 2, D // 2, D // 2)
    out_rows = lambda c: jnp.concatenate(
        [lax.dynamic_index_in_dim(out_halves[i], c, 0, keepdims=False) for i in range(2)], 1
    )
    out_mine, out_theirs = out_rows(me), out_rows(1 - me)

    floats = layer_input.reshape(tokens, D).astype(f32)
    cot = cotangent.reshape(tokens, D)
    scale_attn = lax.rsqrt(jnp.mean(floats * floats, -1, keepdims=True) + epsilon)
    n1 = (floats * scale_attn * gain_one).astype(bf16)
    dot = lambda a, b: lax.dot_general(a, b, NN, preferred_element_type=f32)

    heads_out, w_theirs = project(1, me_arr, n1, full, cosine, sine, piece)
    got = swap(heads_out)
    mine, w_mine = project(0, me_arr, n1, full, cosine, sine, piece)
    mixed, mixed_out, lse = attend(me_arr, mine, got, piece)
    mixed_got = swap(mixed_out)
    residual = floats + (dot(mixed, out_mine) + dot(mixed_got, out_theirs))
    scale_mlp = lax.rsqrt(jnp.mean(residual * residual, -1, keepdims=True) + epsilon)
    n2 = (residual * scale_mlp * gain_two).astype(bf16)
    layer_out, grad_n2, g_mine, g_theirs, gd_mine, gd_theirs = mlp(
        me_arr, n2, n2.T, cot, residual, wide, down_mine, down_theirs
    )
    r_wide = Halving(g_mine, g_theirs)
    r_down = Halving(gd_mine, gd_theirs)
    sum_gain_mlp = jnp.sum(grad_n2 * residual * scale_mlp, 0)
    grad_residual = cot.astype(f32) + norm_back(grad_n2, residual, scale_mlp, gain_two)
    grad_low = grad_residual.astype(bf16)
    d_out = lax.dot_general(grad_low, out_theirs, NT, preferred_element_type=f32).astype(bf16)
    d_got = swap(d_out)
    d_mine = lax.dot_general(grad_low, out_mine, NT, preferred_element_type=f32).astype(bf16)
    low = grad_low[:, : D // 2], grad_low[:, D // 2 :]

    def grad_out(columns):
        a = lax.dot_general(mixed, columns, TN, preferred_element_type=f32).astype(bf16)
        b = lax.dot_general(mixed_got, columns, TN, preferred_element_type=f32).astype(bf16)
        return pick(jnp.concatenate([a, b], 0), jnp.concatenate([b, a], 0))

    r_out = Halving(grad_out(pick(*low)), grad_out(pick(*low[::-1])))
    lins = ()
    for b in range(batch):
        lins = attend_back(
            b, lins, me_arr, mine, got, mixed, mixed_out, d_mine, d_got, lse, cosine, sine, piece
        )
    lin_mine, lin_out = lins
    lin_got = swap(lin_out)
    weight_grad = lambda lin: lax.dot_general(n1, lin, TN, preferred_element_type=f32).astype(bf16)
    lin_got, r_wide.sums, r_down.sums, r_out.sums = lax.optimization_barrier(
        (lin_got, r_wide.sums, r_down.sums, r_out.sums)
    )
    r_wide, r_down, r_out = r_wide.finish(), r_down.finish(), r_out.finish()
    r_pack = Halving(weight_grad(lin_mine), weight_grad(lin_got)).finish()
    grad_n1 = lax.dot_general(lin_mine, w_mine, NT, preferred_element_type=f32) + lax.dot_general(
        lin_got, w_theirs, NT, preferred_element_type=f32
    )
    sum_gain_attn = jnp.sum(grad_n1 * floats * scale_attn, 0)
    grad_input = (grad_residual + norm_back(grad_n1, floats, scale_attn, gain_one)).astype(bf16)
    sums = jnp.pad(jnp.stack([sum_gain_attn, sum_gain_mlp], 1), ((0, 0), (0, 126)))
    r_sums = Halving(sums, sums, f32).finish()
    r_gate, r_up = [
        a.reshape(a.shape[0], -1).astype(f32)
        for a in jnp.split(r_wide.reshape(-1, FF // 2 // FT, 2, FT), 2, 2)
    ]
    a, b, c = HQ * HEAD_SIZE, (HQ + HK) * HEAD_SIZE, QKV
    shape = layer_input.shape
    return (
        layer_out.reshape(shape),
        grad_input.reshape(shape),
        r_pack[:, :a],
        r_pack[:, a:b],
        r_pack[:, b:c],
        r_out,
        r_sums[:, 0],
        r_gate,
        r_up,
        r_down,
        r_sums[:, 1],
    )


def solution(mesh):
    tokens, matrix, vector = P(None, "dp", "seq", None), P("dp", "seq"), P("dp")
    placed = (tokens, *[matrix] * 4, vector, *[matrix] * 3, vector, tokens)
    return jax.shard_map(
        local,
        mesh=mesh,
        in_specs=placed,
        out_specs=(tokens, tokens, *[matrix] * 4, vector, *[matrix] * 3, vector),
        check_vma=False,
    )
```

```python
import functools

import jax
import jax.numpy as jnp
from jax import lax
from jax.experimental import pallas as pl
from jax.experimental.pallas import tpu as pltpu
from jax.sharding import PartitionSpec as P

D = 1152
QUERY_HEADS = 18
KEY_VALUE_HEADS = 6
HEAD_SIZE = 64
FF = 3072
BLOCK = 256
QD = 1152
KVD = 384
HQ, HK = QUERY_HEADS // 2, KEY_VALUE_HEADS // 2
HALL = HQ + 2 * HK
QKV = HALL * HEAD_SIZE
FT = 256
WIDE = 1024

epsilon = 1e-05
bf16, f32 = jnp.bfloat16, jnp.float32
NT = (((1,), (1,)), ((), ()))
NN = (((1,), (0,)), ((), ()))
TN = (((0,), (0,)), ((), ()))
VMEM_BYTES = 62 << 20


def dg(a, b, dims):
    return lax.dot_general(a, b, dims, preferred_element_type=f32)


def assemble(w):
    if w.shape[0] == 1:
        return w[0, 0]
    return jnp.concatenate([w[i, 0].astype(f32) for i in range(w.shape[0])], 0).astype(bf16)


def turned(u, cosine, sine):
    lane = lax.broadcasted_iota(jnp.int32, u.shape, 1)
    h = HEAD_SIZE // 2
    other = jnp.where(lane % HEAD_SIZE < h, pltpu.roll(u, 128 - h, 1), pltpu.roll(u, h, 1))
    return u * cosine + other * sine


def project_body(me, n1, w, cosine, sine, out, flat):
    @pl.when(pl.program_id(0) == 0)
    def _():
        flat[...] = assemble(w)

    u = dg(n1[...], flat[...], NN)
    turns = (HQ + HK) * HEAD_SIZE
    for c in range(0, turns, 128):
        out[:, c : c + 128] = turned(u[:, c : c + 128], cosine[...], sine[...]).astype(bf16)
    out[:, turns:] = u[:, turns:].astype(bf16)


def project(half, me, n1, w, cosine, sine, piece):
    n, _, rows, _ = w.shape
    width = WIDE
    batch = n1.shape[0] // piece
    return pl.pallas_call(
        project_body,
        grid_spec=pltpu.PrefetchScalarGridSpec(
            num_scalar_prefetch=1,
            grid=(batch,),
            in_specs=[
                pl.BlockSpec((piece, D), lambda b, m: (b, 0)),
                pl.BlockSpec((n, 1, rows, width), lambda b, m: (0, m[0] ^ half, 0, 0)),
                pl.BlockSpec((piece, 128), lambda b, m: (m[0], 0)),
                pl.BlockSpec((piece, 128), lambda b, m: (m[0], 0)),
            ],
            out_specs=[
                pl.BlockSpec((piece, width), lambda b, m: (b, 0)),
                pl.BlockSpec((D, width), lambda b, m: (0, 0)),
            ],
        ),
        out_shape=[
            jax.ShapeDtypeStruct((n1.shape[0], width), bf16),
            jax.ShapeDtypeStruct((D, width), bf16),
        ],
        compiler_params=pltpu.CompilerParams(vmem_limit_bytes=VMEM_BYTES),
        cost_estimate=pl.CostEstimate(flops=3 * 10**9, bytes_accessed=12 * 10**6, transcendentals=0),
        name="project",
    )(me, n1, w, cosine, sine)


def head_cols(j):
    return slice(j * HEAD_SIZE, (j + 1) * HEAD_SIZE)


def lane_of(j, shape):
    return lax.broadcasted_iota(jnp.int32, shape, 1) == j


def place(me, mine, got, q, k, v):
    piece = mine.shape[0]
    at = [pl.ds(pl.multiple_of((me[0] ^ a) * piece, piece), piece) for a in range(2)]
    for src, rows in zip((mine, got), at):
        for j in range(HQ):
            q[j, rows, :] = src[:, head_cols(j)] * jnp.asarray(0.125, bf16)
        for j in range(HK):
            k[j, rows, :] = src[:, head_cols(HQ + j)]
            v[j, rows, :] = src[:, head_cols(HQ + HK + j)]
    return at


def fwd_body(me, mine, got, o_mine, o_theirs, lse, q, k, v, o):
    at = place(me, mine, got, q, k, v)
    lse[...] = jnp.zeros_like(lse)

    def head(j, _):
        g = j // (HQ // HK)
        for i in range(lse.shape[0] // BLOCK):
            r = pl.ds(i * BLOCK, BLOCK)
            kw = (i + 1) * BLOCK
            s = dg(q[j, r, :], k[g, :kw, :], NT)
            m = jnp.max(s, axis=1, keepdims=True)
            p = jnp.exp(s - m)
            l = jnp.sum(p, axis=1, keepdims=True)
            mix = dg(p.astype(bf16), v[g, :kw, :], NN)
            o[j, r, :] = (mix / l).astype(bf16)
            lse[r, :] = jnp.where(lane_of(j, (BLOCK, 128)), m + jnp.log(l), lse[r, :])
        return 0

    lax.fori_loop(0, HQ, head, 0)
    for dst, rows in zip((o_mine, o_theirs), at):
        for j in range(HQ):
            dst[:, head_cols(j)] = o[j, rows, :]


def bwd_body(
    me, mine, got, o_mine, o_theirs, do_mine, do_got, lse, cosine, sine, *rest
):
    lin_mine, lin_theirs, q, k, v, do, d, dka, dva, inner = rest[-10:]
    at = place(me, mine, got, q, k, v)
    inner[...] = jnp.zeros_like(inner)
    for dsrc, osrc, rows in zip((do_mine, do_got), (o_mine, o_theirs), at):
        for j in range(HQ):
            dj = dsrc[:, head_cols(j)]
            do[j, rows, :] = dj
            part = jnp.sum(dj.astype(f32) * osrc[:, head_cols(j)].astype(f32), axis=1, keepdims=True)
            inner[rows, :] = jnp.where(lane_of(j, (dj.shape[0], 128)), part, inner[rows, :])

    def group(g, _):
        dka[...] = jnp.zeros_like(dka)
        dva[...] = jnp.zeros_like(dva)
        for jj in range(HQ // HK):
            j = g * (HQ // HK) + jj
            for i in range(lse.shape[0] // BLOCK):
                r = pl.ds(i * BLOCK, BLOCK)
                kw = (i + 1) * BLOCK
                mark = lane_of(j, (BLOCK, 128))
                column = lambda a: jnp.sum(jnp.where(mark, a[r, :], 0.0), axis=1, keepdims=True)
                qs = q[j, r, :]
                dO = do[j, r, :]
                kk = k[g, :kw, :]
                p = jnp.exp(dg(qs, kk, NT) - column(lse))
                dp = dg(dO, v[g, :kw, :], NT)
                ds = (p * (dp - column(inner))).astype(bf16)
                d[j, r, :] = dg(ds, kk, NN) * 0.125
                dka[:, :kw] += dg(qs.T, ds, NN)
                dva[:, :kw] += dg(dO.T, p.astype(bf16), NN)
        d[HQ + g] = dka[...].T
        d[HQ + HK + g] = dva[...].T
        return 0

    lax.fori_loop(0, HK, group, 0)
    turns = HQ + HK
    for dst, rows in zip((lin_mine, lin_theirs), at):
        for j in range(0, HALL + 1, 2):
            a = d[j, rows, :]
            b = d[j + 1, rows, :] if j + 1 < HALL else jnp.zeros_like(a)
            u = jnp.concatenate([a, b], 1)
            if j < turns:
                u = turned(u, cosine[rows, :], -sine[rows, :])
            dst[:, j * HEAD_SIZE : (j + 2) * HEAD_SIZE] = u.astype(bf16)


def attend(me, mine, got, piece):
    tokens, width = mine.shape
    batch = tokens // piece
    row = lambda a, c: pl.BlockSpec((a, c), lambda b, m: (b, 0))
    cols = HQ * HEAD_SIZE
    heads = lambda n: pltpu.VMEM((n, 2 * piece, HEAD_SIZE), bf16)
    return pl.pallas_call(
        fwd_body,
        grid_spec=pltpu.PrefetchScalarGridSpec(
            num_scalar_prefetch=1,
            grid=(batch,),
            in_specs=[row(piece, width)] * 2,
            out_specs=[row(piece, cols), row(piece, cols), row(2 * piece, 128)],
            scratch_shapes=[heads(HQ), heads(HK), heads(HK), heads(HQ)],
        ),
        out_shape=[
            jax.ShapeDtypeStruct((tokens, cols), bf16),
            jax.ShapeDtypeStruct((tokens, cols), bf16),
            jax.ShapeDtypeStruct((2 * tokens, 128), f32),
        ],
        compiler_params=pltpu.CompilerParams(vmem_limit_bytes=VMEM_BYTES),
        cost_estimate=pl.CostEstimate(flops=24 * 10**9, bytes_accessed=20 * 10**6, transcendentals=12 * 10**6),
        name="attend",
    )(me, mine, got)


def attend_back(b, before, me, mine, got, o_mine, o_theirs, do_mine, do_got, lse, cosine, sine, piece):
    tokens, width = mine.shape
    row = lambda a, c: pl.BlockSpec((a, c), lambda _, m: (b, 0))
    cols = HQ * HEAD_SIZE
    table = pl.BlockSpec((2 * piece, 128), lambda _, m: (0, 0))
    heads = lambda n, t: pltpu.VMEM((n, 2 * piece, HEAD_SIZE), t)
    return pl.pallas_call(
        bwd_body,
        grid_spec=pltpu.PrefetchScalarGridSpec(
            num_scalar_prefetch=1,
            grid=(1,),
            in_specs=[row(piece, width)] * 2
            + [row(piece, cols)] * 4
            + [row(2 * piece, 128), table, table]
            + [pl.BlockSpec(memory_space=pl.ANY)] * len(before),
            out_specs=[row(piece, width)] * 2,
            scratch_shapes=[heads(HQ, bf16), heads(HK, bf16), heads(HK, bf16), heads(HQ, bf16)]
            + [heads(HALL, f32)]
            + [pltpu.VMEM((HEAD_SIZE, 2 * piece), f32)] * 2
            + [pltpu.VMEM((2 * piece, 128), f32)],
        ),
        out_shape=[jax.ShapeDtypeStruct((tokens, width), bf16)] * 2,
        input_output_aliases={10 + i: i for i in range(len(before))},
        compiler_params=pltpu.CompilerParams(vmem_limit_bytes=VMEM_BYTES),
        cost_estimate=pl.CostEstimate(flops=13 * 10**9, bytes_accessed=20 * 10**6, transcendentals=6 * 10**6),
        name="attend_back",
    )(me, mine, got, o_mine, o_theirs, do_mine, do_got, lse, cosine, sine, *before)


def mlp_body(me, n2, n2t, cot, res, wg, wu, wd_mine, wd_theirs, out, gn, g_mine, g_theirs, gd_mine, gd_theirs, y, wd):
    t = pl.program_id(0)
    per = pl.num_programs(0) // 2

    @pl.when(t == 0)
    def _():
        y[...] = res[...]
        gn[...] = jnp.zeros_like(gn)

    half = wd_mine.shape[1]
    first = me[0] == 0

    @pl.when(first)
    def _():
        wd[:, :half] = wd_mine[...]
        wd[:, half:] = wd_theirs[...]

    @pl.when(jnp.logical_not(first))
    def _():
        wd[:, :half] = wd_theirs[...]
        wd[:, half:] = wd_mine[...]

    wgt, wut = assemble(wg), assemble(wu)
    gate = dg(n2[...], wgt, NN)
    up = dg(n2[...], wut, NN)
    gh = dg(cot[...], wd[...], NT)
    sig = jax.nn.sigmoid(gate)
    act = gate * sig
    hidden = (act * up).astype(bf16)
    ggv = (gh * up * sig * (1.0 + gate * (1.0 - sig))).astype(bf16)
    guv = (gh * act).astype(bf16)
    y[...] += dg(hidden, wd[...], NN)
    gdt = dg(hidden, cot[...], TN)
    gd_mine[...] = jnp.where(first, gdt[:, :half], gdt[:, half:]).astype(bf16)
    gd_theirs[...] = jnp.where(first, gdt[:, half:], gdt[:, :half]).astype(bf16)
    gg = dg(n2t[...], ggv, NN).astype(bf16)
    gu = dg(n2t[...], guv, NN).astype(bf16)

    @pl.when(t < per)
    def _():
        g_theirs[:, :FT] = gg
        g_theirs[:, FT:] = gu

    @pl.when(t >= per)
    def _():
        g_mine[:, :FT] = gg
        g_mine[:, FT:] = gu

    gn[...] += dg(ggv, wgt, NT) + dg(guv, wut, NT)

    @pl.when(t == pl.num_programs(0) - 1)
    def _():
        out[...] = y[...].astype(bf16)


def mlp(me, n2, n2t, cot, res, wide, wd_mine, wd_theirs):
    tokens = n2.shape[0]
    n, _, rows, _ = wide.shape
    cols = FF // 2
    per = cols // FT
    half = lambda t, m: 1 - m[0] ^ t // per
    whole = lambda a: pl.BlockSpec(a.shape, lambda t, m: (0, 0), pipeline_mode=pl.Buffered(1))
    col = lambda first: pl.BlockSpec(
        (n, 1, rows, FT), lambda t, m: (0, half(t, m), 0, first + t % per)
    )
    part = pl.BlockSpec((FT, D // 2), lambda t, m: (half(t, m) * per + t % per, 0))
    one = lambda: pl.BlockSpec((tokens, D), lambda t, m: (0, 0), pipeline_mode=pl.Buffered(1))
    return pl.pallas_call(
        mlp_body,
        grid_spec=pltpu.PrefetchScalarGridSpec(
            num_scalar_prefetch=1,
            grid=(FF // FT,),
            in_specs=[whole(n2), whole(n2t), whole(cot), whole(res), col(0), col(per), part, part],
            out_specs=[
                one(),
                one(),
                pl.BlockSpec((D, 2 * FT), lambda t, m: (0, jnp.maximum(t - per, 0))),
                pl.BlockSpec((D, 2 * FT), lambda t, m: (0, jnp.minimum(t, per - 1))),
                part,
                part,
            ],
            scratch_shapes=[pltpu.VMEM((tokens, D), f32), pltpu.VMEM((FT, D), bf16)],
        ),
        out_shape=[
            jax.ShapeDtypeStruct((tokens, D), bf16),
            jax.ShapeDtypeStruct((tokens, D), f32),
            jax.ShapeDtypeStruct((D, 2 * cols), bf16),
            jax.ShapeDtypeStruct((D, 2 * cols), bf16),
            jax.ShapeDtypeStruct((FF, D // 2), bf16),
            jax.ShapeDtypeStruct((FF, D // 2), bf16),
        ],
        compiler_params=pltpu.CompilerParams(vmem_limit_bytes=VMEM_BYTES),
        cost_estimate=pl.CostEstimate(flops=65 * 10**9, bytes_accessed=60 * 10**6, transcendentals=3 * 10**6),
        name="mlp",
    )(me, n2, n2t, cot, res, wide, wide, wd_mine, wd_theirs)


def norm_back(grad_norm, rows_in, scale_rows, gain_rows):
    weighted = grad_norm * gain_rows
    cube_rows = scale_rows * scale_rows * scale_rows
    return scale_rows * weighted - rows_in * cube_rows * jnp.mean(
        weighted * rows_in, -1, keepdims=True
    )


def swap(a):
    return lax.ppermute(a, "seq", [(0, 1), (1, 0)])


BOTH = ("dp", "seq")


def whole_halves(g):
    return jnp.swapaxes(g, 0, 1).reshape(1, 2, -1, g.shape[3])


def fetch(w):
    g = lax.all_gather(w, BOTH, axis=0, tiled=True).reshape(lax.axis_size("dp"), 2, *w.shape)
    return g if w.shape[0] % 8 == 0 else whole_halves(g)


def exchange(a, bit):
    return lax.ppermute(a, "dp", [(i, i ^ (1 << bit)) for i in range(lax.axis_size("dp"))])


def column_parts(cols, split=True):
    cut = cols // 256 * 128 * split
    parts = (slice(0, cut), (0, 1)), (slice(cut, cols), (1, 0))
    return parts if cut else parts[1:]


def gather_doubling(w):
    bits = lax.axis_size("dp").bit_length() - 1
    dp = lax.axis_index("dp")
    out = []
    for part, order in column_parts(w.shape[1]):
        a, have = w[:, part], []
        for bit in list(range(bits))[:1:-1] + list(order[::-1]):
            got = exchange(a, bit)
            axis = sum(b > bit for b in have)
            have.append(bit)
            a = jnp.where((dp >> bit) & 1 == 0, jnp.stack([a, got], axis), jnp.stack([got, a], axis))
        out.append(a.reshape(-1, a.shape[-1]))
    mine = jnp.concatenate(out, 1)
    return mine, swap(mine)


def add(a, b):
    return a.astype(f32) + b.astype(f32)


class Halving:
    def __init__(self, mine, theirs, kind=bf16, split=True):
        self.kind = kind
        bits = lax.axis_size("dp").bit_length() - 1
        self.steps = bits
        got = swap(theirs)
        self.orders, self.stay, self.got = [], [], []
        for part, order in column_parts(mine.shape[1], split):
            self.orders.append(list(order) + list(range(2, bits)))
            for to, u in ((self.stay, mine), (self.got, got)):
                to.append(u[:, part].reshape(*[2] * bits, -1, u[:, part].shape[1]))

    def prepare(self, step):
        self.send = []
        for p, order in enumerate(self.orders):
            bit = order[step]
            axis = sum(b > bit for b in order[step:])
            mybit = (lax.axis_index("dp") >> bit) & 1
            at = lambda u, i: lax.dynamic_index_in_dim(u, i, axis, keepdims=False)
            total = lambda i: add(at(self.stay[p], i), at(self.got[p], i)).astype(self.kind)
            self.send.append(total(1 - mybit))
            self.stay[p] = total(mybit)

    def move(self, step):
        self.got = [exchange(a, order[step]) for a, order in zip(self.send, self.orders)]

    def advance(self, step):
        self.prepare(step)
        self.move(step)

    def finish(self, step=0):
        for i in range(step, self.steps):
            self.advance(i)
        return jnp.concatenate([add(*u) for u in zip(self.stay, self.got)], 1)


def local(
    layer_input,
    w_query,
    w_key,
    w_value,
    w_out,
    gain_attn,
    w_gate,
    w_up,
    w_down,
    gain_mlp,
    cotangent,
):
    batch, _, piece, _ = layer_input.shape
    tokens = batch * piece
    me = lax.axis_index("seq")
    me_arr = jnp.full((1,), me, jnp.int32)
    pick = lambda a, b: jnp.where(me == 0, a, b)
    h = HEAD_SIZE // 2
    frequency = 10000.0 ** (-2.0 * jnp.arange(h).astype(f32) / HEAD_SIZE)
    angles = jnp.arange(2 * piece).astype(f32)[:, None] * jnp.tile(frequency, 128 // h)[None, :]
    cosine = jnp.cos(angles)
    sine = jnp.sin(angles) * jnp.where(jnp.arange(128) % HEAD_SIZE < h, -1.0, 1.0)[None, :]

    gains = jnp.pad(jnp.stack([gain_attn, gain_mlp], 1), ((0, 0), (0, WIDE - QKV - 2)))
    full = fetch(jnp.concatenate([w_query, w_key, w_value, gains, w_out], 1))
    wide = fetch(jnp.concatenate([w_gate, w_up], 1))
    down_mine, down_theirs = gather_doubling(w_down)
    gain_one = full[:, 0, :, QKV].reshape(D).astype(f32)
    gain_two = full[:, 0, :, QKV + 1].reshape(D).astype(f32)
    out_halves = whole_halves(full[..., WIDE:])[0].reshape(2, 2, D // 2, D // 2)
    out_rows = lambda c: jnp.concatenate(
        [lax.dynamic_index_in_dim(out_halves[i], c, 0, keepdims=False) for i in range(2)], 1
    )
    out_mine, out_theirs = out_rows(me), out_rows(1 - me)

    floats = layer_input.reshape(tokens, D).astype(f32)
    cot = cotangent.reshape(tokens, D)
    scale_attn = lax.rsqrt(jnp.mean(floats * floats, -1, keepdims=True) + epsilon)
    n1 = (floats * scale_attn * gain_one).astype(bf16)
    dot = lambda a, b: lax.dot_general(a, b, NN, preferred_element_type=f32)

    heads_out, w_theirs = project(1, me_arr, n1, full, cosine, sine, piece)
    got = swap(heads_out)
    mine, w_mine = project(0, me_arr, n1, full, cosine, sine, piece)
    mixed, mixed_out, lse = attend(me_arr, mine, got, piece)
    mixed_got = swap(mixed_out)
    residual = floats + (dot(mixed, out_mine) + dot(mixed_got, out_theirs))
    scale_mlp = lax.rsqrt(jnp.mean(residual * residual, -1, keepdims=True) + epsilon)
    n2 = (residual * scale_mlp * gain_two).astype(bf16)
    layer_out, grad_n2, g_mine, g_theirs, gd_mine, gd_theirs = mlp(
        me_arr, n2, n2.T, cot, residual, wide, down_mine, down_theirs
    )
    tie = lax.optimization_barrier
    wide_sum, down_sum = Halving(g_mine, g_theirs), Halving(gd_mine, gd_theirs)
    sum_gain_mlp = jnp.sum(grad_n2 * residual * scale_mlp, 0)
    grad_residual = cot.astype(f32) + norm_back(grad_n2, residual, scale_mlp, gain_two)
    grad_low = grad_residual.astype(bf16)
    d_out = lax.dot_general(grad_low, out_theirs, NT, preferred_element_type=f32).astype(bf16)
    d_got = swap(d_out)
    d_mine = lax.dot_general(grad_low, out_mine, NT, preferred_element_type=f32).astype(bf16)
    low = grad_low[:, : D // 2], grad_low[:, D // 2 :]

    def grad_out(columns):
        a = lax.dot_general(mixed, columns, TN, preferred_element_type=f32).astype(bf16)
        b = lax.dot_general(mixed_got, columns, TN, preferred_element_type=f32).astype(bf16)
        return pick(jnp.concatenate([a, b], 0), jnp.concatenate([b, a], 0))

    out_sum = Halving(grad_out(pick(*low)), grad_out(pick(*low[::-1])), split=False)
    early = wide_sum, down_sum, out_sum
    for u in early:
        u.prepare(0)
    (d_mine, d_got), sends = tie(((d_mine, d_got), [u.send for u in early]))
    for u, send in zip(early, sends):
        u.send = send
        u.move(0)
    lins = ()
    for b in range(batch):
        lins = attend_back(
            b, lins, me_arr, mine, got, mixed, mixed_out, d_mine, d_got, lse, cosine, sine, piece
        )
    (lin_mine, lin_out), gots = tie((lins, [u.got for u in early]))
    for u, arrived in zip(early, gots):
        u.got = arrived
        u.advance(1)
    lin_got = swap(lin_out)
    weight_grad = lambda lin: lax.dot_general(n1, lin, TN, preferred_element_type=f32).astype(bf16)
    pack_sum = Halving(weight_grad(lin_mine), weight_grad(lin_got))
    pack_sum.prepare(0)
    pack_sum.send, gots = tie((pack_sum.send, [u.got for u in early]))
    pack_sum.move(0)
    for u, arrived in zip(early, gots):
        u.got = arrived
        u.advance(2)
    grad_n1 = lax.dot_general(lin_mine, w_mine, NT, preferred_element_type=f32) + lax.dot_general(
        lin_got, w_theirs, NT, preferred_element_type=f32
    )
    grad_n1, pack_sum.got, gots = tie((grad_n1, pack_sum.got, [u.got for u in early]))
    pack_sum.advance(1)
    for u, arrived in zip(early, gots):
        u.got = arrived
    sum_gain_attn = jnp.sum(grad_n1 * floats * scale_attn, 0)
    grad_input = (grad_residual + norm_back(grad_n1, floats, scale_attn, gain_one)).astype(bf16)
    sums = jnp.pad(jnp.stack([sum_gain_attn, sum_gain_mlp], 1), ((0, 0), (0, 126)))
    r_wide, r_down, r_out = [u.finish(3) for u in early]
    r_pack = pack_sum.finish(2)
    r_sums = Halving(sums, sums, f32).finish()
    r_gate, r_up = [
        a.reshape(a.shape[0], -1).astype(f32)
        for a in jnp.split(r_wide.reshape(-1, FF // 2 // FT, 2, FT), 2, 2)
    ]
    a, b, c = HQ * HEAD_SIZE, (HQ + HK) * HEAD_SIZE, QKV
    shape = layer_input.shape
    return (
        layer_out.reshape(shape),
        grad_input.reshape(shape),
        r_pack[:, :a],
        r_pack[:, a:b],
        r_pack[:, b:c],
        r_out,
        r_sums[:, 0],
        r_gate,
        r_up,
        r_down,
        r_sums[:, 1],
    )


def solution(mesh):
    tokens, matrix, vector = P(None, "dp", "seq", None), P("dp", "seq"), P("dp")
    placed = (tokens, *[matrix] * 4, vector, *[matrix] * 3, vector, tokens)
    return jax.shard_map(
        local,
        mesh=mesh,
        in_specs=placed,
        out_specs=(tokens, tokens, *[matrix] * 4, vector, *[matrix] * 3, vector),
        check_vma=False,
    )
```

```python
import functools

import jax
import jax.numpy as jnp
from jax import lax
from jax.experimental import pallas as pl
from jax.experimental.pallas import tpu as pltpu
from jax.sharding import PartitionSpec as P

D = 1152
QUERY_HEADS = 18
KEY_VALUE_HEADS = 6
HEAD_SIZE = 64
FF = 3072
BLOCK = 256
QD = 1152
KVD = 384
HQ, HK = QUERY_HEADS // 2, KEY_VALUE_HEADS // 2
HALL = HQ + 2 * HK
QKV = HALL * HEAD_SIZE
FT = 256
HALF = 640
WIDE = 1024

epsilon = 1e-05
bf16, f32 = jnp.bfloat16, jnp.float32
NT = (((1,), (1,)), ((), ()))
NN = (((1,), (0,)), ((), ()))
TN = (((0,), (0,)), ((), ()))
VMEM_BYTES = 62 << 20


def dg(a, b, dims):
    return lax.dot_general(a, b, dims, preferred_element_type=f32)


def assemble(w):
    if w.shape[0] == 1:
        return w[0, 0]
    return jnp.concatenate([w[i, 0].astype(f32) for i in range(w.shape[0])], 0).astype(bf16)


def turned(u, cosine, sine):
    lane = lax.broadcasted_iota(jnp.int32, u.shape, 1)
    h = HEAD_SIZE // 2
    other = jnp.where(lane % HEAD_SIZE < h, pltpu.roll(u, 128 - h, 1), pltpu.roll(u, h, 1))
    return u * cosine + other * sine


def project_body(me, n1, w, cosine, sine, out, flat):
    @pl.when(pl.program_id(0) == 0)
    def _():
        flat[...] = assemble(w)

    u = dg(n1[...], flat[...], NN)
    turns = (HQ + HK) * HEAD_SIZE
    for c in range(0, turns, 128):
        out[:, c : c + 128] = turned(u[:, c : c + 128], cosine[...], sine[...]).astype(bf16)
    out[:, turns:] = u[:, turns:].astype(bf16)


def project(half, me, n1, w, cosine, sine, piece):
    n, _, rows, _ = w.shape
    width = WIDE
    batch = n1.shape[0] // piece
    return pl.pallas_call(
        project_body,
        grid_spec=pltpu.PrefetchScalarGridSpec(
            num_scalar_prefetch=1,
            grid=(batch,),
            in_specs=[
                pl.BlockSpec((piece, D), lambda b, m: (b, 0)),
                pl.BlockSpec((n, 1, rows, width), lambda b, m: (0, m[0] ^ half, 0, 0)),
                pl.BlockSpec((piece, 128), lambda b, m: (m[0], 0)),
                pl.BlockSpec((piece, 128), lambda b, m: (m[0], 0)),
            ],
            out_specs=[
                pl.BlockSpec((piece, width), lambda b, m: (b, 0)),
                pl.BlockSpec((D, width), lambda b, m: (0, 0)),
            ],
        ),
        out_shape=[
            jax.ShapeDtypeStruct((n1.shape[0], width), bf16),
            jax.ShapeDtypeStruct((D, width), bf16),
        ],
        compiler_params=pltpu.CompilerParams(vmem_limit_bytes=VMEM_BYTES),
        cost_estimate=pl.CostEstimate(flops=3 * 10**9, bytes_accessed=12 * 10**6, transcendentals=0),
        name="project",
    )(me, n1, w, cosine, sine)


def head_cols(j):
    return slice(j * HEAD_SIZE, (j + 1) * HEAD_SIZE)


def lane_of(j, shape):
    return lax.broadcasted_iota(jnp.int32, shape, 1) == j


def place(me, mine, got, q, k, v):
    piece = mine.shape[0]
    at = [pl.ds(pl.multiple_of((me[0] ^ a) * piece, piece), piece) for a in range(2)]
    for src, rows in zip((mine, got), at):
        for j in range(HQ):
            q[j, rows, :] = src[:, head_cols(j)] * jnp.asarray(0.125, bf16)
        for j in range(HK):
            k[j, rows, :] = src[:, head_cols(HQ + j)]
            v[j, rows, :] = src[:, head_cols(HQ + HK + j)]
    return at


def fwd_body(me, mine, got, o_mine, o_theirs, lse, q, k, v, o):
    at = place(me, mine, got, q, k, v)
    lse[...] = jnp.zeros_like(lse)

    def head(j, _):
        g = j // (HQ // HK)
        for i in range(lse.shape[0] // BLOCK):
            r = pl.ds(i * BLOCK, BLOCK)
            kw = (i + 1) * BLOCK
            s = dg(q[j, r, :], k[g, :kw, :], NT)
            m = jnp.max(s, axis=1, keepdims=True)
            p = jnp.exp(s - m)
            l = jnp.sum(p, axis=1, keepdims=True)
            mix = dg(p.astype(bf16), v[g, :kw, :], NN)
            o[j, r, :] = (mix / l).astype(bf16)
            lse[r, :] = jnp.where(lane_of(j, (BLOCK, 128)), m + jnp.log(l), lse[r, :])
        return 0

    lax.fori_loop(0, HQ, head, 0)
    for dst, rows in zip((o_mine, o_theirs), at):
        for j in range(HQ):
            dst[:, head_cols(j)] = o[j, rows, :]
        dst[:, HQ * HEAD_SIZE :] = jnp.zeros_like(dst[:, HQ * HEAD_SIZE :])


def bwd_body(
    me, mine, got, o_mine, o_theirs, do_mine, do_got, lse, cosine, sine, *rest
):
    lin_mine, lin_theirs, q, k, v, do, d, dka, dva, inner = rest[-10:]
    at = place(me, mine, got, q, k, v)
    inner[...] = jnp.zeros_like(inner)
    for dsrc, osrc, rows in zip((do_mine, do_got), (o_mine, o_theirs), at):
        for j in range(HQ):
            dj = dsrc[:, head_cols(j)]
            do[j, rows, :] = dj
            part = jnp.sum(dj.astype(f32) * osrc[:, head_cols(j)].astype(f32), axis=1, keepdims=True)
            inner[rows, :] = jnp.where(lane_of(j, (dj.shape[0], 128)), part, inner[rows, :])

    def group(g, _):
        dka[...] = jnp.zeros_like(dka)
        dva[...] = jnp.zeros_like(dva)
        for jj in range(HQ // HK):
            j = g * (HQ // HK) + jj
            for i in range(lse.shape[0] // BLOCK):
                r = pl.ds(i * BLOCK, BLOCK)
                kw = (i + 1) * BLOCK
                mark = lane_of(j, (BLOCK, 128))
                column = lambda a: jnp.sum(jnp.where(mark, a[r, :], 0.0), axis=1, keepdims=True)
                qs = q[j, r, :]
                dO = do[j, r, :]
                kk = k[g, :kw, :]
                p = jnp.exp(dg(qs, kk, NT) - column(lse))
                dp = dg(dO, v[g, :kw, :], NT)
                ds = (p * (dp - column(inner))).astype(bf16)
                d[j, r, :] = dg(ds, kk, NN) * 0.125
                dka[:, :kw] += dg(qs.T, ds, NN)
                dva[:, :kw] += dg(dO.T, p.astype(bf16), NN)
        d[HQ + g] = dka[...].T
        d[HQ + HK + g] = dva[...].T
        return 0

    lax.fori_loop(0, HK, group, 0)
    turns = HQ + HK
    for dst, rows in zip((lin_mine, lin_theirs), at):
        for j in range(0, HALL + 1, 2):
            a = d[j, rows, :]
            b = d[j + 1, rows, :] if j + 1 < HALL else jnp.zeros_like(a)
            u = jnp.concatenate([a, b], 1)
            if j < turns:
                u = turned(u, cosine[rows, :], -sine[rows, :])
            dst[:, j * HEAD_SIZE : (j + 2) * HEAD_SIZE] = u.astype(bf16)


def attend(me, mine, got, piece):
    tokens, width = mine.shape
    batch = tokens // piece
    row = lambda a, c: pl.BlockSpec((a, c), lambda b, m: (b, 0))
    cols = HALF
    heads = lambda n: pltpu.VMEM((n, 2 * piece, HEAD_SIZE), bf16)
    return pl.pallas_call(
        fwd_body,
        grid_spec=pltpu.PrefetchScalarGridSpec(
            num_scalar_prefetch=1,
            grid=(batch,),
            in_specs=[row(piece, width)] * 2,
            out_specs=[row(piece, cols), row(piece, cols), row(2 * piece, 128)],
            scratch_shapes=[heads(HQ), heads(HK), heads(HK), heads(HQ)],
        ),
        out_shape=[
            jax.ShapeDtypeStruct((tokens, cols), bf16),
            jax.ShapeDtypeStruct((tokens, cols), bf16),
            jax.ShapeDtypeStruct((2 * tokens, 128), f32),
        ],
        compiler_params=pltpu.CompilerParams(vmem_limit_bytes=VMEM_BYTES),
        cost_estimate=pl.CostEstimate(flops=24 * 10**9, bytes_accessed=20 * 10**6, transcendentals=12 * 10**6),
        name="attend",
    )(me, mine, got)


def attend_back(b, before, me, mine, got, o_mine, o_theirs, do_mine, do_got, lse, cosine, sine, piece):
    tokens, width = mine.shape
    row = lambda a, c: pl.BlockSpec((a, c), lambda _, m: (b, 0))
    cols = HALF
    table = pl.BlockSpec((2 * piece, 128), lambda _, m: (0, 0))
    heads = lambda n, t: pltpu.VMEM((n, 2 * piece, HEAD_SIZE), t)
    return pl.pallas_call(
        bwd_body,
        grid_spec=pltpu.PrefetchScalarGridSpec(
            num_scalar_prefetch=1,
            grid=(1,),
            in_specs=[row(piece, width)] * 2
            + [row(piece, cols)] * 4
            + [row(2 * piece, 128), table, table]
            + [pl.BlockSpec(memory_space=pl.ANY)] * len(before),
            out_specs=[row(piece, width)] * 2,
            scratch_shapes=[heads(HQ, bf16), heads(HK, bf16), heads(HK, bf16), heads(HQ, bf16)]
            + [heads(HALL, f32)]
            + [pltpu.VMEM((HEAD_SIZE, 2 * piece), f32)] * 2
            + [pltpu.VMEM((2 * piece, 128), f32)],
        ),
        out_shape=[jax.ShapeDtypeStruct((tokens, width), bf16)] * 2,
        input_output_aliases={10 + i: i for i in range(len(before))},
        compiler_params=pltpu.CompilerParams(vmem_limit_bytes=VMEM_BYTES),
        cost_estimate=pl.CostEstimate(flops=13 * 10**9, bytes_accessed=20 * 10**6, transcendentals=6 * 10**6),
        name="attend_back",
    )(me, mine, got, o_mine, o_theirs, do_mine, do_got, lse, cosine, sine, *before)


def mlp_body(me, n2, n2t, cot, res, wg, wu, wd_mine, wd_theirs, out, gn, gg_mine, gu_mine, gg_theirs, gu_theirs, gd_mine, gd_theirs, y, wd):
    t = pl.program_id(0)
    per = pl.num_programs(0) // 2

    @pl.when(t == 0)
    def _():
        y[...] = res[...]
        gn[...] = jnp.zeros_like(gn)

    half = D // 2
    first = me[0] == 0

    @pl.when(first)
    def _():
        wd[:, :half] = wd_mine[:, :half]
        wd[:, half:] = wd_theirs[:, :half]

    @pl.when(jnp.logical_not(first))
    def _():
        wd[:, :half] = wd_theirs[:, :half]
        wd[:, half:] = wd_mine[:, :half]

    wgt, wut = assemble(wg), assemble(wu)
    gate = dg(n2[...], wgt, NN)
    up = dg(n2[...], wut, NN)
    gh = dg(cot[...], wd[...], NT)
    sig = jax.nn.sigmoid(gate)
    act = gate * sig
    hidden = (act * up).astype(bf16)
    ggv = (gh * up * sig * (1.0 + gate * (1.0 - sig))).astype(bf16)
    guv = (gh * act).astype(bf16)
    y[...] += dg(hidden, wd[...], NN)
    gdt = dg(hidden, cot[...], TN)
    for dst, u in (
        (gd_mine, jnp.where(first, gdt[:, :half], gdt[:, half:])),
        (gd_theirs, jnp.where(first, gdt[:, half:], gdt[:, :half])),
    ):
        dst[:, :half] = u.astype(bf16)
        dst[:, half:] = jnp.zeros((FT, HALF - half), bf16)
    gg = dg(n2t[...], ggv, NN).astype(bf16)
    gu = dg(n2t[...], guv, NN).astype(bf16)

    @pl.when(t < per)
    def _():
        gg_theirs[...] = gg
        gu_theirs[...] = gu

    @pl.when(t >= per)
    def _():
        gg_mine[...] = gg
        gu_mine[...] = gu

    gn[...] += dg(ggv, wgt, NT) + dg(guv, wut, NT)

    @pl.when(t == pl.num_programs(0) - 1)
    def _():
        out[...] = y[...].astype(bf16)


def mlp(me, n2, n2t, cot, res, wide, wd_mine, wd_theirs):
    tokens = n2.shape[0]
    n, _, rows, _ = wide.shape
    cols = FF // 2
    per = cols // FT
    half = lambda t, m: 1 - m[0] ^ t // per
    whole = lambda a: pl.BlockSpec(a.shape, lambda t, m: (0, 0), pipeline_mode=pl.Buffered(1))
    col = lambda first: pl.BlockSpec(
        (n, 1, rows, FT), lambda t, m: (0, half(t, m), 0, first + t % per)
    )
    part = pl.BlockSpec((FT, HALF), lambda t, m: (half(t, m) * per + t % per, 0))
    one = lambda: pl.BlockSpec((tokens, D), lambda t, m: (0, 0), pipeline_mode=pl.Buffered(1))
    return pl.pallas_call(
        mlp_body,
        grid_spec=pltpu.PrefetchScalarGridSpec(
            num_scalar_prefetch=1,
            grid=(FF // FT,),
            in_specs=[whole(n2), whole(n2t), whole(cot), whole(res), col(0), col(per), part, part],
            out_specs=[
                one(),
                one(),
                *[pl.BlockSpec((D, FT), lambda t, m: (0, jnp.maximum(t - per, 0)))] * 2,
                *[pl.BlockSpec((D, FT), lambda t, m: (0, jnp.minimum(t, per - 1)))] * 2,
                part,
                part,
            ],
            scratch_shapes=[pltpu.VMEM((tokens, D), f32), pltpu.VMEM((FT, D), bf16)],
        ),
        out_shape=[
            jax.ShapeDtypeStruct((tokens, D), bf16),
            jax.ShapeDtypeStruct((tokens, D), f32),
            *[jax.ShapeDtypeStruct((D, cols), bf16)] * 4,
            jax.ShapeDtypeStruct((FF, HALF), bf16),
            jax.ShapeDtypeStruct((FF, HALF), bf16),
        ],
        compiler_params=pltpu.CompilerParams(vmem_limit_bytes=VMEM_BYTES),
        cost_estimate=pl.CostEstimate(flops=65 * 10**9, bytes_accessed=60 * 10**6, transcendentals=3 * 10**6),
        name="mlp",
    )(me, n2, n2t, cot, res, wide, wide, wd_mine, wd_theirs)


def norm_back(grad_norm, rows_in, scale_rows, gain_rows):
    weighted = grad_norm * gain_rows
    cube_rows = scale_rows * scale_rows * scale_rows
    return scale_rows * weighted - rows_in * cube_rows * jnp.mean(
        weighted * rows_in, -1, keepdims=True
    )


def swap(a):
    return lax.ppermute(a, "seq", [(0, 1), (1, 0)])


BOTH = ("dp", "seq")


def whole_halves(g):
    return jnp.swapaxes(g, 0, 1).reshape(1, 2, -1, g.shape[3])


def fetch(w):
    g = lax.all_gather(w, BOTH, axis=0, tiled=True).reshape(lax.axis_size("dp"), 2, *w.shape)
    return g if w.shape[0] % 8 == 0 else whole_halves(g)


def exchange(a, bit):
    return lax.ppermute(a, "dp", [(i, i ^ (1 << bit)) for i in range(lax.axis_size("dp"))])


ORDERS = (0, 1), (1, 0)


def gather_doubling(w):
    bits = lax.axis_size("dp").bit_length() - 1
    dp = lax.axis_index("dp")
    cut = w.shape[1] // 256 * 128
    out = []
    for part, order in ((w[:, :cut], ORDERS[0]), (w[:, cut:], ORDERS[1])):
        a, have = part, []
        for bit in list(range(bits))[:1:-1] + list(order[::-1]):
            got = exchange(a, bit)
            axis = sum(b > bit for b in have)
            have.append(bit)
            a = jnp.where((dp >> bit) & 1 == 0, jnp.stack([a, got], axis), jnp.stack([got, a], axis))
        out.append(a.reshape(-1, a.shape[-1]))
    mine = jnp.concatenate(out, 1)
    return mine, swap(mine)


def add(a, b):
    return a.astype(f32) + b.astype(f32)


class Halving:
    def __init__(self, parts, kind=bf16):
        self.kind = kind
        bits = lax.axis_size("dp").bit_length() - 1
        self.steps = bits
        self.orders = [[*order, *range(2, bits)] for _, _, order in parts]
        shape = lambda u: u.reshape(*[2] * bits, -1, u.shape[-1])
        self.stay = [shape(u) for u, _, _ in parts]
        self.got = [shape(v) for _, v, _ in parts]

    def prepare(self, step):
        self.send = []
        for p, order in enumerate(self.orders):
            bit = order[step]
            axis = sum(b > bit for b in order[step:])
            mybit = (lax.axis_index("dp") >> bit) & 1
            at = lambda u, i: lax.dynamic_index_in_dim(u, i, axis, keepdims=False)
            total = lambda i: add(at(self.stay[p], i), at(self.got[p], i)).astype(self.kind)
            self.send.append(total(1 - mybit))
            self.stay[p] = total(mybit)

    def move(self, step):
        self.got = [exchange(a, order[step]) for a, order in zip(self.send, self.orders)]

    def advance(self, step):
        self.prepare(step)
        self.move(step)

    def finish(self, step=0):
        for i in range(step, self.steps):
            self.advance(i)
        return [add(*u) for u in zip(self.stay, self.got)]


def local(
    layer_input,
    w_query,
    w_key,
    w_value,
    w_out,
    gain_attn,
    w_gate,
    w_up,
    w_down,
    gain_mlp,
    cotangent,
):
    batch, _, piece, _ = layer_input.shape
    tokens = batch * piece
    me = lax.axis_index("seq")
    me_arr = jnp.full((1,), me, jnp.int32)
    pick = lambda a, b: jnp.where(me == 0, a, b)
    h = HEAD_SIZE // 2
    frequency = 10000.0 ** (-2.0 * jnp.arange(h).astype(f32) / HEAD_SIZE)
    angles = jnp.arange(2 * piece).astype(f32)[:, None] * jnp.tile(frequency, 128 // h)[None, :]
    cosine = jnp.cos(angles)
    sine = jnp.sin(angles) * jnp.where(jnp.arange(128) % HEAD_SIZE < h, -1.0, 1.0)[None, :]

    gains = jnp.pad(jnp.stack([gain_attn, gain_mlp], 1), ((0, 0), (0, WIDE - QKV - 2)))
    full = fetch(jnp.concatenate([w_query, w_key, w_value, gains, w_out], 1))
    wide = fetch(jnp.concatenate([w_gate, w_up], 1))
    widen = lambda a: jnp.pad(a, ((0, 0), (0, HALF - D // 2)))
    down_mine, down_theirs = gather_doubling(widen(w_down))
    gain_one = full[:, 0, :, QKV].reshape(D).astype(f32)
    gain_two = full[:, 0, :, QKV + 1].reshape(D).astype(f32)
    out_halves = whole_halves(full[..., WIDE:])[0].reshape(2, 2, D // 2, D // 2)
    out_rows = lambda c: jnp.concatenate(
        [lax.dynamic_index_in_dim(out_halves[i], c, 0, keepdims=False) for i in range(2)], 1
    )
    out_mine, out_theirs = [jnp.pad(out_rows(c), ((0, HALF - D // 2), (0, 0))) for c in (me, 1 - me)]

    floats = layer_input.reshape(tokens, D).astype(f32)
    cot = cotangent.reshape(tokens, D)
    scale_attn = lax.rsqrt(jnp.mean(floats * floats, -1, keepdims=True) + epsilon)
    n1 = (floats * scale_attn * gain_one).astype(bf16)
    dot = lambda a, b: lax.dot_general(a, b, NN, preferred_element_type=f32)

    heads_out, w_theirs = project(1, me_arr, n1, full, cosine, sine, piece)
    got = swap(heads_out)
    mine, w_mine = project(0, me_arr, n1, full, cosine, sine, piece)
    mixed, mixed_out, lse = attend(me_arr, mine, got, piece)
    mixed_got = swap(mixed_out)
    residual = floats + (dot(mixed, out_mine) + dot(mixed_got, out_theirs))
    scale_mlp = lax.rsqrt(jnp.mean(residual * residual, -1, keepdims=True) + epsilon)
    n2 = (residual * scale_mlp * gain_two).astype(bf16)
    layer_out, grad_n2, gg_mine, gu_mine, gg_theirs, gu_theirs, gd_mine, gd_theirs = mlp(
        me_arr, n2, n2.T, cot, residual, wide, down_mine, down_theirs
    )
    tie = lax.optimization_barrier
    wide_sum = Halving([(gg_mine, swap(gg_theirs), ORDERS[0]), (gu_mine, swap(gu_theirs), ORDERS[1])])
    wide_sum.prepare(0)
    sum_gain_mlp = jnp.sum(grad_n2 * residual * scale_mlp, 0)
    grad_residual = cot.astype(f32) + norm_back(grad_n2, residual, scale_mlp, gain_two)
    grad_residual, wide_sum.send = tie((grad_residual, wide_sum.send))
    wide_sum.move(0)
    grad_low = grad_residual.astype(bf16)
    d_out = lax.dot_general(grad_low, out_theirs, NT, preferred_element_type=f32).astype(bf16)
    d_got = swap(d_out)
    d_mine = lax.dot_general(grad_low, out_mine, NT, preferred_element_type=f32).astype(bf16)
    down_sum = Halving([(gd_mine, swap(gd_theirs), ORDERS[1])])
    down_sum.prepare(0)
    d_mine, d_got, down_sum.send = tie((d_mine, d_got, down_sum.send))
    down_sum.move(0)
    back = lambda b, before: attend_back(
        b, before, me_arr, mine, got, mixed, mixed_out, d_mine, d_got, lse, cosine, sine, piece
    )
    lins = back(0, ())

    lins, grad_low, wide_sum.got = tie((lins, grad_low, wide_sum.got))
    low = widen(grad_low[:, : D // 2]), widen(grad_low[:, D // 2 :])

    def grad_out(columns):
        a, b = [
            lax.dot_general(u, columns, TN, preferred_element_type=f32).astype(bf16)[: QD // 2]
            for u in (mixed, mixed_got)
        ]
        return pick(jnp.concatenate([a, b], 0), jnp.concatenate([b, a], 0))

    wide_sum.prepare(1)
    out_sum = Halving([(grad_out(pick(*low)), swap(grad_out(pick(*low[::-1]))), ORDERS[0])])
    out_sum.prepare(0)
    lins, wide_sum.send, out_sum.send = tie((lins, wide_sum.send, out_sum.send))
    wide_sum.move(1)
    out_sum.move(0)
    for b in range(1, batch):
        lins = back(b, lins)
    (lin_mine, lin_out), wide_sum.got, down_sum.got, out_sum.got = tie(
        (lins, wide_sum.got, down_sum.got, out_sum.got)
    )
    lin_got = swap(lin_out)
    down_sum.advance(1)
    out_sum.advance(1)
    wide_sum.advance(2)
    grad_n1 = lax.dot_general(lin_mine, w_mine, NT, preferred_element_type=f32) + lax.dot_general(
        lin_got, w_theirs, NT, preferred_element_type=f32
    )
    sum_gain_attn = jnp.sum(grad_n1 * floats * scale_attn, 0)
    column = lax.broadcasted_iota(jnp.int32, (1, WIDE), 1)
    sums = jnp.where(column == QKV, sum_gain_attn[:, None], 0.0) + jnp.where(
        column == QKV + 1, sum_gain_mlp[:, None], 0.0
    )
    weight_grad = lambda lin: (
        lax.dot_general(n1, lin, TN, preferred_element_type=f32) + sums
    ).astype(bf16)
    half = WIDE // 2
    grad_mine, grad_theirs = weight_grad(lin_mine), weight_grad(lin_got)
    grad_got = swap(grad_theirs)
    pack_sum = Halving(
        [
            (grad_mine[:, :half], grad_got[:, :half], ORDERS[0]),
            (grad_mine[:, half:], grad_got[:, half:], ORDERS[1]),
        ]
    )
    pack_sum.prepare(0)
    pack_sum.send, down_sum.got, out_sum.got = tie((pack_sum.send, down_sum.got, out_sum.got))
    pack_sum.move(0)
    down_sum.advance(2)
    out_sum.advance(2)
    grad_input = (grad_residual + norm_back(grad_n1, floats, scale_attn, gain_one)).astype(bf16)
    pack_sum.got, wide_sum.got = tie((pack_sum.got, wide_sum.got))
    pack_sum.advance(1)
    r_gate, r_up = wide_sum.finish(3)
    r_down = down_sum.finish(3)[0][:, : D // 2]
    r_out = out_sum.finish(3)[0][:, : D // 2]
    r_pack = jnp.concatenate(pack_sum.finish(2), 1)
    a, b, c = HQ * HEAD_SIZE, (HQ + HK) * HEAD_SIZE, QKV
    shape = layer_input.shape
    return (
        layer_out.reshape(shape),
        grad_input.reshape(shape),
        r_pack[:, :a],
        r_pack[:, a:b],
        r_pack[:, b:c],
        r_out,
        r_pack[:, c],
        r_gate,
        r_up,
        r_down,
        r_pack[:, c + 1],
    )


def solution(mesh):
    tokens, matrix, vector = P(None, "dp", "seq", None), P("dp", "seq"), P("dp")
    placed = (tokens, *[matrix] * 4, vector, *[matrix] * 3, vector, tokens)
    return jax.shard_map(
        local,
        mesh=mesh,
        in_specs=placed,
        out_specs=(tokens, tokens, *[matrix] * 4, vector, *[matrix] * 3, vector),
        check_vma=False,
    )
```

```python
import functools

import jax
import jax.numpy as jnp
from jax import lax
from jax.experimental import pallas as pl
from jax.experimental.pallas import tpu as pltpu
from jax.sharding import PartitionSpec as P

D = 1152
QUERY_HEADS = 18
KEY_VALUE_HEADS = 6
HEAD_SIZE = 64
FF = 3072
BLOCK = 256
QD = 1152
KVD = 384
HQ, HK = QUERY_HEADS // 2, KEY_VALUE_HEADS // 2
HALL = HQ + 2 * HK
QKV = HALL * HEAD_SIZE
FT = 256
HALF = 640
WIDE = 1024

epsilon = 1e-05
bf16, f32 = jnp.bfloat16, jnp.float32
NT = (((1,), (1,)), ((), ()))
NN = (((1,), (0,)), ((), ()))
TN = (((0,), (0,)), ((), ()))
VMEM_BYTES = 62 << 20


def dg(a, b, dims):
    return lax.dot_general(a, b, dims, preferred_element_type=f32)


def assemble(w):
    if w.shape[0] == 1:
        return w[0, 0]
    return jnp.concatenate([w[i, 0].astype(f32) for i in range(w.shape[0])], 0).astype(bf16)


def turned(u, cosine, sine):
    lane = lax.broadcasted_iota(jnp.int32, u.shape, 1)
    h = HEAD_SIZE // 2
    other = jnp.where(lane % HEAD_SIZE < h, pltpu.roll(u, 128 - h, 1), pltpu.roll(u, h, 1))
    return u * cosine + other * sine


def project_body(me, n1, w, cosine, sine, out, flat):
    @pl.when(pl.program_id(0) == 0)
    def _():
        flat[...] = assemble(w)

    u = dg(n1[...], flat[...], NN)
    turns = (HQ + HK) * HEAD_SIZE
    for c in range(0, turns, 128):
        out[:, c : c + 128] = turned(u[:, c : c + 128], cosine[...], sine[...]).astype(bf16)
    out[:, turns:] = u[:, turns:].astype(bf16)


def project(half, me, n1, w, cosine, sine, piece):
    n, _, rows, _ = w.shape
    width = WIDE
    batch = n1.shape[0] // piece
    return pl.pallas_call(
        project_body,
        grid_spec=pltpu.PrefetchScalarGridSpec(
            num_scalar_prefetch=1,
            grid=(batch,),
            in_specs=[
                pl.BlockSpec((piece, D), lambda b, m: (b, 0)),
                pl.BlockSpec((n, 1, rows, width), lambda b, m: (0, m[0] ^ half, 0, 0)),
                pl.BlockSpec((piece, 128), lambda b, m: (m[0], 0)),
                pl.BlockSpec((piece, 128), lambda b, m: (m[0], 0)),
            ],
            out_specs=[
                pl.BlockSpec((piece, width), lambda b, m: (b, 0)),
                pl.BlockSpec((D, width), lambda b, m: (0, 0)),
            ],
        ),
        out_shape=[
            jax.ShapeDtypeStruct((n1.shape[0], width), bf16),
            jax.ShapeDtypeStruct((D, width), bf16),
        ],
        compiler_params=pltpu.CompilerParams(vmem_limit_bytes=VMEM_BYTES),
        cost_estimate=pl.CostEstimate(flops=3 * 10**9, bytes_accessed=12 * 10**6, transcendentals=0),
        name="project",
    )(me, n1, w, cosine, sine)


def head_cols(j):
    return slice(j * HEAD_SIZE, (j + 1) * HEAD_SIZE)


def lane_of(j, shape):
    return lax.broadcasted_iota(jnp.int32, shape, 1) == j


def place(me, mine, got, q, k, v):
    piece = mine.shape[0]
    at = [pl.ds(pl.multiple_of((me[0] ^ a) * piece, piece), piece) for a in range(2)]
    for src, rows in zip((mine, got), at):
        for j in range(HQ):
            q[j, rows, :] = src[:, head_cols(j)] * jnp.asarray(0.125, bf16)
        for j in range(HK):
            k[j, rows, :] = src[:, head_cols(HQ + j)]
            v[j, rows, :] = src[:, head_cols(HQ + HK + j)]
    return at


def fwd_body(me, mine, got, o_mine, o_theirs, lse, q, k, v, o):
    at = place(me, mine, got, q, k, v)
    lse[...] = jnp.zeros_like(lse)

    def head(j, _):
        g = j // (HQ // HK)
        for i in range(lse.shape[0] // BLOCK):
            r = pl.ds(i * BLOCK, BLOCK)
            kw = (i + 1) * BLOCK
            s = dg(q[j, r, :], k[g, :kw, :], NT)
            m = jnp.max(s, axis=1, keepdims=True)
            p = jnp.exp(s - m)
            l = jnp.sum(p, axis=1, keepdims=True)
            mix = dg(p.astype(bf16), v[g, :kw, :], NN)
            o[j, r, :] = (mix / l).astype(bf16)
            lse[r, :] = jnp.where(lane_of(j, (BLOCK, 128)), m + jnp.log(l), lse[r, :])
        return 0

    lax.fori_loop(0, HQ, head, 0)
    for dst, rows in zip((o_mine, o_theirs), at):
        for j in range(HQ):
            dst[:, head_cols(j)] = o[j, rows, :]
        dst[:, HQ * HEAD_SIZE :] = jnp.zeros_like(dst[:, HQ * HEAD_SIZE :])


def bwd_body(
    me, mine, got, o_mine, o_theirs, do_mine, do_got, lse, cosine, sine, *rest
):
    lin_mine, lin_theirs, q, k, v, do, d, dka, dva, inner = rest[-10:]
    at = place(me, mine, got, q, k, v)
    inner[...] = jnp.zeros_like(inner)
    for dsrc, osrc, rows in zip((do_mine, do_got), (o_mine, o_theirs), at):
        for j in range(HQ):
            dj = dsrc[:, head_cols(j)]
            do[j, rows, :] = dj
            part = jnp.sum(dj.astype(f32) * osrc[:, head_cols(j)].astype(f32), axis=1, keepdims=True)
            inner[rows, :] = jnp.where(lane_of(j, (dj.shape[0], 128)), part, inner[rows, :])

    per = HQ // HK

    def head(j, _):
        g = j // per

        @pl.when(j % per == 0)
        def _():
            dka[...] = jnp.zeros_like(dka)
            dva[...] = jnp.zeros_like(dva)

        for i in range(lse.shape[0] // BLOCK):
            r = pl.ds(i * BLOCK, BLOCK)
            kw = (i + 1) * BLOCK
            mark = lane_of(j, (BLOCK, 128))
            column = lambda a: jnp.sum(jnp.where(mark, a[r, :], 0.0), axis=1, keepdims=True)
            qs = q[j, r, :]
            dO = do[j, r, :]
            kk = k[g, :kw, :]
            p = jnp.exp(dg(qs, kk, NT) - column(lse))
            dp = dg(dO, v[g, :kw, :], NT)
            ds = (p * (dp - column(inner))).astype(bf16)
            d[j, r, :] = dg(ds, kk, NN) * 0.125
            dka[:, :kw] += dg(qs.T, ds, NN)
            dva[:, :kw] += dg(dO.T, p.astype(bf16), NN)

        @pl.when(j % per == per - 1)
        def _():
            d[HQ + g] = dka[...].T
            d[HQ + HK + g] = dva[...].T

        return 0

    lax.fori_loop(0, HQ, head, 0)
    turns = HQ + HK
    for dst, rows in zip((lin_mine, lin_theirs), at):
        for j in range(0, HALL + 1, 2):
            a = d[j, rows, :]
            b = d[j + 1, rows, :] if j + 1 < HALL else jnp.zeros_like(a)
            u = jnp.concatenate([a, b], 1)
            if j < turns:
                u = turned(u, cosine[rows, :], -sine[rows, :])
            dst[:, j * HEAD_SIZE : (j + 2) * HEAD_SIZE] = u.astype(bf16)


def attend(me, mine, got, piece):
    tokens, width = mine.shape
    batch = tokens // piece
    row = lambda a, c: pl.BlockSpec((a, c), lambda b, m: (b, 0))
    cols = HALF
    heads = lambda n: pltpu.VMEM((n, 2 * piece, HEAD_SIZE), bf16)
    return pl.pallas_call(
        fwd_body,
        grid_spec=pltpu.PrefetchScalarGridSpec(
            num_scalar_prefetch=1,
            grid=(batch,),
            in_specs=[row(piece, width)] * 2,
            out_specs=[row(piece, cols), row(piece, cols), row(2 * piece, 128)],
            scratch_shapes=[heads(HQ), heads(HK), heads(HK), heads(HQ)],
        ),
        out_shape=[
            jax.ShapeDtypeStruct((tokens, cols), bf16),
            jax.ShapeDtypeStruct((tokens, cols), bf16),
            jax.ShapeDtypeStruct((2 * tokens, 128), f32),
        ],
        compiler_params=pltpu.CompilerParams(vmem_limit_bytes=VMEM_BYTES),
        cost_estimate=pl.CostEstimate(flops=24 * 10**9, bytes_accessed=20 * 10**6, transcendentals=12 * 10**6),
        name="attend",
    )(me, mine, got)


def attend_back(b, before, me, mine, got, o_mine, o_theirs, do_mine, do_got, lse, cosine, sine, piece):
    tokens, width = mine.shape
    row = lambda a, c: pl.BlockSpec((a, c), lambda _, m: (b, 0))
    cols = HALF
    table = pl.BlockSpec((2 * piece, 128), lambda _, m: (0, 0))
    heads = lambda n, t: pltpu.VMEM((n, 2 * piece, HEAD_SIZE), t)
    return pl.pallas_call(
        bwd_body,
        grid_spec=pltpu.PrefetchScalarGridSpec(
            num_scalar_prefetch=1,
            grid=(1,),
            in_specs=[row(piece, width)] * 2
            + [row(piece, cols)] * 4
            + [row(2 * piece, 128), table, table]
            + [pl.BlockSpec(memory_space=pl.ANY)] * len(before),
            out_specs=[row(piece, width)] * 2,
            scratch_shapes=[heads(HQ, bf16), heads(HK, bf16), heads(HK, bf16), heads(HQ, bf16)]
            + [heads(HALL, f32)]
            + [pltpu.VMEM((HEAD_SIZE, 2 * piece), f32)] * 2
            + [pltpu.VMEM((2 * piece, 128), f32)],
        ),
        out_shape=[jax.ShapeDtypeStruct((tokens, width), bf16)] * 2,
        input_output_aliases={10 + i: i for i in range(len(before))},
        compiler_params=pltpu.CompilerParams(vmem_limit_bytes=VMEM_BYTES),
        cost_estimate=pl.CostEstimate(flops=13 * 10**9, bytes_accessed=20 * 10**6, transcendentals=6 * 10**6),
        name="attend_back",
    )(me, mine, got, o_mine, o_theirs, do_mine, do_got, lse, cosine, sine, *before)


def mlp_body(me, n2, n2t, cot, res, wg, wu, wd_mine, wd_theirs, out, gn, gg_mine, gu_mine, gg_theirs, gu_theirs, gd_mine, gd_theirs, y):
    t = pl.program_id(0)
    per = pl.num_programs(0) // 2

    @pl.when(t == 0)
    def _():
        y[...] = res[...]
        gn[...] = jnp.zeros_like(gn)

    half = D // 2
    first = me[0] == 0

    da, db = wd_mine[:, :half], wd_theirs[:, :half]
    wd = jnp.concatenate([jnp.where(first, da, db), jnp.where(first, db, da)], axis=1)
    wgt, wut = assemble(wg), assemble(wu)
    gate = dg(n2[...], wgt, NN)
    up = dg(n2[...], wut, NN)
    gh = dg(cot[...], wd, NT)
    sig = jax.nn.sigmoid(gate)
    act = gate * sig
    hidden = (act * up).astype(bf16)
    ggv = (gh * up * sig * (1.0 + gate * (1.0 - sig))).astype(bf16)
    guv = (gh * act).astype(bf16)
    y[...] += dg(hidden, wd, NN)
    gdt = dg(hidden, cot[...], TN)
    for dst, u in (
        (gd_mine, jnp.where(first, gdt[:, :half], gdt[:, half:])),
        (gd_theirs, jnp.where(first, gdt[:, half:], gdt[:, :half])),
    ):
        dst[:, :half] = u.astype(bf16)
        dst[:, half:] = jnp.zeros((FT, HALF - half), bf16)
    gg = dg(n2t[...], ggv, NN).astype(bf16)
    gu = dg(n2t[...], guv, NN).astype(bf16)

    @pl.when(t < per)
    def _():
        gg_theirs[...] = gg
        gu_theirs[...] = gu

    @pl.when(t >= per)
    def _():
        gg_mine[...] = gg
        gu_mine[...] = gu

    gn[...] += dg(ggv, wgt, NT) + dg(guv, wut, NT)

    @pl.when(t == pl.num_programs(0) - 1)
    def _():
        out[...] = y[...].astype(bf16)


def mlp(me, n2, n2t, cot, res, wide, wd_mine, wd_theirs):
    tokens = n2.shape[0]
    n, _, rows, _ = wide.shape
    cols = FF // 2
    per = cols // FT
    half = lambda t, m: 1 - m[0] ^ t // per
    whole = lambda a: pl.BlockSpec(a.shape, lambda t, m: (0, 0), pipeline_mode=pl.Buffered(1))
    col = lambda first: pl.BlockSpec(
        (n, 1, rows, FT), lambda t, m: (0, half(t, m), 0, first + t % per)
    )
    part = pl.BlockSpec((FT, HALF), lambda t, m: (half(t, m) * per + t % per, 0))
    one = lambda: pl.BlockSpec((tokens, D), lambda t, m: (0, 0), pipeline_mode=pl.Buffered(1))
    return pl.pallas_call(
        mlp_body,
        grid_spec=pltpu.PrefetchScalarGridSpec(
            num_scalar_prefetch=1,
            grid=(FF // FT,),
            in_specs=[whole(n2), whole(n2t), whole(cot), whole(res), col(0), col(per), part, part],
            out_specs=[
                one(),
                one(),
                *[pl.BlockSpec((D, FT), lambda t, m: (0, jnp.maximum(t - per, 0)))] * 2,
                *[pl.BlockSpec((D, FT), lambda t, m: (0, jnp.minimum(t, per - 1)))] * 2,
                part,
                part,
            ],
            scratch_shapes=[pltpu.VMEM((tokens, D), f32)],
        ),
        out_shape=[
            jax.ShapeDtypeStruct((tokens, D), bf16),
            jax.ShapeDtypeStruct((tokens, D), f32),
            *[jax.ShapeDtypeStruct((D, cols), bf16)] * 4,
            jax.ShapeDtypeStruct((FF, HALF), bf16),
            jax.ShapeDtypeStruct((FF, HALF), bf16),
        ],
        compiler_params=pltpu.CompilerParams(vmem_limit_bytes=VMEM_BYTES),
        cost_estimate=pl.CostEstimate(flops=65 * 10**9, bytes_accessed=60 * 10**6, transcendentals=3 * 10**6),
        name="mlp",
    )(me, n2, n2t, cot, res, wide, wide, wd_mine, wd_theirs)


def norm_back(grad_norm, rows_in, scale_rows, gain_rows):
    weighted = grad_norm * gain_rows
    cube_rows = scale_rows * scale_rows * scale_rows
    return scale_rows * weighted - rows_in * cube_rows * jnp.mean(
        weighted * rows_in, -1, keepdims=True
    )


def swap(a):
    return lax.ppermute(a, "seq", [(0, 1), (1, 0)])


BOTH = ("dp", "seq")


def whole_halves(g):
    return jnp.swapaxes(g, 0, 1).reshape(1, 2, -1, g.shape[3])


def fetch(w):
    g = lax.all_gather(w, BOTH, axis=0, tiled=True).reshape(lax.axis_size("dp"), 2, *w.shape)
    return g if w.shape[0] % 8 == 0 else whole_halves(g)


def exchange(a, bit):
    return lax.ppermute(a, "dp", [(i, i ^ (1 << bit)) for i in range(lax.axis_size("dp"))])


ORDERS = (0, 1), (1, 0)


def doubled(a, got, bit, axis):
    low = (lax.axis_index("dp") >> bit) & 1 == 0
    return jnp.where(low, jnp.stack([a, got], axis), jnp.stack([got, a], axis))


def gather_doubling(w):
    bits = lax.axis_size("dp").bit_length() - 1
    cut = w.shape[1] // 256 * 128
    out = []
    for part, order in ((w[:, :cut], ORDERS[0]), (w[:, cut:], ORDERS[1])):
        last, have = None, []
        for bit in list(range(bits))[:1:-1] + list(order[::-1]):
            a = part if last is None else doubled(*last)
            last = a, exchange(a, bit), bit, sum(b > bit for b in have)
            have.append(bit)
        out.append(last)
    return out


def gather_finish(lasts):
    out = [doubled(*last) for last in lasts]
    mine = jnp.concatenate([a.reshape(-1, a.shape[-1]) for a in out], 1)
    return mine, swap(mine)


def add(a, b):
    return a.astype(f32) + b.astype(f32)


class Halving:
    def __init__(self, parts, kind=bf16):
        self.kind = kind
        bits = lax.axis_size("dp").bit_length() - 1
        self.steps = bits
        self.orders = [[*order, *range(2, bits)] for _, _, order in parts]
        shape = lambda u: u.reshape(*[2] * bits, -1, u.shape[-1])
        self.stay = [shape(u) for u, _, _ in parts]
        self.got = [shape(v) for _, v, _ in parts]

    def prepare(self, step):
        self.send = []
        for p, order in enumerate(self.orders):
            bit = order[step]
            axis = sum(b > bit for b in order[step:])
            mybit = (lax.axis_index("dp") >> bit) & 1
            at = lambda u, i: lax.dynamic_index_in_dim(u, i, axis, keepdims=False)
            total = lambda i: add(at(self.stay[p], i), at(self.got[p], i)).astype(self.kind)
            self.send.append(total(1 - mybit))
            self.stay[p] = total(mybit)

    def move(self, step):
        self.got = [exchange(a, order[step]) for a, order in zip(self.send, self.orders)]

    def advance(self, step):
        self.prepare(step)
        self.move(step)

    def finish(self, step=0):
        for i in range(step, self.steps):
            self.advance(i)
        return [add(*u) for u in zip(self.stay, self.got)]


def local(
    layer_input,
    w_query,
    w_key,
    w_value,
    w_out,
    gain_attn,
    w_gate,
    w_up,
    w_down,
    gain_mlp,
    cotangent,
):
    batch, _, piece, _ = layer_input.shape
    tokens = batch * piece
    me = lax.axis_index("seq")
    me_arr = jnp.full((1,), me, jnp.int32)
    pick = lambda a, b: jnp.where(me == 0, a, b)
    tie = lax.optimization_barrier
    h = HEAD_SIZE // 2
    frequency = 10000.0 ** (-2.0 * jnp.arange(h).astype(f32) / HEAD_SIZE)
    angles = jnp.arange(2 * piece).astype(f32)[:, None] * jnp.tile(frequency, 128 // h)[None, :]
    cosine = jnp.cos(angles)
    sine = jnp.sin(angles) * jnp.where(jnp.arange(128) % HEAD_SIZE < h, -1.0, 1.0)[None, :]

    gains = jnp.pad(jnp.stack([gain_attn, gain_mlp], 1), ((0, 0), (0, WIDE - QKV - 2)))
    full = fetch(jnp.concatenate([w_query, w_key, w_value, gains, w_out], 1))
    wide = fetch(jnp.concatenate([w_gate, w_up], 1))
    widen = lambda a: jnp.pad(a, ((0, 0), (0, HALF - D // 2)))
    down_last = gather_doubling(widen(w_down))
    full, _ = tie((full, [last[0] for last in down_last]))
    gain_one = full[:, 0, :, QKV].reshape(D).astype(f32)
    gain_two = full[:, 0, :, QKV + 1].reshape(D).astype(f32)
    out_halves = whole_halves(full[..., WIDE:])[0].reshape(2, 2, D // 2, D // 2)
    out_rows = lambda c: jnp.concatenate(
        [lax.dynamic_index_in_dim(out_halves[i], c, 0, keepdims=False) for i in range(2)], 1
    )
    out_mine, out_theirs = [jnp.pad(out_rows(c), ((0, HALF - D // 2), (0, 0))) for c in (me, 1 - me)]

    floats = layer_input.reshape(tokens, D).astype(f32)
    cot = cotangent.reshape(tokens, D)
    scale_attn = lax.rsqrt(jnp.mean(floats * floats, -1, keepdims=True) + epsilon)
    n1 = (floats * scale_attn * gain_one).astype(bf16)
    dot = lambda a, b: lax.dot_general(a, b, NN, preferred_element_type=f32)

    heads_out, w_theirs = project(1, me_arr, n1, full, cosine, sine, piece)
    got = swap(heads_out)
    mine, w_mine = project(0, me_arr, n1, full, cosine, sine, piece)
    mixed, mixed_out, lse = attend(me_arr, mine, got, piece)
    mixed_out, arrived = tie((mixed_out, [last[1] for last in down_last]))
    down_mine, down_theirs = gather_finish(
        [(a, b, bit, axis) for (a, _, bit, axis), b in zip(down_last, arrived)]
    )
    mixed_got = swap(mixed_out)
    residual = floats + (dot(mixed, out_mine) + dot(mixed_got, out_theirs))
    scale_mlp = lax.rsqrt(jnp.mean(residual * residual, -1, keepdims=True) + epsilon)
    n2 = (residual * scale_mlp * gain_two).astype(bf16)
    layer_out, grad_n2, gg_mine, gu_mine, gg_theirs, gu_theirs, gd_mine, gd_theirs = mlp(
        me_arr, n2, n2.T, cot, residual, wide, down_mine, down_theirs
    )
    wide_sum = Halving([(gg_mine, swap(gg_theirs), ORDERS[0]), (gu_mine, swap(gu_theirs), ORDERS[1])])
    wide_sum.prepare(0)
    sum_gain_mlp = jnp.sum(grad_n2 * residual * scale_mlp, 0)
    grad_residual = cot.astype(f32) + norm_back(grad_n2, residual, scale_mlp, gain_two)
    grad_residual, wide_sum.send = tie((grad_residual, wide_sum.send))
    wide_sum.move(0)
    grad_low = grad_residual.astype(bf16)
    d_out = lax.dot_general(grad_low, out_theirs, NT, preferred_element_type=f32).astype(bf16)
    d_got = swap(d_out)
    d_mine = lax.dot_general(grad_low, out_mine, NT, preferred_element_type=f32).astype(bf16)
    down_sum = Halving([(gd_mine, swap(gd_theirs), ORDERS[1])])
    down_sum.prepare(0)
    d_mine, d_got, down_sum.send = tie((d_mine, d_got, down_sum.send))
    down_sum.move(0)
    back = lambda b, before: attend_back(
        b, before, me_arr, mine, got, mixed, mixed_out, d_mine, d_got, lse, cosine, sine, piece
    )
    lins = back(0, ())

    lins, grad_low, wide_sum.got = tie((lins, grad_low, wide_sum.got))
    low = widen(grad_low[:, : D // 2]), widen(grad_low[:, D // 2 :])

    def grad_out(columns):
        a, b = [
            lax.dot_general(u, columns, TN, preferred_element_type=f32).astype(bf16)[: QD // 2]
            for u in (mixed, mixed_got)
        ]
        return pick(jnp.concatenate([a, b], 0), jnp.concatenate([b, a], 0))

    wide_sum.prepare(1)
    out_sum = Halving([(grad_out(pick(*low)), swap(grad_out(pick(*low[::-1]))), ORDERS[0])])
    out_sum.prepare(0)
    lins, wide_sum.send, out_sum.send = tie((lins, wide_sum.send, out_sum.send))
    wide_sum.move(1)
    out_sum.move(0)
    for b in range(1, batch):
        lins = back(b, lins)
    (lin_mine, lin_out), wide_sum.got, down_sum.got, out_sum.got = tie(
        (lins, wide_sum.got, down_sum.got, out_sum.got)
    )
    lin_got = swap(lin_out)
    down_sum.advance(1)
    out_sum.advance(1)
    wide_sum.advance(2)
    grad_n1 = lax.dot_general(lin_mine, w_mine, NT, preferred_element_type=f32) + lax.dot_general(
        lin_got, w_theirs, NT, preferred_element_type=f32
    )
    sum_gain_attn = jnp.sum(grad_n1 * floats * scale_attn, 0)
    column = lax.broadcasted_iota(jnp.int32, (1, WIDE), 1)
    sums = jnp.where(column == QKV, sum_gain_attn[:, None], 0.0) + jnp.where(
        column == QKV + 1, sum_gain_mlp[:, None], 0.0
    )
    weight_grad = lambda lin: (
        lax.dot_general(n1, lin, TN, preferred_element_type=f32) + sums
    ).astype(bf16)
    half = WIDE // 2
    grad_mine, grad_theirs = weight_grad(lin_mine), weight_grad(lin_got)
    grad_got = swap(grad_theirs)
    pack_sum = Halving(
        [
            (grad_mine[:, :half], grad_got[:, :half], ORDERS[0]),
            (grad_mine[:, half:], grad_got[:, half:], ORDERS[1]),
        ]
    )
    pack_sum.prepare(0)
    _, down_sum.got, out_sum.got, wide_sum.got = tie(
        (pack_sum.send, down_sum.got, out_sum.got, wide_sum.got)
    )
    pack_sum.move(0)
    down_sum.advance(2)
    out_sum.advance(2)
    grad_input = (grad_residual + norm_back(grad_n1, floats, scale_attn, gain_one)).astype(bf16)
    pack_sum.advance(1)
    r_gate, r_up = wide_sum.finish(3)
    r_down = down_sum.finish(3)[0][:, : D // 2]
    r_out = out_sum.finish(3)[0][:, : D // 2]
    r_pack = jnp.concatenate(pack_sum.finish(2), 1)
    a, b, c = HQ * HEAD_SIZE, (HQ + HK) * HEAD_SIZE, QKV
    shape = layer_input.shape
    return (
        layer_out.reshape(shape),
        grad_input.reshape(shape),
        r_pack[:, :a],
        r_pack[:, a:b],
        r_pack[:, b:c],
        r_out,
        r_pack[:, c],
        r_gate,
        r_up,
        r_down,
        r_pack[:, c + 1],
    )


def solution(mesh):
    tokens, matrix, vector = P(None, "dp", "seq", None), P("dp", "seq"), P("dp")
    placed = (tokens, *[matrix] * 4, vector, *[matrix] * 3, vector, tokens)
    return jax.shard_map(
        local,
        mesh=mesh,
        in_specs=placed,
        out_specs=(tokens, tokens, *[matrix] * 4, vector, *[matrix] * 3, vector),
        check_vma=False,
    )
```

```python
import functools

import jax
import jax.numpy as jnp
from jax import lax
from jax.experimental import pallas as pl
from jax.experimental.pallas import tpu as pltpu
from jax.sharding import PartitionSpec as P

D = 1152
QUERY_HEADS = 18
KEY_VALUE_HEADS = 6
HEAD_SIZE = 64
FF = 3072
BLOCK = 256
QD = 1152
KVD = 384
HQ, HK = QUERY_HEADS // 2, KEY_VALUE_HEADS // 2
HALL = HQ + 2 * HK
QKV = HALL * HEAD_SIZE
FT = 256
HALF = 640
WIDE = 1024

epsilon = 1e-05
bf16, f32 = jnp.bfloat16, jnp.float32
NT = (((1,), (1,)), ((), ()))
NN = (((1,), (0,)), ((), ()))
TN = (((0,), (0,)), ((), ()))
VMEM_BYTES = 62 << 20


def dg(a, b, dims):
    return lax.dot_general(a, b, dims, preferred_element_type=f32)


def assemble(w):
    if w.shape[0] == 1:
        return w[0, 0]
    return jnp.concatenate([w[i, 0].astype(f32) for i in range(w.shape[0])], 0).astype(bf16)


def turned(u, cosine, sine):
    lane = lax.broadcasted_iota(jnp.int32, u.shape, 1)
    h = HEAD_SIZE // 2
    other = jnp.where(lane % HEAD_SIZE < h, pltpu.roll(u, 128 - h, 1), pltpu.roll(u, h, 1))
    return u * cosine + other * sine


def project_body(me, n1, w, cosine, sine, out, flat):
    @pl.when(pl.program_id(0) == 0)
    def _():
        flat[...] = assemble(w)

    u = dg(n1[...], flat[...], NN)
    turns = (HQ + HK) * HEAD_SIZE
    for c in range(0, turns, 128):
        out[:, c : c + 128] = turned(u[:, c : c + 128], cosine[...], sine[...]).astype(bf16)
    out[:, turns:] = u[:, turns:].astype(bf16)


def project(half, me, n1, w, cosine, sine, piece):
    n, _, rows, _ = w.shape
    width = WIDE
    batch = n1.shape[0] // piece
    return pl.pallas_call(
        project_body,
        grid_spec=pltpu.PrefetchScalarGridSpec(
            num_scalar_prefetch=1,
            grid=(batch,),
            in_specs=[
                pl.BlockSpec((piece, D), lambda b, m: (b, 0)),
                pl.BlockSpec((n, 1, rows, width), lambda b, m: (0, m[0] ^ half, 0, 0)),
                pl.BlockSpec((piece, 128), lambda b, m: (m[0], 0)),
                pl.BlockSpec((piece, 128), lambda b, m: (m[0], 0)),
            ],
            out_specs=[
                pl.BlockSpec((piece, width), lambda b, m: (b, 0)),
                pl.BlockSpec((D, width), lambda b, m: (0, 0)),
            ],
        ),
        out_shape=[
            jax.ShapeDtypeStruct((n1.shape[0], width), bf16),
            jax.ShapeDtypeStruct((D, width), bf16),
        ],
        compiler_params=pltpu.CompilerParams(vmem_limit_bytes=VMEM_BYTES),
        cost_estimate=pl.CostEstimate(flops=3 * 10**9, bytes_accessed=12 * 10**6, transcendentals=0),
        name="project",
    )(me, n1, w, cosine, sine)


def head_cols(j):
    return slice(j * HEAD_SIZE, (j + 1) * HEAD_SIZE)


def lane_of(j, shape):
    return lax.broadcasted_iota(jnp.int32, shape, 1) == j


def place(me, mine, got, q, k, v):
    piece = mine.shape[0]
    at = [pl.ds(pl.multiple_of((me[0] ^ a) * piece, piece), piece) for a in range(2)]
    for src, rows in zip((mine, got), at):
        for j in range(HQ):
            q[j, rows, :] = src[:, head_cols(j)] * jnp.asarray(0.125, bf16)
        for j in range(HK):
            k[j, rows, :] = src[:, head_cols(HQ + j)]
            v[j, rows, :] = src[:, head_cols(HQ + HK + j)]
    return at


def fwd_body(me, mine, got, o_mine, o_theirs, lse, q, k, v, o):
    at = place(me, mine, got, q, k, v)
    lse[...] = jnp.zeros_like(lse)

    def head(j, _):
        g = j // (HQ // HK)
        for i in range(lse.shape[0] // BLOCK):
            r = pl.ds(i * BLOCK, BLOCK)
            kw = (i + 1) * BLOCK
            s = dg(q[j, r, :], k[g, :kw, :], NT)
            m = jnp.max(s, axis=1, keepdims=True)
            p = jnp.exp(s - m)
            l = jnp.sum(p, axis=1, keepdims=True)
            mix = dg(p.astype(bf16), v[g, :kw, :], NN)
            o[j, r, :] = (mix / l).astype(bf16)
            lse[r, :] = jnp.where(lane_of(j, (BLOCK, 128)), m + jnp.log(l), lse[r, :])
        return 0

    lax.fori_loop(0, HQ, head, 0)
    for dst, rows in zip((o_mine, o_theirs), at):
        for j in range(HQ):
            dst[:, head_cols(j)] = o[j, rows, :]
        dst[:, HQ * HEAD_SIZE :] = jnp.zeros_like(dst[:, HQ * HEAD_SIZE :])


def bwd_body(
    me, mine, got, o_mine, o_theirs, do_mine, do_got, lse, cosine, sine, *rest
):
    lin_mine, lin_theirs, q, k, v, do, d, dka, dva, inner = rest[-10:]
    at = place(me, mine, got, q, k, v)
    inner[...] = jnp.zeros_like(inner)
    for dsrc, osrc, rows in zip((do_mine, do_got), (o_mine, o_theirs), at):
        for j in range(HQ):
            dj = dsrc[:, head_cols(j)]
            do[j, rows, :] = dj
            part = jnp.sum(dj.astype(f32) * osrc[:, head_cols(j)].astype(f32), axis=1, keepdims=True)
            inner[rows, :] = jnp.where(lane_of(j, (dj.shape[0], 128)), part, inner[rows, :])

    per = HQ // HK

    def head(j, _):
        g = j // per

        @pl.when(j % per == 0)
        def _():
            dka[...] = jnp.zeros_like(dka)
            dva[...] = jnp.zeros_like(dva)

        for i in range(lse.shape[0] // BLOCK):
            r = pl.ds(i * BLOCK, BLOCK)
            kw = (i + 1) * BLOCK
            mark = lane_of(j, (BLOCK, 128))
            column = lambda a: jnp.sum(jnp.where(mark, a[r, :], 0.0), axis=1, keepdims=True)
            qs = q[j, r, :]
            dO = do[j, r, :]
            kk = k[g, :kw, :]
            p = jnp.exp(dg(qs, kk, NT) - column(lse))
            dp = dg(dO, v[g, :kw, :], NT)
            ds = (p * (dp - column(inner))).astype(bf16)
            d[j, r, :] = dg(ds, kk, NN) * 0.125
            dka[:, :kw] += dg(qs.T, ds, NN)
            dva[:, :kw] += dg(dO.T, p.astype(bf16), NN)

        @pl.when(j % per == per - 1)
        def _():
            d[HQ + g] = dka[...].T
            d[HQ + HK + g] = dva[...].T

        return 0

    lax.fori_loop(0, HQ, head, 0)
    turns = HQ + HK
    for dst, rows in zip((lin_mine, lin_theirs), at):
        for j in range(0, HALL + 1, 2):
            a = d[j, rows, :]
            b = d[j + 1, rows, :] if j + 1 < HALL else jnp.zeros_like(a)
            u = jnp.concatenate([a, b], 1)
            if j < turns:
                u = turned(u, cosine[rows, :], -sine[rows, :])
            dst[:, j * HEAD_SIZE : (j + 2) * HEAD_SIZE] = u.astype(bf16)


def attend(me, mine, got, piece):
    tokens, width = mine.shape
    batch = tokens // piece
    row = lambda a, c: pl.BlockSpec((a, c), lambda b, m: (b, 0))
    cols = HALF
    heads = lambda n: pltpu.VMEM((n, 2 * piece, HEAD_SIZE), bf16)
    return pl.pallas_call(
        fwd_body,
        grid_spec=pltpu.PrefetchScalarGridSpec(
            num_scalar_prefetch=1,
            grid=(batch,),
            in_specs=[row(piece, width)] * 2,
            out_specs=[row(piece, cols), row(piece, cols), row(2 * piece, 128)],
            scratch_shapes=[heads(HQ), heads(HK), heads(HK), heads(HQ)],
        ),
        out_shape=[
            jax.ShapeDtypeStruct((tokens, cols), bf16),
            jax.ShapeDtypeStruct((tokens, cols), bf16),
            jax.ShapeDtypeStruct((2 * tokens, 128), f32),
        ],
        compiler_params=pltpu.CompilerParams(vmem_limit_bytes=VMEM_BYTES),
        cost_estimate=pl.CostEstimate(flops=24 * 10**9, bytes_accessed=20 * 10**6, transcendentals=12 * 10**6),
        name="attend",
    )(me, mine, got)


def attend_back(b, before, me, mine, got, o_mine, o_theirs, do_mine, do_got, lse, cosine, sine, piece):
    tokens, width = mine.shape
    row = lambda a, c: pl.BlockSpec((a, c), lambda _, m: (b, 0))
    cols = HALF
    table = pl.BlockSpec((2 * piece, 128), lambda _, m: (0, 0))
    heads = lambda n, t: pltpu.VMEM((n, 2 * piece, HEAD_SIZE), t)
    return pl.pallas_call(
        bwd_body,
        grid_spec=pltpu.PrefetchScalarGridSpec(
            num_scalar_prefetch=1,
            grid=(1,),
            in_specs=[row(piece, width)] * 2
            + [row(piece, cols)] * 4
            + [row(2 * piece, 128), table, table]
            + [pl.BlockSpec(memory_space=pl.ANY)] * len(before),
            out_specs=[row(piece, width)] * 2,
            scratch_shapes=[heads(HQ, bf16), heads(HK, bf16), heads(HK, bf16), heads(HQ, bf16)]
            + [heads(HALL, f32)]
            + [pltpu.VMEM((HEAD_SIZE, 2 * piece), f32)] * 2
            + [pltpu.VMEM((2 * piece, 128), f32)],
        ),
        out_shape=[jax.ShapeDtypeStruct((tokens, width), bf16)] * 2,
        input_output_aliases={10 + i: i for i in range(len(before))},
        compiler_params=pltpu.CompilerParams(vmem_limit_bytes=VMEM_BYTES),
        cost_estimate=pl.CostEstimate(flops=13 * 10**9, bytes_accessed=20 * 10**6, transcendentals=6 * 10**6),
        name="attend_back",
    )(me, mine, got, o_mine, o_theirs, do_mine, do_got, lse, cosine, sine, *before)


def mlp_body(me, n2, n2t, cot, res, wg, wu, wd_mine, wd_theirs, out, gn, gg_mine, gu_mine, gg_theirs, gu_theirs, gd_mine, gd_theirs, y):
    t = pl.program_id(0)
    per = pl.num_programs(0) // 2

    @pl.when(t == 0)
    def _():
        y[...] = res[...]
        gn[...] = jnp.zeros_like(gn)

    half = D // 2
    first = me[0] == 0

    da, db = wd_mine[:, :half], wd_theirs[:, :half]
    wd = jnp.concatenate([jnp.where(first, da, db), jnp.where(first, db, da)], axis=1)
    wgt, wut = assemble(wg), assemble(wu)
    gate = dg(n2[...], wgt, NN)
    up = dg(n2[...], wut, NN)
    gh = dg(cot[...], wd, NT)
    sig = jax.nn.sigmoid(gate)
    act = gate * sig
    hidden = (act * up).astype(bf16)
    ggv = (gh * up * sig * (1.0 + gate * (1.0 - sig))).astype(bf16)
    guv = (gh * act).astype(bf16)
    y[...] += dg(hidden, wd, NN)
    gdt = dg(hidden, cot[...], TN)
    for dst, u in (
        (gd_mine, jnp.where(first, gdt[:, :half], gdt[:, half:])),
        (gd_theirs, jnp.where(first, gdt[:, half:], gdt[:, :half])),
    ):
        dst[:, :half] = u.astype(bf16)
        dst[:, half:] = jnp.zeros((FT, HALF - half), bf16)
    gg = dg(n2t[...], ggv, NN).astype(bf16)
    gu = dg(n2t[...], guv, NN).astype(bf16)

    @pl.when(t < per)
    def _():
        gg_theirs[...] = gg
        gu_theirs[...] = gu

    @pl.when(t >= per)
    def _():
        gg_mine[...] = gg
        gu_mine[...] = gu

    gn[...] += dg(ggv, wgt, NT) + dg(guv, wut, NT)

    @pl.when(t == pl.num_programs(0) - 1)
    def _():
        out[...] = y[...].astype(bf16)


def mlp(me, n2, n2t, cot, res, wide, wd_mine, wd_theirs):
    tokens = n2.shape[0]
    n, _, rows, _ = wide.shape
    cols = FF // 2
    per = cols // FT
    half = lambda t, m: 1 - m[0] ^ t // per
    whole = lambda a: pl.BlockSpec(a.shape, lambda t, m: (0, 0), pipeline_mode=pl.Buffered(1))
    col = lambda first: pl.BlockSpec(
        (n, 1, rows, FT), lambda t, m: (0, half(t, m), 0, first + t % per)
    )
    part = pl.BlockSpec((FT, HALF), lambda t, m: (half(t, m) * per + t % per, 0))
    one = lambda: pl.BlockSpec((tokens, D), lambda t, m: (0, 0), pipeline_mode=pl.Buffered(1))
    return pl.pallas_call(
        mlp_body,
        grid_spec=pltpu.PrefetchScalarGridSpec(
            num_scalar_prefetch=1,
            grid=(FF // FT,),
            in_specs=[whole(n2), whole(n2t), whole(cot), whole(res), col(0), col(per), part, part],
            out_specs=[
                one(),
                one(),
                *[pl.BlockSpec((D, FT), lambda t, m: (0, jnp.maximum(t - per, 0)))] * 2,
                *[pl.BlockSpec((D, FT), lambda t, m: (0, jnp.minimum(t, per - 1)))] * 2,
                part,
                part,
            ],
            scratch_shapes=[pltpu.VMEM((tokens, D), f32)],
        ),
        out_shape=[
            jax.ShapeDtypeStruct((tokens, D), bf16),
            jax.ShapeDtypeStruct((tokens, D), f32),
            *[jax.ShapeDtypeStruct((D, cols), bf16)] * 4,
            jax.ShapeDtypeStruct((FF, HALF), bf16),
            jax.ShapeDtypeStruct((FF, HALF), bf16),
        ],
        compiler_params=pltpu.CompilerParams(vmem_limit_bytes=VMEM_BYTES),
        cost_estimate=pl.CostEstimate(flops=65 * 10**9, bytes_accessed=60 * 10**6, transcendentals=3 * 10**6),
        name="mlp",
    )(me, n2, n2t, cot, res, wide, wide, wd_mine, wd_theirs)


def norm_back(grad_norm, rows_in, scale_rows, gain_rows):
    weighted = grad_norm * gain_rows
    cube_rows = scale_rows * scale_rows * scale_rows
    return scale_rows * weighted - rows_in * cube_rows * jnp.mean(
        weighted * rows_in, -1, keepdims=True
    )


def swap(a):
    return lax.ppermute(a, "seq", [(0, 1), (1, 0)])


BOTH = ("dp", "seq")


def whole_halves(g):
    return jnp.swapaxes(g, 0, 1).reshape(1, 2, -1, g.shape[3])


def fetch(w):
    g = lax.all_gather(w, BOTH, axis=0, tiled=True).reshape(lax.axis_size("dp"), 2, *w.shape)
    return g if w.shape[0] % 8 == 0 else whole_halves(g)


def exchange(a, bit):
    return lax.ppermute(a, "dp", [(i, i ^ (1 << bit)) for i in range(lax.axis_size("dp"))])


ORDERS = (0, 1), (1, 0)
HIGH, LAST = (), (0, 1)


def doubled(a, got, bit, axis):
    low = (lax.axis_index("dp") >> bit) & 1 == 0
    return jnp.where(low, jnp.stack([a, got], axis), jnp.stack([got, a], axis))


def gather_doubling(w):
    bits = lax.axis_size("dp").bit_length() - 1
    cut = w.shape[1] // 256 * 128
    out = []
    for part, order in ((w[:, :cut], ORDERS[0]), (w[:, cut:], ORDERS[1])):
        last, have = None, []
        for bit in list(range(bits))[:1:-1] + list(order[::-1]):
            a = part if last is None else doubled(*last)
            last = a, exchange(a, bit), bit, sum(b > bit for b in have)
            have.append(bit)
        out.append(last)
    return out


def gather_finish(lasts):
    out = [doubled(*last) for last in lasts]
    mine = jnp.concatenate([a.reshape(-1, a.shape[-1]) for a in out], 1)
    return mine, swap(mine)


def add(a, b):
    return a.astype(f32) + b.astype(f32)


class Halving:
    def __init__(self, parts, kind=bf16):
        self.kind = kind
        bits = lax.axis_size("dp").bit_length() - 1
        self.steps = bits
        rest = list(range(2, bits))
        ways = {ORDERS[0]: [*ORDERS[0], *rest], ORDERS[1]: [*ORDERS[1], *rest[::-1]], HIGH: [*rest, *LAST]}
        self.orders = [ways[order] for _, _, order in parts]
        shape = lambda u: u.reshape(*[2] * bits, -1, u.shape[-1])
        self.stay = [shape(u) for u, _, _ in parts]
        self.got = [shape(v) for _, v, _ in parts]

    def prepare(self, step):
        self.send = []
        for p, order in enumerate(self.orders):
            bit = order[step]
            axis = sum(b > bit for b in order[step:])
            mybit = (lax.axis_index("dp") >> bit) & 1
            at = lambda u, i: lax.dynamic_index_in_dim(u, i, axis, keepdims=False)
            total = lambda i: add(at(self.stay[p], i), at(self.got[p], i)).astype(self.kind)
            self.send.append(total(1 - mybit))
            self.stay[p] = total(mybit)

    def move(self, step):
        self.got = [exchange(a, order[step]) for a, order in zip(self.send, self.orders)]

    def advance(self, step):
        self.prepare(step)
        self.move(step)

    def finish(self, step=0):
        for i in range(step, self.steps):
            self.advance(i)
        return [add(*u) for u in zip(self.stay, self.got)]


def local(
    layer_input,
    w_query,
    w_key,
    w_value,
    w_out,
    gain_attn,
    w_gate,
    w_up,
    w_down,
    gain_mlp,
    cotangent,
):
    batch, _, piece, _ = layer_input.shape
    tokens = batch * piece
    me = lax.axis_index("seq")
    me_arr = jnp.full((1,), me, jnp.int32)
    pick = lambda a, b: jnp.where(me == 0, a, b)
    tie = lax.optimization_barrier
    h = HEAD_SIZE // 2
    frequency = 10000.0 ** (-2.0 * jnp.arange(h).astype(f32) / HEAD_SIZE)
    angles = jnp.arange(2 * piece).astype(f32)[:, None] * jnp.tile(frequency, 128 // h)[None, :]
    cosine = jnp.cos(angles)
    sine = jnp.sin(angles) * jnp.where(jnp.arange(128) % HEAD_SIZE < h, -1.0, 1.0)[None, :]

    gains = jnp.pad(jnp.stack([gain_attn, gain_mlp], 1), ((0, 0), (0, WIDE - QKV - 2)))
    full = fetch(jnp.concatenate([w_query, w_key, w_value, gains, w_out], 1))
    wide = fetch(jnp.concatenate([w_gate, w_up], 1))
    widen = lambda a: jnp.pad(a, ((0, 0), (0, HALF - D // 2)))
    down_last = gather_doubling(widen(w_down))
    full, _ = tie((full, [last[0] for last in down_last]))
    gain_one = full[:, 0, :, QKV].reshape(D).astype(f32)
    gain_two = full[:, 0, :, QKV + 1].reshape(D).astype(f32)
    out_halves = whole_halves(full[..., WIDE:])[0].reshape(2, 2, D // 2, D // 2)
    out_rows = lambda c: jnp.concatenate(
        [lax.dynamic_index_in_dim(out_halves[i], c, 0, keepdims=False) for i in range(2)], 1
    )
    out_mine, out_theirs = [jnp.pad(out_rows(c), ((0, HALF - D // 2), (0, 0))) for c in (me, 1 - me)]

    floats = layer_input.reshape(tokens, D).astype(f32)
    cot = cotangent.reshape(tokens, D)
    scale_attn = lax.rsqrt(jnp.mean(floats * floats, -1, keepdims=True) + epsilon)
    n1 = (floats * scale_attn * gain_one).astype(bf16)
    dot = lambda a, b: lax.dot_general(a, b, NN, preferred_element_type=f32)

    heads_out, w_theirs = project(1, me_arr, n1, full, cosine, sine, piece)
    got = swap(heads_out)
    mine, w_mine = project(0, me_arr, n1, full, cosine, sine, piece)
    mixed, mixed_out, lse = attend(me_arr, mine, got, piece)
    mixed_out, arrived = tie((mixed_out, [last[1] for last in down_last]))
    down_mine, down_theirs = gather_finish(
        [(a, b, bit, axis) for (a, _, bit, axis), b in zip(down_last, arrived)]
    )
    mixed_got = swap(mixed_out)
    residual = floats + (dot(mixed, out_mine) + dot(mixed_got, out_theirs))
    scale_mlp = lax.rsqrt(jnp.mean(residual * residual, -1, keepdims=True) + epsilon)
    n2 = (residual * scale_mlp * gain_two).astype(bf16)
    layer_out, grad_n2, gg_mine, gu_mine, gg_theirs, gu_theirs, gd_mine, gd_theirs = mlp(
        me_arr, n2, n2.T, cot, residual, wide, down_mine, down_theirs
    )
    wide_sum = Halving([(gg_mine, swap(gg_theirs), ORDERS[0]), (gu_mine, swap(gu_theirs), ORDERS[1])])
    wide_sum.prepare(0)
    sum_gain_mlp = jnp.sum(grad_n2 * residual * scale_mlp, 0)
    grad_residual = cot.astype(f32) + norm_back(grad_n2, residual, scale_mlp, gain_two)
    grad_residual, wide_sum.send = tie((grad_residual, wide_sum.send))
    wide_sum.move(0)
    grad_low = grad_residual.astype(bf16)
    d_out = lax.dot_general(grad_low, out_theirs, NT, preferred_element_type=f32).astype(bf16)
    d_got = swap(d_out)
    d_mine = lax.dot_general(grad_low, out_mine, NT, preferred_element_type=f32).astype(bf16)
    down_sum = Halving([(gd_mine, swap(gd_theirs), HIGH)])
    down_sum.prepare(0)
    d_mine, d_got, down_sum.send = tie((d_mine, d_got, down_sum.send))
    down_sum.move(0)
    back = lambda b, before: attend_back(
        b, before, me_arr, mine, got, mixed, mixed_out, d_mine, d_got, lse, cosine, sine, piece
    )
    lins = back(0, ())

    lins, grad_low, wide_sum.got, down_sum.got = tie((lins, grad_low, wide_sum.got, down_sum.got))
    low = widen(grad_low[:, : D // 2]), widen(grad_low[:, D // 2 :])

    def grad_out(columns):
        a, b = [
            lax.dot_general(u, columns, TN, preferred_element_type=f32).astype(bf16)[: QD // 2]
            for u in (mixed, mixed_got)
        ]
        return pick(jnp.concatenate([a, b], 0), jnp.concatenate([b, a], 0))

    wide_sum.prepare(1)
    down_sum.prepare(1)
    out_sum = Halving([(grad_out(pick(*low)), swap(grad_out(pick(*low[::-1]))), ORDERS[0])])
    out_sum.prepare(0)
    lins, wide_sum.send, down_sum.send, out_sum.send = tie(
        (lins, wide_sum.send, down_sum.send, out_sum.send)
    )
    wide_sum.move(1)
    down_sum.move(1)
    out_sum.move(0)
    for b in range(1, batch):
        lins = back(b, lins)
    (lin_mine, lin_out), wide_sum.got, down_sum.got, out_sum.got = tie(
        (lins, wide_sum.got, down_sum.got, out_sum.got)
    )
    lin_got = swap(lin_out)
    down_sum.advance(2)
    out_sum.advance(1)
    wide_sum.advance(2)
    grad_n1 = lax.dot_general(lin_mine, w_mine, NT, preferred_element_type=f32) + lax.dot_general(
        lin_got, w_theirs, NT, preferred_element_type=f32
    )
    sum_gain_attn = jnp.sum(grad_n1 * floats * scale_attn, 0)
    column = lax.broadcasted_iota(jnp.int32, (1, WIDE), 1)
    sums = jnp.where(column == QKV, sum_gain_attn[:, None], 0.0) + jnp.where(
        column == QKV + 1, sum_gain_mlp[:, None], 0.0
    )
    weight_grad = lambda lin: (
        lax.dot_general(n1, lin, TN, preferred_element_type=f32) + sums
    ).astype(bf16)
    half = WIDE // 2
    grad_mine, grad_theirs = weight_grad(lin_mine), weight_grad(lin_got)
    grad_got = swap(grad_theirs)
    pack_sum = Halving(
        [
            (grad_mine[:, :half], grad_got[:, :half], ORDERS[0]),
            (grad_mine[:, half:], grad_got[:, half:], ORDERS[1]),
        ]
    )
    pack_sum.prepare(0)
    _, down_sum.got, out_sum.got, wide_sum.got = tie(
        (pack_sum.send, down_sum.got, out_sum.got, wide_sum.got)
    )
    pack_sum.move(0)
    wide_sum.advance(3)
    down_sum.advance(3)
    out_sum.advance(2)
    grad_input = (grad_residual + norm_back(grad_n1, floats, scale_attn, gain_one)).astype(bf16)
    pack_sum.advance(1)
    _, down_sum.got, out_sum.got, wide_sum.got = tie(
        (pack_sum.send, down_sum.got, out_sum.got, wide_sum.got)
    )
    out_sum.advance(3)
    pack_sum.advance(2)
    _, down_sum.got, out_sum.got = tie((pack_sum.send, down_sum.got, out_sum.got))
    r_gate, r_up = wide_sum.finish(4)
    r_down = down_sum.finish(4)[0][:, : D // 2]
    r_out = out_sum.finish(4)[0][:, : D // 2]
    r_pack = jnp.concatenate(pack_sum.finish(3), 1)
    a, b, c = HQ * HEAD_SIZE, (HQ + HK) * HEAD_SIZE, QKV
    shape = layer_input.shape
    return (
        layer_out.reshape(shape),
        grad_input.reshape(shape),
        r_pack[:, :a],
        r_pack[:, a:b],
        r_pack[:, b:c],
        r_out,
        r_pack[:, c],
        r_gate,
        r_up,
        r_down,
        r_pack[:, c + 1],
    )


def solution(mesh):
    tokens, matrix, vector = P(None, "dp", "seq", None), P("dp", "seq"), P("dp")
    placed = (tokens, *[matrix] * 4, vector, *[matrix] * 3, vector, tokens)
    return jax.shard_map(
        local,
        mesh=mesh,
        in_specs=placed,
        out_specs=(tokens, tokens, *[matrix] * 4, vector, *[matrix] * 3, vector),
        check_vma=False,
    )
```

```python
import functools

import jax
import jax.numpy as jnp
from jax import lax
from jax.experimental import pallas as pl
from jax.experimental.pallas import tpu as pltpu
from jax.sharding import PartitionSpec as P

D = 1152
QUERY_HEADS = 18
KEY_VALUE_HEADS = 6
HEAD_SIZE = 64
FF = 3072
BLOCK = 256
QD = 1152
KVD = 384
HQ, HK = QUERY_HEADS // 2, KEY_VALUE_HEADS // 2
HALL = HQ + 2 * HK
QKV = HALL * HEAD_SIZE
FT = 256
HALF = 640
WIDE = 1024

epsilon = 1e-05
bf16, f32 = jnp.bfloat16, jnp.float32
NT = (((1,), (1,)), ((), ()))
NN = (((1,), (0,)), ((), ()))
TN = (((0,), (0,)), ((), ()))
VMEM_BYTES = 62 << 20


def dg(a, b, dims):
    return lax.dot_general(a, b, dims, preferred_element_type=f32)


def assemble(w):
    if w.shape[0] == 1:
        return w[0, 0]
    return jnp.concatenate([w[i, 0].astype(f32) for i in range(w.shape[0])], 0).astype(bf16)


def turned(u, cosine, sine):
    lane = lax.broadcasted_iota(jnp.int32, u.shape, 1)
    h = HEAD_SIZE // 2
    other = jnp.where(lane % HEAD_SIZE < h, pltpu.roll(u, 128 - h, 1), pltpu.roll(u, h, 1))
    return u * cosine + other * sine


def project_body(me, n1, w, cosine, sine, out, flat):
    @pl.when(pl.program_id(0) == 0)
    def _():
        flat[...] = assemble(w)

    u = dg(n1[...], flat[...], NN)
    turns = (HQ + HK) * HEAD_SIZE
    for c in range(0, turns, 128):
        out[:, c : c + 128] = turned(u[:, c : c + 128], cosine[...], sine[...]).astype(bf16)
    out[:, turns:] = u[:, turns:].astype(bf16)


def project(half, me, n1, w, cosine, sine, piece):
    n, _, rows, _ = w.shape
    width = WIDE
    batch = n1.shape[0] // piece
    return pl.pallas_call(
        project_body,
        grid_spec=pltpu.PrefetchScalarGridSpec(
            num_scalar_prefetch=1,
            grid=(batch,),
            in_specs=[
                pl.BlockSpec((piece, D), lambda b, m: (b, 0)),
                pl.BlockSpec((n, 1, rows, width), lambda b, m: (0, m[0] ^ half, 0, 0)),
                pl.BlockSpec((piece, 128), lambda b, m: (m[0], 0)),
                pl.BlockSpec((piece, 128), lambda b, m: (m[0], 0)),
            ],
            out_specs=[
                pl.BlockSpec((piece, width), lambda b, m: (b, 0)),
                pl.BlockSpec((D, width), lambda b, m: (0, 0)),
            ],
        ),
        out_shape=[
            jax.ShapeDtypeStruct((n1.shape[0], width), bf16),
            jax.ShapeDtypeStruct((D, width), bf16),
        ],
        compiler_params=pltpu.CompilerParams(vmem_limit_bytes=VMEM_BYTES),
        cost_estimate=pl.CostEstimate(flops=3 * 10**9, bytes_accessed=12 * 10**6, transcendentals=0),
        name="project",
    )(me, n1, w, cosine, sine)


def head_cols(j):
    return slice(j * HEAD_SIZE, (j + 1) * HEAD_SIZE)


def lane_of(j, shape):
    return lax.broadcasted_iota(jnp.int32, shape, 1) == j


def place(me, mine, got, q, k, v):
    piece = mine.shape[0]
    at = [pl.ds(pl.multiple_of((me[0] ^ a) * piece, piece), piece) for a in range(2)]
    for src, rows in zip((mine, got), at):
        for j in range(HQ):
            q[j, rows, :] = src[:, head_cols(j)] * jnp.asarray(0.125, bf16)
        for j in range(HK):
            k[j, rows, :] = src[:, head_cols(HQ + j)]
            v[j, rows, :] = src[:, head_cols(HQ + HK + j)]
    return at


def fwd_body(me, mine, got, o_mine, o_theirs, lse, q, k, v, o):
    at = place(me, mine, got, q, k, v)
    lse[...] = jnp.zeros_like(lse)

    def head(j, _):
        g = j // (HQ // HK)
        for i in range(lse.shape[0] // BLOCK):
            r = pl.ds(i * BLOCK, BLOCK)
            kw = (i + 1) * BLOCK
            s = dg(q[j, r, :], k[g, :kw, :], NT)
            m = jnp.max(s, axis=1, keepdims=True)
            p = jnp.exp(s - m)
            l = jnp.sum(p, axis=1, keepdims=True)
            mix = dg(p.astype(bf16), v[g, :kw, :], NN)
            o[j, r, :] = (mix / l).astype(bf16)
            lse[r, :] = jnp.where(lane_of(j, (BLOCK, 128)), m + jnp.log(l), lse[r, :])
        return 0

    lax.fori_loop(0, HQ, head, 0)
    for dst, rows in zip((o_mine, o_theirs), at):
        for j in range(HQ):
            dst[:, head_cols(j)] = o[j, rows, :]
        dst[:, HQ * HEAD_SIZE :] = jnp.zeros_like(dst[:, HQ * HEAD_SIZE :])


def bwd_body(
    me, mine, got, o_mine, o_theirs, do_mine, do_got, lse, cosine, sine, *rest
):
    lin_mine, lin_theirs, q, k, v, do, d, dka, dva, inner = rest[-10:]
    at = place(me, mine, got, q, k, v)
    inner[...] = jnp.zeros_like(inner)
    for dsrc, osrc, rows in zip((do_mine, do_got), (o_mine, o_theirs), at):
        for j in range(HQ):
            dj = dsrc[:, head_cols(j)]
            do[j, rows, :] = dj
            part = jnp.sum(dj.astype(f32) * osrc[:, head_cols(j)].astype(f32), axis=1, keepdims=True)
            inner[rows, :] = jnp.where(lane_of(j, (dj.shape[0], 128)), part, inner[rows, :])

    per = HQ // HK

    def head(j, _):
        g = j // per

        @pl.when(j % per == 0)
        def _():
            dka[...] = jnp.zeros_like(dka)
            dva[...] = jnp.zeros_like(dva)

        for i in range(lse.shape[0] // BLOCK):
            r = pl.ds(i * BLOCK, BLOCK)
            kw = (i + 1) * BLOCK
            mark = lane_of(j, (BLOCK, 128))
            column = lambda a: jnp.sum(jnp.where(mark, a[r, :], 0.0), axis=1, keepdims=True)
            qs = q[j, r, :]
            dO = do[j, r, :]
            kk = k[g, :kw, :]
            p = jnp.exp(dg(qs, kk, NT) - column(lse))
            dp = dg(dO, v[g, :kw, :], NT)
            ds = (p * (dp - column(inner))).astype(bf16)
            d[j, r, :] = dg(ds, kk, NN) * 0.125
            dka[:, :kw] += dg(qs.T, ds, NN)
            dva[:, :kw] += dg(dO.T, p.astype(bf16), NN)

        @pl.when(j % per == per - 1)
        def _():
            d[HQ + g] = dka[...].T
            d[HQ + HK + g] = dva[...].T

        return 0

    lax.fori_loop(0, HQ, head, 0)
    turns = HQ + HK
    for dst, rows in zip((lin_mine, lin_theirs), at):
        for j in range(0, HALL + 1, 2):
            a = d[j, rows, :]
            b = d[j + 1, rows, :] if j + 1 < HALL else jnp.zeros_like(a)
            u = jnp.concatenate([a, b], 1)
            if j < turns:
                u = turned(u, cosine[rows, :], -sine[rows, :])
            dst[:, j * HEAD_SIZE : (j + 2) * HEAD_SIZE] = u.astype(bf16)


def attend(me, mine, got, piece):
    tokens, width = mine.shape
    batch = tokens // piece
    row = lambda a, c: pl.BlockSpec((a, c), lambda b, m: (b, 0))
    cols = HALF
    heads = lambda n: pltpu.VMEM((n, 2 * piece, HEAD_SIZE), bf16)
    return pl.pallas_call(
        fwd_body,
        grid_spec=pltpu.PrefetchScalarGridSpec(
            num_scalar_prefetch=1,
            grid=(batch,),
            in_specs=[row(piece, width)] * 2,
            out_specs=[row(piece, cols), row(piece, cols), row(2 * piece, 128)],
            scratch_shapes=[heads(HQ), heads(HK), heads(HK), heads(HQ)],
        ),
        out_shape=[
            jax.ShapeDtypeStruct((tokens, cols), bf16),
            jax.ShapeDtypeStruct((tokens, cols), bf16),
            jax.ShapeDtypeStruct((2 * tokens, 128), f32),
        ],
        compiler_params=pltpu.CompilerParams(vmem_limit_bytes=VMEM_BYTES),
        cost_estimate=pl.CostEstimate(flops=24 * 10**9, bytes_accessed=20 * 10**6, transcendentals=12 * 10**6),
        name="attend",
    )(me, mine, got)


def attend_back(b, before, me, mine, got, o_mine, o_theirs, do_mine, do_got, lse, cosine, sine, piece):
    tokens, width = mine.shape
    row = lambda a, c: pl.BlockSpec((a, c), lambda _, m: (b, 0))
    cols = HALF
    table = pl.BlockSpec((2 * piece, 128), lambda _, m: (0, 0))
    heads = lambda n, t: pltpu.VMEM((n, 2 * piece, HEAD_SIZE), t)
    return pl.pallas_call(
        bwd_body,
        grid_spec=pltpu.PrefetchScalarGridSpec(
            num_scalar_prefetch=1,
            grid=(1,),
            in_specs=[row(piece, width)] * 2
            + [row(piece, cols)] * 4
            + [row(2 * piece, 128), table, table]
            + [pl.BlockSpec(memory_space=pl.ANY)] * len(before),
            out_specs=[row(piece, width)] * 2,
            scratch_shapes=[heads(HQ, bf16), heads(HK, bf16), heads(HK, bf16), heads(HQ, bf16)]
            + [heads(HALL, f32)]
            + [pltpu.VMEM((HEAD_SIZE, 2 * piece), f32)] * 2
            + [pltpu.VMEM((2 * piece, 128), f32)],
        ),
        out_shape=[jax.ShapeDtypeStruct((tokens, width), bf16)] * 2,
        input_output_aliases={10 + i: i for i in range(len(before))},
        compiler_params=pltpu.CompilerParams(vmem_limit_bytes=VMEM_BYTES),
        cost_estimate=pl.CostEstimate(flops=13 * 10**9, bytes_accessed=20 * 10**6, transcendentals=6 * 10**6),
        name="attend_back",
    )(me, mine, got, o_mine, o_theirs, do_mine, do_got, lse, cosine, sine, *before)


def mlp_body(me, n2, n2t, cot, res, wg, wu, wd_mine, wd_theirs, out, gn, gg_mine, gu_mine, gg_theirs, gu_theirs, gd_mine, gd_theirs, y):
    t = pl.program_id(0)
    per = pl.num_programs(0) // 2

    @pl.when(t == 0)
    def _():
        y[...] = res[...]
        gn[...] = jnp.zeros_like(gn)

    half = D // 2
    first = me[0] == 0

    da, db = wd_mine[:, :half], wd_theirs[:, :half]
    wd = jnp.concatenate([jnp.where(first, da, db), jnp.where(first, db, da)], axis=1)
    wgt, wut = assemble(wg), assemble(wu)
    gate = dg(n2[...], wgt, NN)
    up = dg(n2[...], wut, NN)
    gh = dg(cot[...], wd, NT)
    sig = jax.nn.sigmoid(gate)
    act = gate * sig
    hidden = (act * up).astype(bf16)
    ggv = (gh * up * sig * (1.0 + gate * (1.0 - sig))).astype(bf16)
    guv = (gh * act).astype(bf16)
    y[...] += dg(hidden, wd, NN)
    gdt = dg(hidden, cot[...], TN)
    for dst, u in (
        (gd_mine, jnp.where(first, gdt[:, :half], gdt[:, half:])),
        (gd_theirs, jnp.where(first, gdt[:, half:], gdt[:, :half])),
    ):
        dst[:, :half] = u.astype(bf16)
        dst[:, half:] = jnp.zeros((FT, HALF - half), bf16)
    gg = dg(n2t[...], ggv, NN).astype(bf16)
    gu = dg(n2t[...], guv, NN).astype(bf16)

    @pl.when(t < per)
    def _():
        gg_theirs[...] = gg
        gu_theirs[...] = gu

    @pl.when(t >= per)
    def _():
        gg_mine[...] = gg
        gu_mine[...] = gu

    gn[...] += dg(ggv, wgt, NT) + dg(guv, wut, NT)

    @pl.when(t == pl.num_programs(0) - 1)
    def _():
        out[...] = y[...].astype(bf16)


def mlp(me, n2, n2t, cot, res, wide, wd_mine, wd_theirs):
    tokens = n2.shape[0]
    n, _, rows, _ = wide.shape
    cols = FF // 2
    per = cols // FT
    half = lambda t, m: 1 - m[0] ^ t // per
    whole = lambda a: pl.BlockSpec(a.shape, lambda t, m: (0, 0), pipeline_mode=pl.Buffered(1))
    col = lambda first: pl.BlockSpec(
        (n, 1, rows, FT), lambda t, m: (0, half(t, m), 0, first + t % per)
    )
    part = pl.BlockSpec((FT, HALF), lambda t, m: (half(t, m) * per + t % per, 0))
    one = lambda: pl.BlockSpec((tokens, D), lambda t, m: (0, 0), pipeline_mode=pl.Buffered(1))
    return pl.pallas_call(
        mlp_body,
        grid_spec=pltpu.PrefetchScalarGridSpec(
            num_scalar_prefetch=1,
            grid=(FF // FT,),
            in_specs=[whole(n2), whole(n2t), whole(cot), whole(res), col(0), col(per), part, part],
            out_specs=[
                one(),
                one(),
                *[pl.BlockSpec((D, FT), lambda t, m: (0, jnp.maximum(t - per, 0)))] * 2,
                *[pl.BlockSpec((D, FT), lambda t, m: (0, jnp.minimum(t, per - 1)))] * 2,
                part,
                part,
            ],
            scratch_shapes=[pltpu.VMEM((tokens, D), f32)],
        ),
        out_shape=[
            jax.ShapeDtypeStruct((tokens, D), bf16),
            jax.ShapeDtypeStruct((tokens, D), f32),
            *[jax.ShapeDtypeStruct((D, cols), bf16)] * 4,
            jax.ShapeDtypeStruct((FF, HALF), bf16),
            jax.ShapeDtypeStruct((FF, HALF), bf16),
        ],
        compiler_params=pltpu.CompilerParams(vmem_limit_bytes=VMEM_BYTES),
        cost_estimate=pl.CostEstimate(flops=65 * 10**9, bytes_accessed=60 * 10**6, transcendentals=3 * 10**6),
        name="mlp",
    )(me, n2, n2t, cot, res, wide, wide, wd_mine, wd_theirs)


def norm_back(grad_norm, rows_in, scale_rows, gain_rows):
    weighted = grad_norm * gain_rows
    cube_rows = scale_rows * scale_rows * scale_rows
    return scale_rows * weighted - rows_in * cube_rows * jnp.mean(
        weighted * rows_in, -1, keepdims=True
    )


def swap(a):
    return lax.ppermute(a, "seq", [(0, 1), (1, 0)])


BOTH = ("dp", "seq")


def whole_halves(g):
    return jnp.swapaxes(g, 0, 1).reshape(1, 2, -1, g.shape[3])


def fetch(w):
    g = lax.all_gather(w, BOTH, axis=0, tiled=True).reshape(lax.axis_size("dp"), 2, *w.shape)
    return g if w.shape[0] % 8 == 0 else whole_halves(g)


def exchange(a, bit):
    return lax.ppermute(a, "dp", [(i, i ^ (1 << bit)) for i in range(lax.axis_size("dp"))])


ORDERS = (0, 1), (1, 0)
HIGH, LAST = (), (0, 1)


def doubled(a, got, bit, axis):
    low = (lax.axis_index("dp") >> bit) & 1 == 0
    return jnp.where(low, jnp.stack([a, got], axis), jnp.stack([got, a], axis))


def gather_doubling(w):
    bits = lax.axis_size("dp").bit_length() - 1
    cut = w.shape[1] // 256 * 128
    out = []
    for part, order in ((w[:, :cut], ORDERS[0]), (w[:, cut:], ORDERS[1])):
        last, have = None, []
        for bit in list(range(bits))[:1:-1] + list(order[::-1]):
            a = part if last is None else doubled(*last)
            last = a, exchange(a, bit), bit, sum(b > bit for b in have)
            have.append(bit)
        out.append(last)
    return out


def gather_finish(lasts):
    out = [doubled(*last) for last in lasts]
    mine = jnp.concatenate([a.reshape(-1, a.shape[-1]) for a in out], 1)
    return mine, swap(mine)


def add(a, b):
    return a.astype(f32) + b.astype(f32)


class Halving:
    def __init__(self, parts, kind=bf16):
        self.kind = kind
        bits = lax.axis_size("dp").bit_length() - 1
        self.steps = bits
        rest = list(range(2, bits))
        ways = {ORDERS[0]: [*ORDERS[0], *rest], ORDERS[1]: [*ORDERS[1], *rest[::-1]], HIGH: [*rest, *LAST]}
        self.orders = [ways[order] for _, _, order in parts]
        shape = lambda u: u.reshape(*[2] * bits, -1, u.shape[-1])
        self.stay = [shape(u) for u, _, _ in parts]
        self.got = [shape(v) for _, v, _ in parts]

    def prepare(self, step):
        self.send = []
        for p, order in enumerate(self.orders):
            bit = order[step]
            axis = sum(b > bit for b in order[step:])
            mybit = (lax.axis_index("dp") >> bit) & 1
            at = lambda u, i: lax.dynamic_index_in_dim(u, i, axis, keepdims=False)
            total = lambda i: add(at(self.stay[p], i), at(self.got[p], i)).astype(self.kind)
            self.send.append(total(1 - mybit))
            self.stay[p] = total(mybit)

    def move(self, step):
        self.got = [exchange(a, order[step]) for a, order in zip(self.send, self.orders)]

    def advance(self, step):
        self.prepare(step)
        self.move(step)

    def finish(self, step=0):
        for i in range(step, self.steps):
            self.advance(i)
        return [add(*u) for u in zip(self.stay, self.got)]


def local(
    layer_input,
    w_query,
    w_key,
    w_value,
    w_out,
    gain_attn,
    w_gate,
    w_up,
    w_down,
    gain_mlp,
    cotangent,
):
    batch, _, piece, _ = layer_input.shape
    tokens = batch * piece
    me = lax.axis_index("seq")
    me_arr = jnp.full((1,), me, jnp.int32)
    pick = lambda a, b: jnp.where(me == 0, a, b)
    tie = lax.optimization_barrier
    h = HEAD_SIZE // 2
    frequency = 10000.0 ** (-2.0 * jnp.arange(h).astype(f32) / HEAD_SIZE)
    angles = jnp.arange(2 * piece).astype(f32)[:, None] * jnp.tile(frequency, 128 // h)[None, :]
    cosine = jnp.cos(angles)
    sine = jnp.sin(angles) * jnp.where(jnp.arange(128) % HEAD_SIZE < h, -1.0, 1.0)[None, :]

    gains = jnp.pad(jnp.stack([gain_attn, gain_mlp], 1), ((0, 0), (0, WIDE - QKV - 2)))
    full = fetch(jnp.concatenate([w_query, w_key, w_value, gains, w_out], 1))
    wide = fetch(jnp.concatenate([w_gate, w_up], 1))
    widen = lambda a: jnp.pad(a, ((0, 0), (0, HALF - D // 2)))
    down_last = gather_doubling(widen(w_down))
    full, _ = tie((full, [last[0] for last in down_last]))
    gain_one = full[:, 0, :, QKV].reshape(D).astype(f32)
    gain_two = full[:, 0, :, QKV + 1].reshape(D).astype(f32)
    out_halves = whole_halves(full[..., WIDE:])[0].reshape(2, 2, D // 2, D // 2)
    out_rows = lambda c: jnp.concatenate(
        [lax.dynamic_index_in_dim(out_halves[i], c, 0, keepdims=False) for i in range(2)], 1
    )
    out_mine, out_theirs = [jnp.pad(out_rows(c), ((0, HALF - D // 2), (0, 0))) for c in (me, 1 - me)]

    floats = layer_input.reshape(tokens, D).astype(f32)
    cot = cotangent.reshape(tokens, D)
    scale_attn = lax.rsqrt(jnp.mean(floats * floats, -1, keepdims=True) + epsilon)
    n1 = (floats * scale_attn * gain_one).astype(bf16)
    dot = lambda a, b: lax.dot_general(a, b, NN, preferred_element_type=f32)

    heads_out, w_theirs = project(1, me_arr, n1, full, cosine, sine, piece)
    got = swap(heads_out)
    mine, w_mine = project(0, me_arr, n1, full, cosine, sine, piece)
    mixed, mixed_out, lse = attend(me_arr, mine, got, piece)
    mixed_out, arrived = tie((mixed_out, [last[1] for last in down_last]))
    down_mine, down_theirs = gather_finish(
        [(a, b, bit, axis) for (a, _, bit, axis), b in zip(down_last, arrived)]
    )
    mixed_got = swap(mixed_out)
    residual = floats + (dot(mixed, out_mine) + dot(mixed_got, out_theirs))
    scale_mlp = lax.rsqrt(jnp.mean(residual * residual, -1, keepdims=True) + epsilon)
    n2 = (residual * scale_mlp * gain_two).astype(bf16)
    layer_out, grad_n2, gg_mine, gu_mine, gg_theirs, gu_theirs, gd_mine, gd_theirs = mlp(
        me_arr, n2, n2.T, cot, residual, wide, down_mine, down_theirs
    )
    wide_sum = Halving([(gg_mine, swap(gg_theirs), ORDERS[0]), (gu_mine, swap(gu_theirs), ORDERS[1])])
    wide_sum.prepare(0)
    sum_gain_mlp = jnp.sum(grad_n2 * residual * scale_mlp, 0)
    grad_residual = cot.astype(f32) + norm_back(grad_n2, residual, scale_mlp, gain_two)
    grad_residual, wide_sum.send = tie((grad_residual, wide_sum.send))
    wide_sum.move(0)
    grad_low = grad_residual.astype(bf16)
    d_out = lax.dot_general(grad_low, out_theirs, NT, preferred_element_type=f32).astype(bf16)
    d_got = swap(d_out)
    d_mine = lax.dot_general(grad_low, out_mine, NT, preferred_element_type=f32).astype(bf16)
    down_sum = Halving([(gd_mine, swap(gd_theirs), HIGH)])
    down_sum.prepare(0)
    d_mine, d_got, down_sum.send = tie((d_mine, d_got, down_sum.send))
    down_sum.move(0)
    back = lambda b, before: attend_back(
        b, before, me_arr, mine, got, mixed, mixed_out, d_mine, d_got, lse, cosine, sine, piece
    )
    lins = back(0, ())

    lins, grad_low = tie((lins, grad_low))
    parts_of = lambda u: (widen(u[:, : D // 2]), widen(u[:, D // 2 :]))

    def grad_out(columns):
        a, b = [
            lax.dot_general(u, columns, TN, preferred_element_type=f32).astype(bf16)[: QD // 2]
            for u in (mixed, mixed_got)
        ]
        return pick(jnp.concatenate([a, b], 0), jnp.concatenate([b, a], 0))

    out_theirs_grad = grad_out(pick(*parts_of(grad_low)[::-1]))
    out_theirs_grad, grad_low, wide_sum.got, down_sum.got = tie(
        (out_theirs_grad, grad_low, wide_sum.got, down_sum.got)
    )
    wide_sum.prepare(1)
    down_sum.prepare(1)
    out_sum = Halving([(grad_out(pick(*parts_of(grad_low))), swap(out_theirs_grad), ORDERS[0])])
    out_sum.prepare(0)
    lins, wide_sum.send, down_sum.send, out_sum.send = tie(
        (lins, wide_sum.send, down_sum.send, out_sum.send)
    )
    wide_sum.move(1)
    down_sum.move(1)
    out_sum.move(0)
    for b in range(1, batch):
        lins = back(b, lins)
    (lin_mine, lin_out), wide_sum.got, down_sum.got, out_sum.got = tie(
        (lins, wide_sum.got, down_sum.got, out_sum.got)
    )
    lin_got = swap(lin_out)
    down_sum.advance(2)
    out_sum.advance(1)
    wide_sum.advance(2)
    grad_n1 = lax.dot_general(lin_mine, w_mine, NT, preferred_element_type=f32) + lax.dot_general(
        lin_got, w_theirs, NT, preferred_element_type=f32
    )
    sum_gain_attn = jnp.sum(grad_n1 * floats * scale_attn, 0)
    column = lax.broadcasted_iota(jnp.int32, (1, WIDE), 1)
    sums = jnp.where(column == QKV, sum_gain_attn[:, None], 0.0) + jnp.where(
        column == QKV + 1, sum_gain_mlp[:, None], 0.0
    )
    weight_grad = lambda lin: (
        lax.dot_general(n1, lin, TN, preferred_element_type=f32) + sums
    ).astype(bf16)
    half = WIDE // 2
    grad_mine, grad_theirs = weight_grad(lin_mine), weight_grad(lin_got)
    grad_got = swap(grad_theirs)
    pack_sum = Halving(
        [
            (grad_mine[:, :half], grad_got[:, :half], ORDERS[0]),
            (grad_mine[:, half:], grad_got[:, half:], ORDERS[1]),
        ]
    )
    pack_sum.prepare(0)
    _, down_sum.got, out_sum.got, wide_sum.got = tie(
        (pack_sum.send, down_sum.got, out_sum.got, wide_sum.got)
    )
    pack_sum.move(0)
    wide_sum.advance(3)
    down_sum.advance(3)
    out_sum.advance(2)
    grad_input = (grad_residual + norm_back(grad_n1, floats, scale_attn, gain_one)).astype(bf16)
    pack_sum.advance(1)
    _, down_sum.got, out_sum.got, wide_sum.got = tie(
        (pack_sum.send, down_sum.got, out_sum.got, wide_sum.got)
    )
    out_sum.advance(3)
    pack_sum.advance(2)
    _, down_sum.got, out_sum.got = tie((pack_sum.send, down_sum.got, out_sum.got))
    r_gate, r_up = wide_sum.finish(4)
    r_down = down_sum.finish(4)[0][:, : D // 2]
    r_out = out_sum.finish(4)[0][:, : D // 2]
    r_pack = jnp.concatenate(pack_sum.finish(3), 1)
    a, b, c = HQ * HEAD_SIZE, (HQ + HK) * HEAD_SIZE, QKV
    shape = layer_input.shape
    return (
        layer_out.reshape(shape),
        grad_input.reshape(shape),
        r_pack[:, :a],
        r_pack[:, a:b],
        r_pack[:, b:c],
        r_out,
        r_pack[:, c],
        r_gate,
        r_up,
        r_down,
        r_pack[:, c + 1],
    )


def solution(mesh):
    tokens, matrix, vector = P(None, "dp", "seq", None), P("dp", "seq"), P("dp")
    placed = (tokens, *[matrix] * 4, vector, *[matrix] * 3, vector, tokens)
    return jax.shard_map(
        local,
        mesh=mesh,
        in_specs=placed,
        out_specs=(tokens, tokens, *[matrix] * 4, vector, *[matrix] * 3, vector),
        check_vma=False,
    )
```

```python
import functools

import jax
import jax.numpy as jnp
from jax import lax
from jax.experimental import pallas as pl
from jax.experimental.pallas import tpu as pltpu
from jax.sharding import PartitionSpec as P

D = 1152
QUERY_HEADS = 18
KEY_VALUE_HEADS = 6
HEAD_SIZE = 64
FF = 3072
BLOCK = 256
QD = 1152
KVD = 384
HQ, HK = QUERY_HEADS // 2, KEY_VALUE_HEADS // 2
HALL = HQ + 2 * HK
QKV = HALL * HEAD_SIZE
FT = 256
HALF = 640
WIDE = 1024

epsilon = 1e-05
bf16, f32 = jnp.bfloat16, jnp.float32
NT = (((1,), (1,)), ((), ()))
NN = (((1,), (0,)), ((), ()))
TN = (((0,), (0,)), ((), ()))
VMEM_BYTES = 62 << 20


def dg(a, b, dims):
    return lax.dot_general(a, b, dims, preferred_element_type=f32)


def assemble(w):
    if w.shape[0] == 1:
        return w[0, 0]
    return jnp.concatenate([w[i, 0].astype(f32) for i in range(w.shape[0])], 0).astype(bf16)


def turned(u, cosine, sine):
    lane = lax.broadcasted_iota(jnp.int32, u.shape, 1)
    h = HEAD_SIZE // 2
    other = jnp.where(lane % HEAD_SIZE < h, pltpu.roll(u, 128 - h, 1), pltpu.roll(u, h, 1))
    return u * cosine + other * sine


def project_body(me, n1, w, cosine, sine, out, flat):
    @pl.when(pl.program_id(0) == 0)
    def _():
        flat[...] = assemble(w)

    u = dg(n1[...], flat[...], NN)
    turns = (HQ + HK) * HEAD_SIZE
    for c in range(0, turns, 128):
        out[:, c : c + 128] = turned(u[:, c : c + 128], cosine[...], sine[...]).astype(bf16)
    out[:, turns:] = u[:, turns:].astype(bf16)


def project(half, me, n1, w, cosine, sine, piece):
    n, _, rows, _ = w.shape
    width = WIDE
    batch = n1.shape[0] // piece
    return pl.pallas_call(
        project_body,
        grid_spec=pltpu.PrefetchScalarGridSpec(
            num_scalar_prefetch=1,
            grid=(batch,),
            in_specs=[
                pl.BlockSpec((piece, D), lambda b, m: (b, 0)),
                pl.BlockSpec((n, 1, rows, width), lambda b, m: (0, m[0] ^ half, 0, 0)),
                pl.BlockSpec((piece, 128), lambda b, m: (m[0], 0)),
                pl.BlockSpec((piece, 128), lambda b, m: (m[0], 0)),
            ],
            out_specs=[
                pl.BlockSpec((piece, width), lambda b, m: (b, 0)),
                pl.BlockSpec((D, width), lambda b, m: (0, 0)),
            ],
        ),
        out_shape=[
            jax.ShapeDtypeStruct((n1.shape[0], width), bf16),
            jax.ShapeDtypeStruct((D, width), bf16),
        ],
        compiler_params=pltpu.CompilerParams(vmem_limit_bytes=VMEM_BYTES),
        cost_estimate=pl.CostEstimate(flops=3 * 10**9, bytes_accessed=12 * 10**6, transcendentals=0),
        name="project",
    )(me, n1, w, cosine, sine)


def head_cols(j):
    return slice(j * HEAD_SIZE, (j + 1) * HEAD_SIZE)


def lane_of(j, shape):
    return lax.broadcasted_iota(jnp.int32, shape, 1) == j


def place(me, mine, got, q, k, v):
    piece = mine.shape[0]
    at = [pl.ds(pl.multiple_of((me[0] ^ a) * piece, piece), piece) for a in range(2)]
    for src, rows in zip((mine, got), at):
        for j in range(HQ):
            q[j, rows, :] = src[:, head_cols(j)] * jnp.asarray(0.125, bf16)
        for j in range(HK):
            k[j, rows, :] = src[:, head_cols(HQ + j)]
            v[j, rows, :] = src[:, head_cols(HQ + HK + j)]
    return at


def fwd_body(me, mine, got, o_mine, o_theirs, lse, q, k, v, o):
    at = place(me, mine, got, q, k, v)
    lse[...] = jnp.zeros_like(lse)

    def head(j, _):
        g = j // (HQ // HK)
        for i in range(lse.shape[0] // BLOCK):
            r = pl.ds(i * BLOCK, BLOCK)
            kw = (i + 1) * BLOCK
            s = dg(q[j, r, :], k[g, :kw, :], NT)
            m = jnp.max(s, axis=1, keepdims=True)
            p = jnp.exp(s - m)
            l = jnp.sum(p, axis=1, keepdims=True)
            mix = dg(p.astype(bf16), v[g, :kw, :], NN)
            o[j, r, :] = (mix / l).astype(bf16)
            lse[r, :] = jnp.where(lane_of(j, (BLOCK, 128)), m + jnp.log(l), lse[r, :])
        return 0

    lax.fori_loop(0, HQ, head, 0)
    for dst, rows in zip((o_mine, o_theirs), at):
        for j in range(HQ):
            dst[:, head_cols(j)] = o[j, rows, :]
        dst[:, HQ * HEAD_SIZE :] = jnp.zeros_like(dst[:, HQ * HEAD_SIZE :])


def bwd_body(
    me, mine, got, o_mine, o_theirs, do_mine, do_got, lse, cosine, sine, *rest
):
    lin_mine, lin_theirs, q, k, v, do, d, dka, dva, inner = rest[-10:]
    at = place(me, mine, got, q, k, v)
    inner[...] = jnp.zeros_like(inner)
    for dsrc, osrc, rows in zip((do_mine, do_got), (o_mine, o_theirs), at):
        for j in range(HQ):
            dj = dsrc[:, head_cols(j)]
            do[j, rows, :] = dj
            part = jnp.sum(dj.astype(f32) * osrc[:, head_cols(j)].astype(f32), axis=1, keepdims=True)
            inner[rows, :] = jnp.where(lane_of(j, (dj.shape[0], 128)), part, inner[rows, :])

    per = HQ // HK

    def head(j, _):
        g = j // per

        @pl.when(j % per == 0)
        def _():
            dka[...] = jnp.zeros_like(dka)
            dva[...] = jnp.zeros_like(dva)

        for i in range(lse.shape[0] // BLOCK):
            r = pl.ds(i * BLOCK, BLOCK)
            kw = (i + 1) * BLOCK
            mark = lane_of(j, (BLOCK, 128))
            column = lambda a: jnp.sum(jnp.where(mark, a[r, :], 0.0), axis=1, keepdims=True)
            qs = q[j, r, :]
            dO = do[j, r, :]
            kk = k[g, :kw, :]
            p = jnp.exp(dg(qs, kk, NT) - column(lse))
            dp = dg(dO, v[g, :kw, :], NT)
            ds = (p * (dp - column(inner))).astype(bf16)
            d[j, r, :] = dg(ds, kk, NN) * 0.125
            dka[:, :kw] += dg(qs.T, ds, NN)
            dva[:, :kw] += dg(dO.T, p.astype(bf16), NN)

        @pl.when(j % per == per - 1)
        def _():
            d[HQ + g] = dka[...].T
            d[HQ + HK + g] = dva[...].T

        return 0

    lax.fori_loop(0, HQ, head, 0)
    turns = HQ + HK
    for dst, rows in zip((lin_mine, lin_theirs), at):
        for j in range(0, HALL + 1, 2):
            a = d[j, rows, :]
            b = d[j + 1, rows, :] if j + 1 < HALL else jnp.zeros_like(a)
            u = jnp.concatenate([a, b], 1)
            if j < turns:
                u = turned(u, cosine[rows, :], -sine[rows, :])
            dst[:, j * HEAD_SIZE : (j + 2) * HEAD_SIZE] = u.astype(bf16)


def attend(me, mine, got, piece):
    tokens, width = mine.shape
    batch = tokens // piece
    row = lambda a, c: pl.BlockSpec((a, c), lambda b, m: (b, 0))
    cols = HALF
    heads = lambda n: pltpu.VMEM((n, 2 * piece, HEAD_SIZE), bf16)
    return pl.pallas_call(
        fwd_body,
        grid_spec=pltpu.PrefetchScalarGridSpec(
            num_scalar_prefetch=1,
            grid=(batch,),
            in_specs=[row(piece, width)] * 2,
            out_specs=[row(piece, cols), row(piece, cols), row(2 * piece, 128)],
            scratch_shapes=[heads(HQ), heads(HK), heads(HK), heads(HQ)],
        ),
        out_shape=[
            jax.ShapeDtypeStruct((tokens, cols), bf16),
            jax.ShapeDtypeStruct((tokens, cols), bf16),
            jax.ShapeDtypeStruct((2 * tokens, 128), f32),
        ],
        compiler_params=pltpu.CompilerParams(vmem_limit_bytes=VMEM_BYTES),
        cost_estimate=pl.CostEstimate(flops=24 * 10**9, bytes_accessed=20 * 10**6, transcendentals=12 * 10**6),
        name="attend",
    )(me, mine, got)


def attend_back(b, before, me, mine, got, o_mine, o_theirs, do_mine, do_got, lse, cosine, sine, piece):
    tokens, width = mine.shape
    row = lambda a, c: pl.BlockSpec((a, c), lambda _, m: (b, 0))
    cols = HALF
    table = pl.BlockSpec((2 * piece, 128), lambda _, m: (0, 0))
    heads = lambda n, t: pltpu.VMEM((n, 2 * piece, HEAD_SIZE), t)
    return pl.pallas_call(
        bwd_body,
        grid_spec=pltpu.PrefetchScalarGridSpec(
            num_scalar_prefetch=1,
            grid=(1,),
            in_specs=[row(piece, width)] * 2
            + [row(piece, cols)] * 4
            + [row(2 * piece, 128), table, table]
            + [pl.BlockSpec(memory_space=pl.ANY)] * len(before),
            out_specs=[row(piece, width)] * 2,
            scratch_shapes=[heads(HQ, bf16), heads(HK, bf16), heads(HK, bf16), heads(HQ, bf16)]
            + [heads(HALL, f32)]
            + [pltpu.VMEM((HEAD_SIZE, 2 * piece), f32)] * 2
            + [pltpu.VMEM((2 * piece, 128), f32)],
        ),
        out_shape=[jax.ShapeDtypeStruct((tokens, width), bf16)] * 2,
        input_output_aliases={10 + i: i for i in range(len(before))},
        compiler_params=pltpu.CompilerParams(vmem_limit_bytes=VMEM_BYTES),
        cost_estimate=pl.CostEstimate(flops=13 * 10**9, bytes_accessed=20 * 10**6, transcendentals=6 * 10**6),
        name="attend_back",
    )(me, mine, got, o_mine, o_theirs, do_mine, do_got, lse, cosine, sine, *before)


def mlp_body(me, n2, n2t, cot, res, wg, wu, wd_mine, wd_theirs, out, gn, gg_mine, gu_mine, gg_theirs, gu_theirs, gd_mine, gd_theirs, y):
    t = pl.program_id(0)
    per = pl.num_programs(0) // 2

    @pl.when(t == 0)
    def _():
        y[...] = res[...]
        gn[...] = jnp.zeros_like(gn)

    half = D // 2
    first = me[0] == 0

    da, db = wd_mine[:, :half], wd_theirs[:, :half]
    wd = jnp.concatenate([jnp.where(first, da, db), jnp.where(first, db, da)], axis=1)
    wgt, wut = assemble(wg), assemble(wu)
    gate = dg(n2[...], wgt, NN)
    up = dg(n2[...], wut, NN)
    gh = dg(cot[...], wd, NT)
    sig = jax.nn.sigmoid(gate)
    act = gate * sig
    hidden = (act * up).astype(bf16)
    ggv = (gh * up * sig * (1.0 + gate * (1.0 - sig))).astype(bf16)
    guv = (gh * act).astype(bf16)
    y[...] += dg(hidden, wd, NN)
    gdt = dg(hidden, cot[...], TN)
    for dst, u in (
        (gd_mine, jnp.where(first, gdt[:, :half], gdt[:, half:])),
        (gd_theirs, jnp.where(first, gdt[:, half:], gdt[:, :half])),
    ):
        dst[:, :half] = u.astype(bf16)
        dst[:, half:] = jnp.zeros((FT, HALF - half), bf16)
    gg = dg(n2t[...], ggv, NN).astype(bf16)
    gu = dg(n2t[...], guv, NN).astype(bf16)

    @pl.when(t < per)
    def _():
        gg_theirs[...] = gg
        gu_theirs[...] = gu

    @pl.when(t >= per)
    def _():
        gg_mine[...] = gg
        gu_mine[...] = gu

    gn[...] += dg(ggv, wgt, NT) + dg(guv, wut, NT)

    @pl.when(t == pl.num_programs(0) - 1)
    def _():
        out[...] = y[...].astype(bf16)


def mlp(me, n2, n2t, cot, res, wide, wd_mine, wd_theirs):
    tokens = n2.shape[0]
    n, _, rows, _ = wide.shape
    cols = FF // 2
    per = cols // FT
    half = lambda t, m: 1 - m[0] ^ t // per
    whole = lambda a: pl.BlockSpec(a.shape, lambda t, m: (0, 0), pipeline_mode=pl.Buffered(1))
    col = lambda first: pl.BlockSpec(
        (n, 1, rows, FT), lambda t, m: (0, half(t, m), 0, first + t % per)
    )
    part = pl.BlockSpec((FT, HALF), lambda t, m: (half(t, m) * per + t % per, 0))
    one = lambda: pl.BlockSpec((tokens, D), lambda t, m: (0, 0), pipeline_mode=pl.Buffered(1))
    return pl.pallas_call(
        mlp_body,
        grid_spec=pltpu.PrefetchScalarGridSpec(
            num_scalar_prefetch=1,
            grid=(FF // FT,),
            in_specs=[whole(n2), whole(n2t), whole(cot), whole(res), col(0), col(per), part, part],
            out_specs=[
                one(),
                one(),
                *[pl.BlockSpec((D, FT), lambda t, m: (0, jnp.maximum(t - per, 0)))] * 2,
                *[pl.BlockSpec((D, FT), lambda t, m: (0, jnp.minimum(t, per - 1)))] * 2,
                part,
                part,
            ],
            scratch_shapes=[pltpu.VMEM((tokens, D), f32)],
        ),
        out_shape=[
            jax.ShapeDtypeStruct((tokens, D), bf16),
            jax.ShapeDtypeStruct((tokens, D), f32),
            *[jax.ShapeDtypeStruct((D, cols), bf16)] * 4,
            jax.ShapeDtypeStruct((FF, HALF), bf16),
            jax.ShapeDtypeStruct((FF, HALF), bf16),
        ],
        compiler_params=pltpu.CompilerParams(vmem_limit_bytes=VMEM_BYTES),
        cost_estimate=pl.CostEstimate(flops=65 * 10**9, bytes_accessed=60 * 10**6, transcendentals=3 * 10**6),
        name="mlp",
    )(me, n2, n2t, cot, res, wide, wide, wd_mine, wd_theirs)


def norm_back(grad_norm, rows_in, scale_rows, gain_rows):
    weighted = grad_norm * gain_rows
    cube_rows = scale_rows * scale_rows * scale_rows
    return scale_rows * weighted - rows_in * cube_rows * jnp.mean(
        weighted * rows_in, -1, keepdims=True
    )


def swap(a):
    return lax.ppermute(a, "seq", [(0, 1), (1, 0)])


BOTH = ("dp", "seq")


def whole_halves(g):
    return jnp.swapaxes(g, 0, 1).reshape(1, 2, -1, g.shape[3])


def fetch(w):
    g = lax.all_gather(w, BOTH, axis=0, tiled=True).reshape(lax.axis_size("dp"), 2, *w.shape)
    return g if w.shape[0] % 8 == 0 else whole_halves(g)


def exchange(a, bit):
    return lax.ppermute(a, "dp", [(i, i ^ (1 << bit)) for i in range(lax.axis_size("dp"))])


ORDERS = (0, 1), (1, 0)
HIGH, LAST = (), (0, 1)


def doubled(a, got, bit, axis):
    low = (lax.axis_index("dp") >> bit) & 1 == 0
    return jnp.where(low, jnp.stack([a, got], axis), jnp.stack([got, a], axis))


def gather_doubling(w):
    bits = lax.axis_size("dp").bit_length() - 1
    cut = w.shape[1] // 256 * 128
    out = []
    for part, order in ((w[:, :cut], ORDERS[0]), (w[:, cut:], ORDERS[1])):
        last, have = None, []
        for bit in list(range(bits))[:1:-1] + list(order[::-1]):
            a = part if last is None else doubled(*last)
            last = a, exchange(a, bit), bit, sum(b > bit for b in have)
            have.append(bit)
        out.append(last)
    return out


def gather_finish(lasts):
    out = [doubled(*last) for last in lasts]
    mine = jnp.concatenate([a.reshape(-1, a.shape[-1]) for a in out], 1)
    return mine, swap(mine)


def add(a, b):
    return a.astype(f32) + b.astype(f32)


class Halving:
    def __init__(self, parts, kind=bf16):
        self.kind = kind
        bits = lax.axis_size("dp").bit_length() - 1
        self.steps = bits
        rest = list(range(2, bits))
        ways = {ORDERS[0]: [*ORDERS[0], *rest], ORDERS[1]: [*ORDERS[1], *rest[::-1]], HIGH: [*rest, *LAST]}
        self.orders = [ways[order] for _, _, order in parts]
        shape = lambda u: u.reshape(*[2] * bits, -1, u.shape[-1])
        self.stay = [shape(u) for u, _, _ in parts]
        self.got = [shape(v) for _, v, _ in parts]

    def prepare(self, step):
        self.send = []
        for p, order in enumerate(self.orders):
            bit = order[step]
            axis = sum(b > bit for b in order[step:])
            mybit = (lax.axis_index("dp") >> bit) & 1
            at = lambda u, i: lax.dynamic_index_in_dim(u, i, axis, keepdims=False)
            total = lambda i: add(at(self.stay[p], i), at(self.got[p], i)).astype(self.kind)
            self.send.append(total(1 - mybit))
            self.stay[p] = total(mybit)

    def move(self, step):
        self.got = [exchange(a, order[step]) for a, order in zip(self.send, self.orders)]

    def advance(self, step):
        self.prepare(step)
        self.move(step)

    def finish(self, step=0):
        for i in range(step, self.steps):
            self.advance(i)
        return [add(*u) for u in zip(self.stay, self.got)]


def local(
    layer_input,
    w_query,
    w_key,
    w_value,
    w_out,
    gain_attn,
    w_gate,
    w_up,
    w_down,
    gain_mlp,
    cotangent,
):
    batch, _, piece, _ = layer_input.shape
    tokens = batch * piece
    me = lax.axis_index("seq")
    me_arr = jnp.full((1,), me, jnp.int32)
    pick = lambda a, b: jnp.where(me == 0, a, b)
    tie = lax.optimization_barrier
    h = HEAD_SIZE // 2
    frequency = 10000.0 ** (-2.0 * jnp.arange(h).astype(f32) / HEAD_SIZE)
    angles = jnp.arange(2 * piece).astype(f32)[:, None] * jnp.tile(frequency, 128 // h)[None, :]
    cosine = jnp.cos(angles)
    sine = jnp.sin(angles) * jnp.where(jnp.arange(128) % HEAD_SIZE < h, -1.0, 1.0)[None, :]

    gains = jnp.pad(jnp.stack([gain_attn, gain_mlp], 1), ((0, 0), (0, WIDE - QKV - 2)))
    full = fetch(jnp.concatenate([w_query, w_key, w_value, gains, w_out], 1))
    wide = fetch(jnp.concatenate([w_gate, w_up], 1))
    widen = lambda a: jnp.pad(a, ((0, 0), (0, HALF - D // 2)))
    down_last = gather_doubling(widen(w_down))
    full, _ = tie((full, [last[0] for last in down_last]))
    gain_one = full[:, 0, :, QKV].reshape(D).astype(f32)
    gain_two = full[:, 0, :, QKV + 1].reshape(D).astype(f32)
    out_halves = whole_halves(full[..., WIDE:])[0].reshape(2, 2, D // 2, D // 2)
    out_rows = lambda c: jnp.concatenate(
        [lax.dynamic_index_in_dim(out_halves[i], c, 0, keepdims=False) for i in range(2)], 1
    )
    out_mine, out_theirs = [jnp.pad(out_rows(c), ((0, HALF - D // 2), (0, 0))) for c in (me, 1 - me)]

    floats = layer_input.reshape(tokens, D).astype(f32)
    cot = cotangent.reshape(tokens, D)
    scale_attn = lax.rsqrt(jnp.mean(floats * floats, -1, keepdims=True) + epsilon)
    n1 = (floats * scale_attn * gain_one).astype(bf16)
    dot = lambda a, b: lax.dot_general(a, b, NN, preferred_element_type=f32)

    heads_out, w_theirs = project(1, me_arr, n1, full, cosine, sine, piece)
    got = swap(heads_out)
    mine, w_mine = project(0, me_arr, n1, full, cosine, sine, piece)
    mixed, mixed_out, lse = attend(me_arr, mine, got, piece)
    mixed_out, arrived = tie((mixed_out, [last[1] for last in down_last]))
    down_mine, down_theirs = gather_finish(
        [(a, b, bit, axis) for (a, _, bit, axis), b in zip(down_last, arrived)]
    )
    mixed_got = swap(mixed_out)
    residual = floats + (dot(mixed, out_mine) + dot(mixed_got, out_theirs))
    scale_mlp = lax.rsqrt(jnp.mean(residual * residual, -1, keepdims=True) + epsilon)
    n2 = (residual * scale_mlp * gain_two).astype(bf16)
    layer_out, grad_n2, gg_mine, gu_mine, gg_theirs, gu_theirs, gd_mine, gd_theirs = mlp(
        me_arr, n2, n2.T, cot, residual, wide, down_mine, down_theirs
    )
    wide_sum = Halving([(gg_mine, swap(gg_theirs), ORDERS[0]), (gu_mine, swap(gu_theirs), ORDERS[1])])
    wide_sum.prepare(0)
    sum_gain_mlp = jnp.sum(grad_n2 * residual * scale_mlp, 0)
    grad_residual = cot.astype(f32) + norm_back(grad_n2, residual, scale_mlp, gain_two)
    grad_residual, wide_sum.send = tie((grad_residual, wide_sum.send))
    wide_sum.move(0)
    grad_low = grad_residual.astype(bf16)
    d_out = lax.dot_general(grad_low, out_theirs, NT, preferred_element_type=f32).astype(bf16)
    d_got = swap(d_out)
    d_mine = lax.dot_general(grad_low, out_mine, NT, preferred_element_type=f32).astype(bf16)
    down_sum = Halving([(gd_mine, swap(gd_theirs), HIGH)])
    down_sum.prepare(0)
    d_mine, d_got, down_sum.send = tie((d_mine, d_got, down_sum.send))
    down_sum.move(0)
    back = lambda b, before: attend_back(
        b, before, me_arr, mine, got, mixed, mixed_out, d_mine, d_got, lse, cosine, sine, piece
    )
    lins = back(0, ())

    lins, grad_low = tie((lins, grad_low))
    parts_of = lambda u: (widen(u[:, : D // 2]), widen(u[:, D // 2 :]))

    def grad_out(columns):
        a, b = [
            lax.dot_general(u, columns, TN, preferred_element_type=f32).astype(bf16)[: QD // 2]
            for u in (mixed, mixed_got)
        ]
        return pick(jnp.concatenate([a, b], 0), jnp.concatenate([b, a], 0))

    out_theirs_grad = grad_out(pick(*parts_of(grad_low)[::-1]))
    out_theirs_grad, grad_low, wide_sum.got, down_sum.got = tie(
        (out_theirs_grad, grad_low, wide_sum.got, down_sum.got)
    )
    wide_sum.prepare(1)
    down_sum.prepare(1)
    out_sum = Halving([(grad_out(pick(*parts_of(grad_low))), swap(out_theirs_grad), ORDERS[0])])
    out_sum.prepare(0)
    lins, wide_sum.send, down_sum.send, out_sum.send = tie(
        (lins, wide_sum.send, down_sum.send, out_sum.send)
    )
    wide_sum.move(1)
    down_sum.move(1)
    out_sum.move(0)
    for b in range(1, batch):
        lins = back(b, lins)
    (lin_mine, lin_out), wide_sum.got, down_sum.got = tie((lins, wide_sum.got, down_sum.got))
    _, out_sum.got = tie((lin_mine, out_sum.got))
    lin_got = swap(lin_out)
    down_sum.advance(2)
    out_sum.advance(1)
    wide_sum.advance(2)
    grad_n1 = lax.dot_general(lin_mine, w_mine, NT, preferred_element_type=f32) + lax.dot_general(
        lin_got, w_theirs, NT, preferred_element_type=f32
    )
    sum_gain_attn = jnp.sum(grad_n1 * floats * scale_attn, 0)
    column = lax.broadcasted_iota(jnp.int32, (1, WIDE), 1)
    sums = jnp.where(column == QKV, sum_gain_attn[:, None], 0.0) + jnp.where(
        column == QKV + 1, sum_gain_mlp[:, None], 0.0
    )
    weight_grad = lambda lin: (
        lax.dot_general(n1, lin, TN, preferred_element_type=f32) + sums
    ).astype(bf16)
    half = WIDE // 2
    grad_mine, grad_theirs = weight_grad(lin_mine), weight_grad(lin_got)
    grad_got = swap(grad_theirs)
    pack_sum = Halving(
        [
            (grad_mine[:, :half], grad_got[:, :half], ORDERS[0]),
            (grad_mine[:, half:], grad_got[:, half:], ORDERS[1]),
        ]
    )
    pack_sum.prepare(0)
    _, down_sum.got, out_sum.got, wide_sum.got = tie(
        (pack_sum.send, down_sum.got, out_sum.got, wide_sum.got)
    )
    pack_sum.move(0)
    wide_sum.advance(3)
    down_sum.advance(3)
    out_sum.advance(2)
    grad_input = (grad_residual + norm_back(grad_n1, floats, scale_attn, gain_one)).astype(bf16)
    pack_sum.advance(1)
    _, down_sum.got, out_sum.got, wide_sum.got = tie(
        (pack_sum.send, down_sum.got, out_sum.got, wide_sum.got)
    )
    out_sum.advance(3)
    pack_sum.advance(2)
    _, down_sum.got, out_sum.got = tie((pack_sum.send, down_sum.got, out_sum.got))
    r_gate, r_up = wide_sum.finish(4)
    r_down = down_sum.finish(4)[0][:, : D // 2]
    r_out = out_sum.finish(4)[0][:, : D // 2]
    r_pack = jnp.concatenate(pack_sum.finish(3), 1)
    a, b, c = HQ * HEAD_SIZE, (HQ + HK) * HEAD_SIZE, QKV
    shape = layer_input.shape
    return (
        layer_out.reshape(shape),
        grad_input.reshape(shape),
        r_pack[:, :a],
        r_pack[:, a:b],
        r_pack[:, b:c],
        r_out,
        r_pack[:, c],
        r_gate,
        r_up,
        r_down,
        r_pack[:, c + 1],
    )


def solution(mesh):
    tokens, matrix, vector = P(None, "dp", "seq", None), P("dp", "seq"), P("dp")
    placed = (tokens, *[matrix] * 4, vector, *[matrix] * 3, vector, tokens)
    return jax.shard_map(
        local,
        mesh=mesh,
        in_specs=placed,
        out_specs=(tokens, tokens, *[matrix] * 4, vector, *[matrix] * 3, vector),
        check_vma=False,
    )
```
